32 devices in a mesh: tiles: 2 (over y), sky: 4 (over x, core), visit: 4 (over z).
Axes of the slice: x: 2, y: 2, z: 4, core: 2. Of those that a mesh axis runs over, the one named last changes fastest.
Arguments:
- sky_model: float32 [512, 4096], P(('tiles', 'sky'), 'visit'), parts along dimension 0, may hold values from -6 to 6
- frames: bfloat16 [16, 128, 2048], P(('tiles', 'visit'), 'sky'), parts along dimension 0, may hold values from -8 to 8
- psf_rows: float32 [16, 5], P('tiles'), parts along dimension 0, may hold values from 0.1 to 1
- psf_cols: float32 [16, 5], P('tiles'), parts along dimension 0, may hold values from 0.1 to 1
- dither: int32 [16, 2], P('tiles'), parts along dimension 0, may hold values from -2 to 2
- footprint: int32 [16, 2], P('tiles'), parts along dimension 0, may hold values from 0 to 128, as said below
- huber_cut: float32 [16], P('tiles'), parts along dimension 0, may hold values from 0.3 to 1.5
Outputs:
- gradient: float32 [512, 4096], P(('tiles', 'sky'), 'visit'), parts along dimension 0
The draws below stay inside these ranges and needn't reach their ends.
There are 2 independent parts, one for each index of `tiles`. The reference program is written for one: setup_inputs(seed, part) draws one part's arguments, and reference() takes and returns one part's arrays. A program takes and returns all parts, laid end to end along the dimension named above; each array names one. Nothing has to cross between parts.
Inputs may be any that keep to these rules, and one draw needn't show every extreme that they name: `footprint`: each row is a visit's first covered frame row and one past its last, the first below the second; some visit starts at row 0 and some ends at row 128.
All inputs are finite; a program needn't handle non-finite values.
Results may differ from the reference program's by a relative error of at most 0.0003.
Values may be sent and summed in bfloat16 or wider, within the bound.
A program may use at most 128 MiB of HBM per device.

```python
import math
import jax
import jax.numpy as jnp
from jax import lax

TAPS = 5
H = 256
W = 4096
LH = 128
LW = 2048
K = 8


def draw_footprint(key, part):
    key_a, key_b, key_c, key_d = jax.random.split(jax.random.fold_in(key, 7), 4)
    first = jax.random.randint(key_a, (K,), 0, LH // 2)
    last = jax.random.randint(key_b, (K,), LH // 2 + 1, LH + 1)
    position = jnp.arange(K, dtype=jnp.int32)
    first = jnp.where(position == jax.random.randint(key_c, (), 0, K), 0, first)
    last = jnp.where(position == jax.random.randint(key_d, (), 0, K), LH, last)
    return jnp.stack([first, last], 1).astype(jnp.int32)


def plant(result, own_key, smallest, high):
    dims = result.shape
    spot = [jax.random.randint(jax.random.fold_in(own_key, axis), (), 0, dims[axis]) for axis in range(len(dims))]
    result = result.at[tuple(spot)].set(smallest)
    longest = dims.index(max(dims))
    spot[longest] = (spot[longest] + 1) % dims[longest]
    return result.at[tuple(spot)].set(high)


def level_of(key, extent, cuts, least, largest):
    def one(dim, shards_of):
        draws = jax.random.uniform(jax.random.fold_in(jax.random.fold_in(key, 6), dim), (shards_of,), jnp.float32, least / len(cuts), largest / len(cuts))
        return jnp.repeat(jnp.exp(draws), extent[dim] // shards_of).reshape((-1,) + (1,) * (len(extent) - dim - 1))

    factor_of = one(*cuts[0])
    for cut in cuts[1:]:
        factor_of = factor_of * one(*cut)
    return factor_of


def bell_draw(key, extent, width, reach, cuts=(), kind=jnp.bfloat16):
    values = width * jax.random.normal(key, extent, jnp.float32)
    if cuts:
        values = values * level_of(key, extent, cuts, -0.22, 0.18)
    return jnp.clip(values, -reach, reach).astype(kind)


def setup_inputs(seed: int = 0, part: int = 0) -> dict:
    splits = jax.random.split(jax.random.key(seed), 8)
    part_keys = jax.random.split(jax.random.fold_in(splits[7], part), 8)
    return {
        "sky_model": bell_draw(part_keys[0], (H, W), 1.0, 6.0, ((0, 4), (1, 4)), jnp.float32),
        "frames": bell_draw(part_keys[1], (K, LH, LW), 1.5, 8.0, ((0, 4), (1, 4))),
        "psf_rows": jnp.clip(jnp.exp(jax.random.uniform(part_keys[2], (K, TAPS), jnp.float32, math.log(0.1), math.log(1.0))), 0.1, 1.0),
        "psf_cols": jnp.clip(jnp.exp(jax.random.uniform(part_keys[3], (K, TAPS), jnp.float32, math.log(0.1), math.log(1.0))), 0.1, 1.0),
        "dither": plant(jax.random.randint(part_keys[4], (K, 2), -2, 3), jax.random.fold_in(part_keys[4], 1), -2, 2).astype(jnp.int32),
        "footprint": draw_footprint(jax.random.fold_in(jax.random.fold_in(splits[7], part), 71), part),
        "huber_cut": jnp.clip(jnp.exp(jax.random.uniform(part_keys[6], (K,), jnp.float32, math.log(0.3), math.log(1.5))), 0.3, 1.5),
    }


eps_flux = 0.1
tv_weight = 0.5
dither_bound = 2

def blur_down(values, offset, kernel, length, along_dim):
    half_taps = TAPS // 2
    margin = half_taps + dither_bound
    accum = None
    for b in range(TAPS):
        begin = offset + (b - half_taps + margin)
        piece = kernel[b] * lax.dynamic_slice_in_dim(values, begin, length, along_dim)
        accum = piece if accum is None else accum + piece
    if along_dim == 0:
        return accum[::2]
    return accum[:, ::2]

def spread_up(small, offset, kernel, extra, along_dim):
    half_taps = TAPS // 2
    margin = half_taps + dither_bound
    blank = jnp.zeros_like(small)
    if along_dim == 0:
        upsampled = jnp.stack([small, blank], 1).reshape(2 * small.shape[0], small.shape[1])
        padding = ((margin + extra, margin + extra), (0, 0))
    else:
        upsampled = jnp.stack([small, blank], 2).reshape(small.shape[0], 2 * small.shape[1])
        padding = ((0, 0), (margin + extra, margin + extra))
    padded = jnp.pad(upsampled, padding)
    length = upsampled.shape[along_dim] + 2 * extra
    accum = None
    for b in range(TAPS):
        begin = margin + half_taps - b - offset
        piece = kernel[b] * lax.dynamic_slice_in_dim(padded, begin, length, along_dim)
        accum = piece if accum is None else accum + piece
    return accum

def flux_divergence(window):
    grad_x = window[1:, :-1] - window[:-1, :-1]
    grad_y = window[:-1, 1:] - window[:-1, :-1]
    magnitude = jnp.sqrt(grad_x * grad_x + grad_y * grad_y + eps_flux)
    flux_u = grad_x / magnitude
    flux_w = grad_y / magnitude
    return flux_u[:-1, 1:] - flux_u[1:, 1:] + (flux_w[1:, :-1] - flux_w[1:, 1:])

def reference(sky_model, frames, psf_rows, psf_cols, dither, footprint, huber_cut):
    margin = TAPS // 2 + dither_bound
    padded = jnp.pad(sky_model, margin)
    low_index = jnp.arange(LH, dtype=jnp.int32)

    def one_visit(accum, k):
        row_shift = dither[k, 0]
        col_shift = dither[k, 1]
        columns = blur_down(padded, col_shift, psf_cols[k], W, 1)
        predicted = blur_down(columns, row_shift, psf_rows[k], H, 0)
        inside = (low_index >= footprint[k, 0]) & (low_index < footprint[k, 1])
        cutoff = huber_cut[k]
        clipped = jnp.where(inside[:, None], jnp.clip(predicted - frames[k].astype(jnp.float32), -cutoff, cutoff), jnp.zeros_like(predicted))
        back_rows = spread_up(clipped, row_shift, psf_rows[k], 0, 0)
        return (accum + spread_up(back_rows, col_shift, psf_cols[k], 0, 1), None)
    data_term, _ = lax.scan(one_visit, jnp.zeros((H, W), jnp.float32), jnp.arange(K, dtype=jnp.int32))
    window = jnp.pad(sky_model, 1)
    return data_term / jnp.sqrt(jnp.float32(K)) + tv_weight * flux_divergence(window)
```

```python
import functools

import jax
import jax.numpy as jnp
from jax import lax
from jax.experimental import pallas as pl
from jax.experimental.pallas import tpu as pltpu
from jax.sharding import PartitionSpec as P

TAPS = 5
REACH = 4
SHIFTS = 2 * REACH + 1

eps_flux = 0.1
tv_weight = 0.5

ROWS = 8
LANES = 128

NEIGHBOURS = tuple((y, x) for y in (-1, 0, 1) for x in (-1, 0, 1) if (y, x) != (0, 0))


def split_rows(value):
    high = value.astype(jnp.bfloat16)
    low = (value - high.astype(jnp.float32)).astype(jnp.bfloat16)
    return jnp.concatenate([high, low], axis=0)


def selection(shape, source_of):
    row = lax.broadcasted_iota(jnp.int32, shape, 0)
    col = lax.broadcasted_iota(jnp.int32, shape, 1)
    return jnp.where(source_of(row, col), 1.0, 0.0).astype(jnp.bfloat16)


def dot(a, b):
    return jnp.dot(a, b, preferred_element_type=jnp.float32)


def kernel(
    counts,
    model_ref,
    frames_ref,
    rows_in,
    cols_in,
    dither_in,
    footprint_in,
    cut_in,
    out_ref,
    rows_ref,
    cols_ref,
    dither_ref,
    footprint_ref,
    cut_ref,
    row_taps,
    col_taps,
    grid_ref,
    shifted_ref,
    frame_ref,
    blurred_ref,
    clipped_ref,
    back_ref,
    total_ref,
    whole_ref,
    sum_ref,
    side_out,
    side_in,
    side_ref,
    end_ref,
    corner_ref,
    local_sem,
    small_sem,
    halo_send,
    halo_recv,
    frame_send,
    frame_recv,
    fold_send,
    fold_recv,
):
    sky_count, visit_count = counts
    height, width = out_ref.shape
    per_device, low_rows, low_cols = frame_ref.shape[1:]
    visits = rows_ref.shape[0]
    full_rows, full_cols = grid_ref.shape
    half_rows, half_cols = full_rows // 2, full_cols // 2
    blocks = full_cols // (2 * LANES)
    tile = lax.axis_index("tiles")
    sky = lax.axis_index("sky")
    visit = lax.axis_index("visit")

    def device(y, x):
        return (tile, sky + y, visit + x)

    def exists(y, x):
        ok = None
        for step, at, count in ((y, sky, sky_count), (x, visit, visit_count)):
            if step:
                here = at > 0 if step < 0 else at < count - 1
                ok = here if ok is None else ok & here
        return ok

    def peer_of(o):
        return lax.rem(visit + o, visit_count)

    def row_part(y):
        return (pl.ds(0, ROWS), pl.ds(ROWS, height), pl.ds(ROWS + height, ROWS))[y + 1]

    def col_part(x):
        return (pl.ds(width + LANES, LANES), pl.ds(0, width), pl.ds(width, LANES))[x + 1]

    def edge_of(y, x):
        r = (pl.ds(0, ROWS), pl.ds(0, height), pl.ds(height - ROWS, ROWS))[y + 1]
        c = (pl.ds(0, LANES), pl.ds(0, width), pl.ds(width - LANES, LANES))[x + 1]
        return r, c

    barrier = pltpu.get_barrier_semaphore()

    def greet(o, carry):
        pl.semaphore_signal(
            barrier, inc=1, device_id=(tile, sky, peer_of(o)), device_id_type=pl.DeviceIdType.MESH
        )
        return carry

    lax.fori_loop(1, visit_count, greet, 0)
    for y, x in NEIGHBOURS:
        if y:

            @pl.when(exists(y, x))
            def _():
                pl.semaphore_signal(
                    barrier, inc=1, device_id=device(y, x), device_id_type=pl.DeviceIdType.MESH
                )

    small = [
        pltpu.make_async_copy(source, target, small_sem.at[n])
        for n, (source, target) in enumerate(
            (
                (rows_in, rows_ref),
                (cols_in, cols_ref),
                (dither_in, dither_ref),
                (footprint_in, footprint_ref),
                (cut_in, cut_ref),
            )
        )
    ]
    for copy in small:
        copy.start()
    own_model = pltpu.make_async_copy(
        model_ref, grid_ref.at[pl.ds(ROWS, height), pl.ds(0, width)], local_sem.at[0]
    )
    own_model.start()

    def own_frames():
        return pltpu.make_async_copy(
            frames_ref.at[:, :, pl.ds(pl.multiple_of(visit * low_cols, low_cols), low_cols)],
            frame_ref.at[0],
            local_sem.at[1],
        )

    own_frames().start()

    for copy in small:
        copy.wait()

    def place(k, carry):
        for ref, offset, placed in ((rows_ref, dither_ref[0, k], row_taps), (cols_ref, dither_ref[1, k], col_taps)):
            for d in range(SHIFTS):
                at = d - REACH - offset + TAPS // 2
                value = ref[k, jnp.clip(at, 0, TAPS - 1)]
                placed[k, d] = jnp.where((at >= 0) & (at < TAPS), value, 0.0)
        return carry

    lax.fori_loop(0, visits, place, 0)

    lane = lax.broadcasted_iota(jnp.int32, (8, LANES), 1)
    own_model.wait()
    for side in range(2):
        packed = jnp.zeros((8, LANES), jnp.float32)
        begin = (width - LANES) * side
        for t in range(height // 8):
            piece = grid_ref[ROWS + 8 * t : ROWS + 8 * (t + 1), begin : begin + LANES]
            shift = (8 * t + 8 * side) % LANES
            piece = pltpu.roll(piece, shift, 1) if shift else piece
            packed = jnp.where((lane >= 8 * t) & (lane < 8 * t + 8), piece, packed)
        side_out[side] = packed

    up, down = (sky > 0).astype(jnp.int32), (sky < sky_count - 1).astype(jnp.int32)
    left, right = (visit > 0).astype(jnp.int32), (visit < visit_count - 1).astype(jnp.int32)
    pl.semaphore_wait(barrier, visit_count - 1 + (up + down) * (1 + left + right))

    def halo_copy(n, y, x):
        if y == 0:
            side = (x + 1) // 2
            return pltpu.make_async_remote_copy(
                src_ref=side_out.at[side],
                dst_ref=side_in.at[side],
                send_sem=halo_send.at[n],
                recv_sem=halo_recv.at[n],
                device_id=device(y, x),
                device_id_type=pl.DeviceIdType.MESH,
            )
        return pltpu.make_async_remote_copy(
            src_ref=model_ref.at[edge_of(y, x)],
            dst_ref=grid_ref.at[row_part(-y), col_part(-x)],
            send_sem=halo_send.at[n],
            recv_sem=halo_recv.at[n],
            device_id=device(y, x),
            device_id_type=pl.DeviceIdType.MESH,
        )

    def frame_copy(o):
        peer = peer_of(o)
        return pltpu.make_async_remote_copy(
            src_ref=frames_ref.at[:, :, pl.ds(pl.multiple_of(peer * low_cols, low_cols), low_cols)],
            dst_ref=frame_ref.at[o],
            send_sem=frame_send.at[o],
            recv_sem=frame_recv.at[o],
            device_id=(tile, sky, peer),
            device_id_type=pl.DeviceIdType.MESH,
        )

    for n, (y, x) in enumerate(NEIGHBOURS):

        @pl.when(exists(y, x))
        def _():
            halo_copy(n, y, x).start()

    def send_frames(o, carry):
        frame_copy(o).start()
        return carry

    lax.fori_loop(1, visit_count, send_frames, 0)

    for y, x in NEIGHBOURS:

        @pl.when(jnp.logical_not(exists(y, x)))
        def _():
            part = (row_part(y), col_part(x))
            grid_ref[part] = jnp.zeros(grid_ref.at[part].shape, jnp.float32)

    margin = (clipped_ref.shape[0] - low_rows) // 2
    clipped_ref[0:margin, :] = jnp.zeros((margin, low_cols), jnp.float32)
    clipped_ref[margin + low_rows :, :] = jnp.zeros((margin, low_cols), jnp.float32)
    total_ref[...] = jnp.zeros(total_ref.shape, jnp.float32)
    spread = selection(
        (2 * LANES, 2 * LANES),
        lambda a, b: a == jnp.where(b < LANES, 2 * b, 2 * b - (2 * LANES - 1)),
    )
    join = selection(
        (2 * LANES, 2 * LANES),
        lambda a, b: b == jnp.where(a < LANES, 2 * a, 2 * a - (2 * LANES - 1)),
    )

    def folded(b):
        return jnp.where(b >= full_rows, b - full_rows, b)

    part_rows = selection(
        (full_rows, 2 * full_rows),
        lambda a, b: folded(b) == jnp.where(a < half_rows, 2 * a, 2 * a - (full_rows - 1)),
    )
    join_rows = selection(
        (full_rows, 2 * full_rows),
        lambda a, b: a == jnp.where(folded(b) < half_rows, 2 * folded(b), 2 * folded(b) - (full_rows - 1)),
    )

    for n, (y, x) in enumerate(NEIGHBOURS):
        @pl.when(exists(-y, -x))
        def _():
            halo_copy(n, y, x).wait_recv()
            if y == 0:
                side = (x + 1) // 2
                packed = side_in[side]
                begin = width + LANES * side
                for t in range(height // 8):
                    shift = (-8 * t - 8 * side) % LANES
                    piece = pltpu.roll(packed, shift, 1) if shift else packed
                    keep = lane >= LANES - 8 if side else lane < 8
                    grid_ref[ROWS + 8 * t : ROWS + 8 * (t + 1), begin : begin + LANES] = jnp.where(
                        keep, piece, 0.0
                    )

    for n in range(blocks):
        block = split_rows(grid_ref[:, 2 * LANES * n : 2 * LANES * (n + 1)])
        apart = dot(part_rows, dot(block, spread).astype(jnp.bfloat16))
        whole_ref[:, LANES * n : LANES * (n + 1)] = apart[:, :LANES]
        whole_ref[:, half_cols + LANES * n : half_cols + LANES * (n + 1)] = apart[:, LANES:]
    for d in range(SHIFTS):
        odd, step = (d - REACH) % 2, (d - REACH) // 2
        for p in range(2):
            value = whole_ref[half_rows * p : half_rows * (p + 1), half_cols * odd : half_cols * (odd + 1)]
            if step:
                value = pltpu.roll(value, (-step) % half_cols, 1)
            shifted_ref[d, p] = value[:, :low_cols]

    own_frames().wait()
    low_index = sky * low_rows + lax.broadcasted_iota(jnp.int32, (low_rows, low_cols), 0)

    def chunk(o, carry):
        @pl.when(o > 0)
        def _():
            frame_copy(o).wait_recv()

        owner = lax.rem(visit - o + visit_count, visit_count)
        for j in range(per_device):
            k = owner * per_device + j
            col_shift = dither_ref[1, k]
            for p in range(2):
                value = None
                for b in range(TAPS):
                    piece = cols_ref[k, b] * shifted_ref[col_shift + (b - TAPS // 2 + REACH), p]
                    value = piece if value is None else value + piece
                blurred_ref[p] = value
            predicted = None
            for d in range(SHIFTS):
                odd, step = (d - REACH) % 2, (d - REACH) // 2
                begin = ROWS // 2 + step
                piece = row_taps[k, d] * blurred_ref[odd, begin : begin + low_rows, :]
                predicted = piece if predicted is None else predicted + piece
            cut = cut_ref[k]
            inside = (low_index >= footprint_ref[0, k]) & (low_index < footprint_ref[1, k])
            error = predicted - frame_ref[o, j].astype(jnp.float32)
            clipped_ref[margin : margin + low_rows, :] = jnp.where(
                inside, jnp.minimum(jnp.maximum(error, -cut), cut), 0.0
            )
            for p in range(2):
                value = None
                for d in range(SHIFTS):
                    odd, step = (d - REACH) % 2, (d - REACH) // 2
                    if odd == p:
                        begin = margin - ROWS // 2 - step
                        piece = row_taps[k, d] * clipped_ref[begin : begin + half_rows, :]
                        value = piece if value is None else value + piece
                back_ref[j, p] = value
        weights = [
            [col_taps[owner * per_device + j, d] for d in range(SHIFTS)] for j in range(per_device)
        ]
        for p in range(2):
            for t in range(half_rows // 8):
                rows = slice(8 * t, 8 * (t + 1))
                back = [back_ref[j, p, rows] for j in range(per_device)]
                for d in range(SHIFTS):
                    value = total_ref[d, p, rows, :low_cols]
                    for j in range(per_device):
                        value = value + weights[j][d] * back[j]
                    total_ref[d, p, rows, :low_cols] = value
        return carry

    lax.fori_loop(0, visit_count, chunk, 0)

    for odd in range(2):
        for p in range(2):
            value = None
            for d in range(SHIFTS):
                step = (d - REACH) // 2
                if (d - REACH) % 2 == odd:
                    piece = total_ref[d, p]
                    if step:
                        piece = pltpu.roll(piece, step % half_cols, 1)
                    value = piece if value is None else value + piece
            whole_ref[half_rows * p : half_rows * (p + 1), half_cols * odd : half_cols * (odd + 1)] = value
    def landing(y, x):
        if x == 0:
            return end_ref.at[(y + 1) // 2]
        if y == 0:
            return side_ref.at[(x + 1) // 2]
        return corner_ref.at[(y + 1) + (x + 1) // 2]

    def fold_copy(n, y, x):
        return pltpu.make_async_remote_copy(
            src_ref=sum_ref.at[row_part(y), col_part(x)],
            dst_ref=landing(-y, -x),
            send_sem=fold_send.at[n],
            recv_sem=fold_recv.at[n],
            device_id=device(y, x),
            device_id_type=pl.DeviceIdType.MESH,
        )

    def fold_start(beside):
        for n, (y, x) in enumerate(NEIGHBOURS):
            if (x != 0) == beside:

                @pl.when(exists(y, x))
                def _():
                    fold_copy(n, y, x).start()

    for n in reversed(range(blocks)):
        even = whole_ref[:, LANES * n : LANES * (n + 1)]
        odd = whole_ref[:, half_cols + LANES * n : half_cols + LANES * (n + 1)]
        block = split_rows(jnp.concatenate([even, odd], axis=1))
        sum_ref[:, 2 * LANES * n : 2 * LANES * (n + 1)] = dot(
            join_rows, dot(block, join).astype(jnp.bfloat16)
        )
        if n == blocks - 1:
            fold_start(True)
    fold_start(False)

    share = 1.0 / float(visits) ** 0.5

    strip = 16

    def next_col(value):
        return pltpu.roll(value, full_cols - 1, 1)

    for t in range(height // strip):
        above = grid_ref[ROWS - 1 + strip * t : ROWS - 1 + strip * (t + 1), :]
        here = grid_ref[ROWS + strip * t : ROWS + strip * (t + 1), :]
        below = grid_ref[ROWS + 1 + strip * t : ROWS + 1 + strip * (t + 1), :]
        gx, gy = here - above, next_col(above) - above
        value = gx * lax.rsqrt(gx * gx + gy * gy + eps_flux)
        gx, gy = below - here, next_col(here) - here
        scale = lax.rsqrt(gx * gx + gy * gy + eps_flux)
        flux = gy * scale
        value = value - gx * scale + (pltpu.roll(flux, 1, 1) - flux)
        data = sum_ref[ROWS + strip * t : ROWS + strip * (t + 1), 0:width]
        out_ref[strip * t : strip * (t + 1), :] = share * data + tv_weight * value[:, :width]

    for n, (y, x) in enumerate(NEIGHBOURS):

        @pl.when(exists(-y, -x))
        def _():
            fold_copy(n, y, x).wait_recv()
            part = edge_of(-y, -x)
            out_ref[part] += share * landing(-y, -x)[...]

    for n, (y, x) in enumerate(NEIGHBOURS):

        @pl.when(exists(y, x))
        def _():
            halo_copy(n, y, x).wait_send()
            fold_copy(n, y, x).wait_send()

    def sent(o, carry):
        frame_copy(o).wait_send()
        return carry

    lax.fori_loop(1, visit_count, sent, 0)


def solution(mesh):
    in_specs = (
        P(("tiles", "sky"), "visit"),
        P(("tiles", "visit"), "sky", None),
        P("tiles", None),
        P("tiles", None),
        P("tiles", None),
        P("tiles", None),
        P("tiles"),
    )
    out_specs = P(("tiles", "sky"), "visit")
    sky_count, visit_count = mesh.shape["sky"], mesh.shape["visit"]

    def on_device(sky_model, frames, psf_rows, psf_cols, dither, footprint, huber_cut):
        height, width = sky_model.shape
        per_device, low_rows = frames.shape[:2]
        visits = psf_rows.shape[0]
        low_cols = frames.shape[2] // visit_count
        half_rows, half_cols = height // 2 + ROWS, width // 2 + LANES
        f32 = jnp.float32
        sky_model = pltpu.with_memory_space_constraint(sky_model, pltpu.HBM)
        frames = pltpu.with_memory_space_constraint(frames, pltpu.HBM)
        return pl.pallas_call(
            functools.partial(kernel, (sky_count, visit_count)),
            out_shape=pltpu.VMEM((height, width), f32),
            in_specs=[pl.BlockSpec(memory_space=pltpu.HBM)] * 7,
            out_specs=pl.BlockSpec(memory_space=pltpu.VMEM),
            scratch_shapes=[
                pltpu.SMEM(psf_rows.shape, f32),
                pltpu.SMEM(psf_cols.shape, f32),
                pltpu.SMEM(dither.shape[::-1], jnp.int32),
                pltpu.SMEM(footprint.shape[::-1], jnp.int32),
                pltpu.SMEM(huber_cut.shape, f32),
                pltpu.SMEM((visits, SHIFTS), f32),
                pltpu.SMEM((visits, SHIFTS), f32),
                pltpu.VMEM((height + 2 * ROWS, width + 2 * LANES), f32),
                pltpu.VMEM((SHIFTS, 2, half_rows, low_cols), f32),
                pltpu.VMEM((visit_count, per_device, low_rows, low_cols), jnp.bfloat16),
                pltpu.VMEM((2, half_rows, low_cols), f32),
                pltpu.VMEM((low_rows + 16, low_cols), f32),
                pltpu.VMEM((per_device, 2, half_rows, low_cols), f32),
                pltpu.VMEM((SHIFTS, 2, half_rows, half_cols), f32),
                pltpu.VMEM((height + 2 * ROWS, width + 2 * LANES), f32),
                pltpu.VMEM((height + 2 * ROWS, width + 2 * LANES), f32),
                pltpu.VMEM((2, 8, LANES), f32),
                pltpu.VMEM((2, 8, LANES), f32),
                pltpu.VMEM((2, height, LANES), f32),
                pltpu.VMEM((2, ROWS, width), f32),
                pltpu.VMEM((4, ROWS, LANES), f32),
                pltpu.SemaphoreType.DMA((2,)),
                pltpu.SemaphoreType.DMA((5,)),
                pltpu.SemaphoreType.DMA((8,)),
                pltpu.SemaphoreType.DMA((8,)),
                pltpu.SemaphoreType.DMA((visit_count,)),
                pltpu.SemaphoreType.DMA((visit_count,)),
                pltpu.SemaphoreType.DMA((8,)),
                pltpu.SemaphoreType.DMA((8,)),
            ],
            compiler_params=pltpu.CompilerParams(
                collective_id=0, has_side_effects=True, vmem_limit_bytes=48 * 1024 * 1024
            ),
        )(sky_model, frames, psf_rows, psf_cols, dither.T, footprint.T, huber_cut)

    return jax.shard_map(
        on_device, mesh=mesh, in_specs=in_specs, out_specs=out_specs, check_vma=False
    )
```

```python
import functools

import jax
import jax.numpy as jnp
from jax import lax
from jax.experimental import pallas as pl
from jax.experimental.pallas import tpu as pltpu
from jax.sharding import PartitionSpec as P

TAPS = 5
REACH = 4
SHIFTS = 2 * REACH + 1

eps_flux = 0.1
tv_weight = 0.5

ROWS = 8
LANES = 128
PAIR = 2
SLOT = 80
DEPTH = 256
MESH = pl.DeviceIdType.MESH


def dot(a, b):
    return jnp.dot(a, b, preferred_element_type=jnp.float32)


def iota(shape, dim):
    return lax.broadcasted_iota(jnp.int32, shape, dim)


def selection(shape, source_of):
    row, col = iota(shape, 0), iota(shape, 1)
    return jnp.where(source_of(row, col), 1.0, 0.0).astype(jnp.bfloat16)


def halves(value):
    high = value.astype(jnp.bfloat16)
    return high, (value - high.astype(jnp.float32)).astype(jnp.bfloat16)


def turn(value, shift, axis):
    shift %= value.shape[axis]
    return pltpu.roll(value, shift, axis) if shift else value


def pick(at, taps):
    value = jnp.zeros(at.shape, jnp.float32)
    for a, tap in enumerate(taps):
        value = jnp.where(at == a, tap, value)
    return value


def kernel(
    counts,
    model_ref,
    frames_ref,
    rows_in,
    cols_in,
    dither_in,
    footprint_in,
    cut_in,
    out_ref,
    rows_ref,
    cols_ref,
    dither_ref,
    footprint_ref,
    cut_ref,
    grid_ref,
    own_ref,
    frame_ref,
    edge_out,
    edge_in,
    side_out,
    side_in,
    aux_out,
    aux_in,
    model_stack,
    ahead_ref,
    rowed_ref,
    pred_ref,
    back_ref,
    stack_ref,
    total_ref,
    inter_ref,
    local_sem,
    small_sem,
    here_visit,
    here_sky,
    frame_send,
    frame_recv,
    aux_send,
    aux_recv,
    side_send,
    side_recv,
    rim_send,
    rim_recv,
    edge_send,
    edge_recv,
):
    sky_count, visit_count = counts
    height, width = out_ref.shape
    low_rows, low_cols = frame_ref.shape[2:]
    full_cols = grid_ref.shape[1]
    half_cols = full_cols // 2
    blocks = full_cols // (2 * LANES)
    visits = rows_ref.shape[0]
    tile = lax.axis_index("tiles")
    sky = lax.axis_index("sky")
    visit = lax.axis_index("visit")
    has_up, has_down = sky > 0, sky < sky_count - 1
    has_left, has_right = visit > 0, visit < visit_count - 1
    f32, bf16 = jnp.float32, jnp.bfloat16

    def remote(source, target, send, recv, device):
        return pltpu.make_async_remote_copy(
            src_ref=source, dst_ref=target, send_sem=send, recv_sem=recv, device_id=device, device_id_type=MESH
        )

    def at_visit(q):
        return (tile, sky, q)

    def at_sky(step):
        return (tile, sky + step, visit)

    def columns_of(q):
        return pl.ds(pl.multiple_of(q * low_cols, low_cols), low_cols)

    def frame_copy(peer, owner):
        return remote(
            frames_ref.at[:, :, columns_of(peer)],
            frame_ref.at[owner],
            frame_send.at[peer],
            frame_recv.at[owner],
            at_visit(peer),
        )

    def aux_copy(peer, owner):
        return remote(aux_out.at[peer], aux_in.at[owner], aux_send.at[peer], aux_recv.at[owner], at_visit(peer))

    def side_copy(side):
        return remote(
            side_out.at[side], side_in.at[side], side_send.at[side], side_recv.at[side], at_visit(visit + 2 * side - 1)
        )

    def rim_copy(way):
        source = model_ref.at[pl.ds((height - ROWS) * way, ROWS), :]
        target = grid_ref.at[pl.ds((ROWS + height) * (1 - way), ROWS), pl.ds(0, width)]
        return remote(source, target, rim_send.at[way], rim_recv.at[way], at_sky(2 * way - 1))

    def edge_copy(way):
        return remote(edge_out.at[way], edge_in.at[way], edge_send.at[way], edge_recv.at[way], at_sky(2 * way - 1))

    barrier = pltpu.get_barrier_semaphore()

    def greet(q, carry):
        pl.semaphore_signal(barrier, inc=1, device_id=at_visit(q), device_id_type=MESH)
        return carry

    lax.fori_loop(visit + 1, visit_count, greet, 0)

    @pl.when(has_down)
    def _():
        pl.semaphore_signal(barrier, inc=1, device_id=at_sky(1), device_id_type=MESH)

    small = [
        pltpu.make_async_copy(source, target, small_sem.at[n])
        for n, (source, target) in enumerate(
            (
                (rows_in, rows_ref),
                (cols_in, cols_ref),
                (dither_in, dither_ref),
                (footprint_in, footprint_ref),
                (cut_in, cut_ref),
            )
        )
    ]
    own_model = pltpu.make_async_copy(
        model_ref, grid_ref.at[pl.ds(ROWS, height), pl.ds(0, width)], local_sem.at[0]
    )
    own_frames = pltpu.make_async_copy(frames_ref, own_ref, local_sem.at[1])
    own_block = pltpu.make_async_copy(frames_ref.at[:, :, columns_of(visit)], frame_ref.at[visit], local_sem.at[2])

    smaller = visit + has_up.astype(jnp.int32)

    @pl.when(smaller > 0)
    def _():
        pl.semaphore_wait(barrier, smaller)

    def answer(q, carry):
        pl.semaphore_signal(here_visit.at[visit], inc=1, device_id=at_visit(q), device_id_type=MESH)
        return carry

    lax.fori_loop(0, visit, answer, 0)

    @pl.when(has_up)
    def _():
        pl.semaphore_signal(here_sky, inc=1, device_id=at_sky(-1), device_id_type=MESH)
        rim_copy(0).start()

    own_frames.start()
    own_model.start()
    for copy in small:
        copy.start()

    def send_low(q, carry):
        frame_copy(q, visit).start()
        return carry

    lax.fori_loop(0, visit, send_low, 0)
    own_block.start()

    @pl.when(has_down)
    def _():
        pl.semaphore_wait(here_sky, 1)
        rim_copy(1).start()

    @pl.when(jnp.logical_not(has_up))
    def _():
        grid_ref[0:ROWS, 0:width] = jnp.zeros((ROWS, width), f32)
        edge_in[1] = jnp.zeros(edge_in.shape[1:], bf16)

    @pl.when(jnp.logical_not(has_down))
    def _():
        grid_ref[ROWS + height :, 0:width] = jnp.zeros((ROWS, width), f32)
        edge_in[0] = jnp.zeros(edge_in.shape[1:], bf16)

    own_frames.wait()
    sub = iota((8, low_cols), 0)
    for p2 in range(visit_count // 2):
        for way in range(2):
            tiles = []
            for p in (2 * p2, 2 * p2 + 1):
                cols = slice(low_cols * p, low_cols * (p + 1))
                if way == 0:
                    first = own_ref[0, 0:16, cols].astype(f32)[0:8]
                    second = turn(own_ref[1, 0:16, cols].astype(f32)[0:8], 4, 0)
                    piece = jnp.where(sub < 2, first, jnp.where((sub >= 4) & (sub < 6), second, 0.0))
                else:
                    first = turn(own_ref[0, low_rows - 16 : low_rows, cols].astype(f32)[8:16], 4, 0)
                    second = own_ref[1, low_rows - 16 : low_rows, cols].astype(f32)[8:16]
                    piece = jnp.where((sub >= 2) & (sub < 4), first, jnp.where(sub >= 6, second, 0.0))
                tiles.append(piece)
            edge_out[way, 16 * p2 : 16 * (p2 + 1), :] = jnp.concatenate(tiles, axis=0).astype(bf16)

    @pl.when(has_up)
    def _():
        edge_copy(0).start()

    @pl.when(has_down)
    def _():
        edge_copy(1).start()

    for copy in small:
        copy.wait()
    share = 1.0 / float(visits) ** 0.5

    def col_weights(k):
        weights = []
        for d in range(SHIFTS):
            at = d - REACH - dither_ref[1, k] + TAPS // 2
            value = cols_ref[k, jnp.clip(at, 0, TAPS - 1)]
            weights.append(jnp.where((at >= 0) & (at < TAPS), value, 0.0))
        return weights

    def row_of_halo(n):
        h = n % 4
        return jnp.where(h < 2, low_rows + h, h - 4)

    lane = iota((16, DEPTH), 1)
    row = iota((16, DEPTH), 0)
    model_row = lane % SLOT - ROWS
    is_low = lane >= 2 * SLOT
    blank = lane >= 3 * SLOT
    far = 4 * height

    def low_part(value):
        return jnp.where(is_low, value - value.astype(bf16).astype(f32), value).astype(bf16)

    slot = lane % SLOT
    source_row = jnp.where(slot < 2 * low_rows, slot % low_rows, row_of_halo(slot))
    source_row = jnp.where((slot >= 2 * low_rows + 8) | blank, far, source_row)
    second_visit = jnp.where(slot < 2 * low_rows, slot // low_rows, slot % 8 // 4) > 0
    base_main = jnp.where(blank, -far, model_row + TAPS // 2 - 2 * row)
    halo_row = jnp.where(row < 8, row_of_halo(row), far)
    base_halo = jnp.where(blank, -far, model_row + TAPS // 2 - 2 * halo_row)
    base_back = row + TAPS // 2 - 2 * source_row

    def build(c, carry):
        k0, k1 = PAIR * c, PAIR * c + 1
        shift0, shift1 = dither_ref[0, k0], dither_ref[0, k1]
        taps0 = [rows_ref[k0, a] for a in range(TAPS)]
        taps1 = [rows_ref[k1, a] for a in range(TAPS)]
        for j, (shift, taps) in enumerate(((shift0, taps0), (shift1, taps1))):
            for u in range(low_rows // 16):
                begin = low_rows * j + 16 * u
                ahead_ref[c, begin : begin + 16, :] = low_part(pick(base_main - (32 * u + shift), taps))
        upper = row < 4
        ahead_ref[c, 2 * low_rows : SLOT, :] = low_part(
            pick(
                base_halo - jnp.where(upper, shift0, shift1),
                [jnp.where(upper, a, b) for a, b in zip(taps0, taps1)],
            )
        )
        taps = [jnp.where(second_visit, b, a) for a, b in zip(taps0, taps1)]
        weights = [
            jnp.where(second_visit, b * share, a * share) for a, b in zip(col_weights(k0), col_weights(k1))
        ]
        base = base_back - jnp.where(second_visit, shift1, shift0)
        for u in range(height // 16):
            value = pick(base + 16 * u, taps)
            for d in range(SHIFTS):
                begin = height * d + 16 * u
                back_ref[c, begin : begin + 16, :] = low_part(value * weights[d])
        return carry

    lax.fori_loop(0, visit_count, build, 0)

    own_model.wait()

    @pl.when(has_down)
    def _():
        rim_copy(0).wait_recv()

    @pl.when(has_up)
    def _():
        rim_copy(1).wait_recv()

    lane8 = iota((8, LANES), 1)
    groups = (height + 2 * ROWS) // 8
    for side in range(2):
        packed = jnp.zeros((8, LANES), f32)
        begin = (width - LANES) * side
        for t in range(groups):
            piece = turn(grid_ref[8 * t : 8 * (t + 1), begin : begin + LANES], 8 * t + 8 * side, 1)
            packed = jnp.where((lane8 >= 8 * t) & (lane8 < 8 * t + 8), piece, packed)
        side_out[side] = packed

    @pl.when(has_left)
    def _():
        side_copy(0).start()

    @pl.when(has_down)
    def _():
        edge_copy(0).wait_recv()

    @pl.when(has_up)
    def _():
        edge_copy(1).wait_recv()

    halo = []
    for p2 in range(visit_count // 2):
        both = edge_in[0, 16 * p2 : 16 * (p2 + 1), :].astype(f32) + edge_in[1, 16 * p2 : 16 * (p2 + 1), :].astype(f32)
        halo += [both[0:8], both[8:16]]
    for p in range(visit_count):
        for b in range(low_cols // LANES // 2):
            two = [halo[p][:, LANES * n : LANES * (n + 1)] for n in (2 * b, 2 * b + 1)]
            aux_out[p, 16 * b : 16 * (b + 1), :] = jnp.concatenate(two, axis=0).astype(bf16)
        right = low_cols * (p + 1) if p < visit_count - 1 else 0
        left = low_cols * p - LANES if p > 0 else 0
        pieces = []
        for j in range(PAIR):
            for u in range(low_rows // 16):
                after = own_ref[j, 16 * u : 16 * (u + 1), right : right + LANES].astype(f32)
                before = own_ref[j, 16 * u : 16 * (u + 1), left : left + LANES].astype(f32)
                for n in range(2):
                    pieces.append((after[8 * n : 8 * (n + 1)], before[8 * n : 8 * (n + 1)]))
        pieces.append(
            (
                halo[(p + 1) % visit_count][:, 0:LANES],
                halo[(p - 1) % visit_count][:, low_cols - LANES : low_cols],
            )
        )
        packed = jnp.zeros((8, LANES), f32)
        for g, (after, before) in enumerate(pieces):
            piece = turn(jnp.where(lane8 < LANES // 2, after, before), 4 * g, 1)
            packed = jnp.where((lane8 - 4 * g + 2 + LANES) % LANES < 4, piece, packed)
        aux_out[p, 32:48, :] = jnp.concatenate([packed, jnp.zeros((8, LANES), f32)], axis=0).astype(bf16)
    for u in range(3):
        aux_in[visit, 16 * u : 16 * (u + 1), :] = aux_out[visit, 16 * u : 16 * (u + 1), :]

    def send_aux(q, carry):
        aux_copy(q, visit).start()
        return carry

    lax.fori_loop(0, visit, send_aux, 0)

    def send_high(q, carry):
        pl.semaphore_wait(here_visit.at[q], 1)

        @pl.when(q == visit + 1)
        def _():
            side_copy(1).start()

        frame_copy(q, visit).start()
        aux_copy(q, visit).start()
        return carry

    lax.fori_loop(visit + 1, visit_count, send_high, 0)

    total_ref[...] = jnp.zeros(total_ref.shape, f32)
    model_stack[3 * SLOT : DEPTH, :] = jnp.zeros((DEPTH - 3 * SLOT, full_cols), bf16)
    stack_ref[3 * SLOT : DEPTH, :] = jnp.zeros((DEPTH - 3 * SLOT, half_cols), bf16)

    for side, ok in ((0, has_right), (1, has_left)):
        begin = width + LANES * side

        @pl.when(ok)
        def _():
            side_copy(side).wait_recv()
            packed = side_in[side]
            keep = lane8 >= LANES - 8 if side else lane8 < 8
            for t in range(groups):
                piece = turn(packed, -8 * t - 8 * side, 1)
                grid_ref[8 * t : 8 * (t + 1), begin : begin + LANES] = jnp.where(keep, piece, 0.0)

        @pl.when(jnp.logical_not(ok))
        def _():
            grid_ref[:, begin : begin + LANES] = jnp.zeros((height + 2 * ROWS, LANES), f32)

    spread = selection(
        (2 * LANES, 2 * LANES),
        lambda a, b: a == jnp.where(b < LANES, 2 * b, 2 * b - (2 * LANES - 1)),
    )
    for n in range(blocks):
        high, low = halves(grid_ref[:, 2 * LANES * n : 2 * LANES * (n + 1)])
        for at, part in ((0, high), (SLOT, low), (2 * SLOT, high)):
            if at == 2 * SLOT:
                apart = first
            else:
                apart = dot(part, spread).astype(bf16)
                first = apart if at == 0 else first
            model_stack[at : at + SLOT, LANES * n : LANES * (n + 1)] = apart[:, :LANES]
            model_stack[at : at + SLOT, half_cols + LANES * n : half_cols + LANES * (n + 1)] = apart[:, LANES:]
    operator = ahead_ref[...].reshape(visit_count * SLOT, DEPTH)
    for n in range(blocks):
        cols = slice(2 * LANES * n, 2 * LANES * (n + 1))
        rowed_ref[:, :, cols] = dot(operator, model_stack[:, cols]).reshape(visit_count, SLOT, 2 * LANES)

    sub1 = iota((8, half_cols), 0)

    def predict(c, carry):
        weights0, weights1 = col_weights(PAIR * c), col_weights(PAIR * c + 1)
        for g in range(2 * low_rows // 8 + 1):
            if g < low_rows // 8:
                weights = weights0
            elif g < 2 * low_rows // 8:
                weights = weights1
            else:
                weights = [jnp.where(sub1 < 4, a, b) for a, b in zip(weights0, weights1)]
            even = rowed_ref[c, 8 * g : 8 * (g + 1), 0:half_cols]
            odd = rowed_ref[c, 8 * g : 8 * (g + 1), half_cols:full_cols]
            value = None
            for step in range(-2, 3):
                term = weights[2 * step + REACH] * even
                if step < 2:
                    term = term + weights[2 * step + 1 + REACH] * odd
                term = turn(term, -step, 1)
                value = term if value is None else value + term
            pred_ref[c, 8 * g : 8 * (g + 1), :] = value
        return carry

    lax.fori_loop(0, visit_count, predict, 0)

    def next_col(value):
        return pltpu.roll(value, full_cols - 1, 1)

    strip = 16
    for t in range(height // strip):
        above = grid_ref[ROWS - 1 + strip * t : ROWS - 1 + strip * (t + 1), :]
        here = grid_ref[ROWS + strip * t : ROWS + strip * (t + 1), :]
        below = grid_ref[ROWS + 1 + strip * t : ROWS + 1 + strip * (t + 1), :]
        gx, gy = here - above, next_col(above) - above
        value = gx * lax.rsqrt(gx * gx + gy * gy + eps_flux)
        gx, gy = below - here, next_col(here) - here
        scale = lax.rsqrt(gx * gx + gy * gy + eps_flux)
        flux = gy * scale
        value = value - gx * scale + (pltpu.roll(flux, 1, 1) - flux)
        out_ref[strip * t : strip * (t + 1), :] = tv_weight * value[:, :width]

    own_block.wait()
    row16 = iota((16, low_cols), 0)
    row16n = iota((16, LANES), 0)
    lane16 = iota((16, LANES), 1)
    outer = jnp.where(
        lane16 < LANES // 2, has_right.astype(jnp.int32), has_left.astype(jnp.int32)
    ) > 0
    sub_halo = row_of_halo(iota((8, half_cols), 0)) + sky * low_rows
    upper = sub1 < 4

    order = [sorted(range(visit_count), key=lambda q: (abs(q - v), q)) for v in range(visit_count)]

    def owner_of(o):
        owner = jnp.int32(0)
        for v in range(visit_count):
            for n in range(visit_count):
                if order[v][n]:
                    owner = jnp.where((visit == v) & (o == n), order[v][n], owner)
        return owner

    def clipped(error, cut, inside):
        return jnp.where(inside, jnp.minimum(jnp.maximum(error, -cut), cut), 0.0)

    def put(begin, main, rest):
        for cols, value in ((slice(0, low_cols), main), (slice(low_cols, half_cols), rest)):
            high, low = halves(value)
            stack_ref[begin : begin + 16, cols] = high
            stack_ref[SLOT + begin : SLOT + begin + 16, cols] = low
            stack_ref[2 * SLOT + begin : 2 * SLOT + begin + 16, cols] = high

    def chunk(o, carry):
        c = owner_of(o)

        @pl.when(o > 0)
        def _():
            frame_copy(c, c).wait_recv()
            aux_copy(c, c).wait_recv()

        packed = aux_in[c, 32:48, :].astype(f32)[0:8]
        for j in range(PAIR):
            k = PAIR * c + j
            cut, first, last = cut_ref[k], footprint_ref[0, k], footprint_ref[1, k]
            for u in range(low_rows // 16):
                begin = low_rows * j + 16 * u
                start = sky * low_rows + 16 * u
                error = pred_ref[c, begin : begin + 16, 0:low_cols] - frame_ref[c, j, 16 * u : 16 * (u + 1), :].astype(f32)
                inside = (row16 >= first - start) & (row16 < last - start)
                main = clipped(error, cut, inside)
                g = begin // 8
                beside = jnp.concatenate([turn(packed, -4 * g, 1), turn(packed, -4 * (g + 1), 1)], axis=0)
                error = pred_ref[c, begin : begin + 16, low_cols:half_cols] - beside
                inside = (row16n >= first - start) & (row16n < last - start) & outer
                put(begin, main, clipped(error, cut, inside))
        k0, k1 = PAIR * c, PAIR * c + 1
        tiles = []
        for b in range(low_cols // LANES // 2):
            two = aux_in[c, 16 * b : 16 * (b + 1), :].astype(f32)
            tiles += [two[0:8], two[8:16]]
        tiles.append(turn(packed, -4 * (2 * low_rows // 8), 1))
        error = pred_ref[c, 2 * low_rows : 2 * low_rows + 8, :] - jnp.concatenate(tiles, axis=1)
        inside = (sub_halo >= jnp.where(upper, footprint_ref[0, k0], footprint_ref[0, k1])) & (
            sub_halo < jnp.where(upper, footprint_ref[1, k0], footprint_ref[1, k1])
        )
        value = clipped(error, jnp.where(upper, cut_ref[k0], cut_ref[k1]), inside)
        value = jnp.concatenate([value, jnp.zeros((8, half_cols), f32)], axis=0)
        put(2 * low_rows, value[:, :low_cols], jnp.where(outer, value[:, low_cols:], 0.0))
        for begin in range(0, half_cols, 2 * LANES):
            cols = slice(begin, min(begin + 2 * LANES, half_cols))
            total_ref[:, cols] += dot(back_ref[c], stack_ref[:, cols])
        return carry

    lax.fori_loop(0, visit_count, chunk, 0)

    join = selection(
        (4 * LANES, 2 * LANES),
        lambda a, b: b == jnp.where(a % (2 * LANES) < LANES, 2 * (a % LANES), 2 * (a % LANES) + 1),
    )
    for u in range(height // 16):
        parts = []
        for odd in range(2):
            value = None
            for step in range(-2, 3 - odd):
                begin = height * (2 * step + odd + REACH) + 16 * u
                piece = turn(total_ref[begin : begin + 16, :], step, 1)
                value = piece if value is None else value + piece
            parts.append(halves(value[:, :low_cols]))
        for b in range(low_cols // LANES):
            cols = slice(LANES * b, LANES * (b + 1))
            for n, part in enumerate((parts[0][0], parts[1][0], parts[0][1], parts[1][1])):
                inter_ref[height * b + 16 * u : height * b + 16 * (u + 1), LANES * n : LANES * (n + 1)] = part[:, cols]
    for b in range(low_cols // LANES):
        out_ref[:, 2 * LANES * b : 2 * LANES * (b + 1)] += dot(inter_ref[height * b : height * (b + 1), :], join)

    def sent(q, carry):
        @pl.when(q != visit)
        def _():
            frame_copy(q, visit).wait_send()
            aux_copy(q, visit).wait_send()

        return carry

    lax.fori_loop(0, visit_count, sent, 0)
    for side, ok in ((0, has_left), (1, has_right)):

        @pl.when(ok)
        def _():
            side_copy(side).wait_send()

    for way, ok in ((0, has_up), (1, has_down)):

        @pl.when(ok)
        def _():
            rim_copy(way).wait_send()
            edge_copy(way).wait_send()


def solution(mesh):
    in_specs = (
        P(("tiles", "sky"), "visit"),
        P(("tiles", "visit"), "sky", None),
        P("tiles", None),
        P("tiles", None),
        P("tiles", None),
        P("tiles", None),
        P("tiles"),
    )
    out_specs = P(("tiles", "sky"), "visit")
    sky_count, visit_count = mesh.shape["sky"], mesh.shape["visit"]

    def on_device(sky_model, frames, psf_rows, psf_cols, dither, footprint, huber_cut):
        height, width = sky_model.shape
        per_device, low_rows, all_cols = frames.shape
        visits = psf_rows.shape[0]
        low_cols = all_cols // visit_count
        half_cols = width // 2 + LANES
        f32, bf16 = jnp.float32, jnp.bfloat16
        arguments = [
            pltpu.with_memory_space_constraint(x, pltpu.HBM)
            for x in (sky_model, frames, psf_rows, psf_cols, dither.T, footprint.T, huber_cut)
        ]
        dma = pltpu.SemaphoreType.DMA
        return pl.pallas_call(
            functools.partial(kernel, (sky_count, visit_count)),
            out_shape=pltpu.VMEM((height, width), f32),
            in_specs=[pl.BlockSpec(memory_space=pltpu.HBM)] * 7,
            out_specs=pl.BlockSpec(memory_space=pltpu.VMEM),
            scratch_shapes=[
                pltpu.SMEM(psf_rows.shape, f32),
                pltpu.SMEM(psf_cols.shape, f32),
                pltpu.SMEM(dither.shape[::-1], jnp.int32),
                pltpu.SMEM(footprint.shape[::-1], jnp.int32),
                pltpu.SMEM(huber_cut.shape, f32),
                pltpu.VMEM((height + 2 * ROWS, width + 2 * LANES), f32),
                pltpu.VMEM(frames.shape, bf16),
                pltpu.VMEM((visit_count, per_device, low_rows, low_cols), bf16),
                pltpu.VMEM((2, 8 * visit_count, low_cols), bf16),
                pltpu.VMEM((2, 8 * visit_count, low_cols), bf16),
                pltpu.VMEM((2, 8, LANES), f32),
                pltpu.VMEM((2, 8, LANES), f32),
                pltpu.VMEM((visit_count, 48, LANES), bf16),
                pltpu.VMEM((visit_count, 48, LANES), bf16),
                pltpu.VMEM((DEPTH, 2 * half_cols), bf16),
                pltpu.VMEM((visit_count, SLOT, DEPTH), bf16),
                pltpu.VMEM((visit_count, SLOT, 2 * half_cols), f32),
                pltpu.VMEM((visit_count, SLOT, half_cols), f32),
                pltpu.VMEM((visit_count, SHIFTS * height, DEPTH), bf16),
                pltpu.VMEM((DEPTH, half_cols), bf16),
                pltpu.VMEM((SHIFTS * height, half_cols), f32),
                pltpu.VMEM((low_cols // LANES * height, 4 * LANES), bf16),
                dma((3,)),
                dma((5,)),
                pltpu.SemaphoreType.REGULAR((visit_count,)),
                pltpu.SemaphoreType.REGULAR,
                dma((visit_count,)),
                dma((visit_count,)),
                dma((visit_count,)),
                dma((visit_count,)),
                dma((2,)),
                dma((2,)),
                dma((2,)),
                dma((2,)),
                dma((2,)),
                dma((2,)),
            ],
            compiler_params=pltpu.CompilerParams(
                collective_id=0, has_side_effects=True, vmem_limit_bytes=48 * 1024 * 1024
            ),
        )(*arguments)

    return jax.shard_map(
        on_device, mesh=mesh, in_specs=in_specs, out_specs=out_specs, check_vma=False
    )
```

```python
import functools

import jax
import jax.numpy as jnp
from jax import lax
from jax.experimental import pallas as pl
from jax.experimental.pallas import tpu as pltpu
from jax.sharding import PartitionSpec as P

TAPS = 5
SHIFTS = TAPS + 1

eps_flux = 0.1
tv_weight = 0.5

ROWS = 8
LANES = 128
PAIR = 2
SLOT = 80
DEPTH = 256
MESH = pl.DeviceIdType.MESH


def dot(a, b):
    return jnp.dot(a, b, preferred_element_type=jnp.float32)


def iota(shape, dim):
    return lax.broadcasted_iota(jnp.int32, shape, dim)


def selection(shape, source_of):
    row, col = iota(shape, 0), iota(shape, 1)
    return jnp.where(source_of(row, col), 1.0, 0.0).astype(jnp.bfloat16)


def halves(value):
    high = value.astype(jnp.bfloat16)
    return high, (value - high.astype(jnp.float32)).astype(jnp.bfloat16)


def turn(value, shift, axis):
    shift %= value.shape[axis]
    return pltpu.roll(value, shift, axis) if shift else value


def pick(at, taps):
    value = jnp.zeros(at.shape, jnp.float32)
    for a, tap in enumerate(taps):
        value = jnp.where(at == a, tap, value)
    return value


def kernel(
    counts,
    model_ref,
    frames_ref,
    rows_in,
    cols_in,
    dither_in,
    footprint_in,
    cut_in,
    out_ref,
    rows_ref,
    cols_ref,
    dither_ref,
    footprint_ref,
    cut_ref,
    grid_ref,
    own_ref,
    frame_ref,
    edge_out,
    edge_in,
    side_out,
    side_in,
    aux_out,
    aux_in,
    model_stack,
    ahead_ref,
    rowed_ref,
    pred_ref,
    back_ref,
    stack_ref,
    total_ref,
    inter_ref,
    local_sem,
    small_sem,
    here_visit,
    here_sky,
    frame_send,
    frame_recv,
    aux_send,
    aux_recv,
    side_send,
    side_recv,
    rim_send,
    rim_recv,
    edge_send,
    edge_recv,
):
    sky_count, visit_count = counts
    height, width = out_ref.shape
    low_rows, low_cols = frame_ref.shape[2:]
    full_cols = grid_ref.shape[1]
    half_cols = full_cols // 2
    blocks = full_cols // (2 * LANES)
    visits = rows_ref.shape[0]
    tile = lax.axis_index("tiles")
    sky = lax.axis_index("sky")
    visit = lax.axis_index("visit")
    has_up, has_down = sky > 0, sky < sky_count - 1
    has_left, has_right = visit > 0, visit < visit_count - 1
    f32, bf16 = jnp.float32, jnp.bfloat16

    def remote(source, target, send, recv, device):
        return pltpu.make_async_remote_copy(
            src_ref=source, dst_ref=target, send_sem=send, recv_sem=recv, device_id=device, device_id_type=MESH
        )

    def at_visit(q):
        return (tile, sky, q)

    def at_sky(step):
        return (tile, sky + step, visit)

    def columns_of(q):
        return pl.ds(pl.multiple_of(q * low_cols, low_cols), low_cols)

    def frame_copy(peer, owner):
        return remote(
            frames_ref.at[:, :, columns_of(peer)],
            frame_ref.at[owner],
            frame_send.at[peer],
            frame_recv.at[owner],
            at_visit(peer),
        )

    def aux_copy(peer, owner):
        return remote(aux_out.at[peer], aux_in.at[owner], aux_send.at[peer], aux_recv.at[owner], at_visit(peer))

    def side_copy(side):
        return remote(
            side_out.at[side], side_in.at[side], side_send.at[side], side_recv.at[side], at_visit(visit + 2 * side - 1)
        )

    def rim_copy(way):
        source = model_ref.at[pl.ds((height - ROWS) * way, ROWS), :]
        target = grid_ref.at[pl.ds((ROWS + height) * (1 - way), ROWS), pl.ds(0, width)]
        return remote(source, target, rim_send.at[way], rim_recv.at[way], at_sky(2 * way - 1))

    def edge_copy(way):
        return remote(edge_out.at[way], edge_in.at[way], edge_send.at[way], edge_recv.at[way], at_sky(2 * way - 1))

    barrier = pltpu.get_barrier_semaphore()

    def greet(q, carry):
        pl.semaphore_signal(barrier, inc=1, device_id=at_visit(q), device_id_type=MESH)
        return carry

    lax.fori_loop(visit + 1, visit_count, greet, 0)

    @pl.when(has_down)
    def _():
        pl.semaphore_signal(barrier, inc=1, device_id=at_sky(1), device_id_type=MESH)

    small = [
        pltpu.make_async_copy(source, target, small_sem.at[n])
        for n, (source, target) in enumerate(
            (
                (rows_in, rows_ref),
                (cols_in, cols_ref),
                (dither_in, dither_ref),
                (footprint_in, footprint_ref),
                (cut_in, cut_ref),
            )
        )
    ]
    own_model = pltpu.make_async_copy(
        model_ref, grid_ref.at[pl.ds(ROWS, height), pl.ds(0, width)], local_sem.at[0]
    )
    own_frames = pltpu.make_async_copy(frames_ref, own_ref, local_sem.at[1])
    own_block = pltpu.make_async_copy(frames_ref.at[:, :, columns_of(visit)], frame_ref.at[visit], local_sem.at[2])

    smaller = visit + has_up.astype(jnp.int32)

    @pl.when(smaller > 0)
    def _():
        pl.semaphore_wait(barrier, smaller)

    def answer(q, carry):
        pl.semaphore_signal(here_visit.at[visit], inc=1, device_id=at_visit(q), device_id_type=MESH)
        return carry

    lax.fori_loop(0, visit, answer, 0)

    @pl.when(has_up)
    def _():
        pl.semaphore_signal(here_sky, inc=1, device_id=at_sky(-1), device_id_type=MESH)
        rim_copy(0).start()

    own_frames.start()
    own_model.start()
    for copy in small:
        copy.start()

    @pl.when(has_left)
    def _():
        frame_copy(0, visit).start()

    own_block.start()

    @pl.when(has_down)
    def _():
        pl.semaphore_wait(here_sky, 1)
        rim_copy(1).start()

    @pl.when(jnp.logical_not(has_up))
    def _():
        grid_ref[0:ROWS, 0:width] = jnp.zeros((ROWS, width), f32)
        edge_in[1] = jnp.zeros(edge_in.shape[1:], bf16)

    @pl.when(jnp.logical_not(has_down))
    def _():
        grid_ref[ROWS + height :, 0:width] = jnp.zeros((ROWS, width), f32)
        edge_in[0] = jnp.zeros(edge_in.shape[1:], bf16)

    own_frames.wait()
    sub = iota((8, low_cols), 0)
    for p2 in range(visit_count // 2):
        for way in range(2):
            tiles = []
            for p in (2 * p2, 2 * p2 + 1):
                cols = slice(low_cols * p, low_cols * (p + 1))
                if way == 0:
                    first = own_ref[0, 0:16, cols].astype(f32)[0:8]
                    second = turn(own_ref[1, 0:16, cols].astype(f32)[0:8], 4, 0)
                    piece = jnp.where(sub < 2, first, jnp.where((sub >= 4) & (sub < 6), second, 0.0))
                else:
                    first = turn(own_ref[0, low_rows - 16 : low_rows, cols].astype(f32)[8:16], 4, 0)
                    second = own_ref[1, low_rows - 16 : low_rows, cols].astype(f32)[8:16]
                    piece = jnp.where((sub >= 2) & (sub < 4), first, jnp.where(sub >= 6, second, 0.0))
                tiles.append(piece)
            edge_out[way, 16 * p2 : 16 * (p2 + 1), :] = jnp.concatenate(tiles, axis=0).astype(bf16)

    @pl.when(has_up)
    def _():
        edge_copy(0).start()

    @pl.when(has_down)
    def _():
        edge_copy(1).start()

    for copy in small:
        copy.wait()
    share = 1.0 / float(visits) ** 0.5

    def col_shift(k):
        return (dither_ref[1, k] + 4) // 2 - 2

    def col_weights(k):
        odd = dither_ref[1, k] - 2 * col_shift(k)
        weights = []
        for d in range(SHIFTS):
            value = jnp.where(odd > 0, cols_ref[k, max(d - 1, 0)], cols_ref[k, min(d, TAPS - 1)])
            weights.append(jnp.where(odd > 0, 0.0, value) if d == 0 else value)
        weights[TAPS] = jnp.where(odd > 0, weights[TAPS], 0.0)
        return weights

    def row_of_halo(n):
        h = n % 4
        return jnp.where(h < 2, low_rows + h, h - 4)

    lane = iota((16, DEPTH), 1)
    row = iota((16, DEPTH), 0)
    model_row = lane % SLOT - ROWS
    is_low = lane >= 2 * SLOT
    blank = lane >= 3 * SLOT
    far = 4 * height

    def low_part(value):
        return jnp.where(is_low, value - value.astype(bf16).astype(f32), value).astype(bf16)

    slot = lane % SLOT
    source_row = jnp.where(slot < 2 * low_rows, slot % low_rows, row_of_halo(slot))
    source_row = jnp.where((slot >= 2 * low_rows + 8) | blank, far, source_row)
    second_visit = jnp.where(slot < 2 * low_rows, slot // low_rows, slot % 8 // 4) > 0
    base_main = jnp.where(blank, -far, model_row + TAPS // 2 - 2 * row)
    halo_row = jnp.where(row < 8, row_of_halo(row), far)
    base_halo = jnp.where(blank, -far, model_row + TAPS // 2 - 2 * halo_row)
    base_back = row + TAPS // 2 - 2 * source_row

    def build(c, carry):
        k0, k1 = PAIR * c, PAIR * c + 1
        shift0, shift1 = dither_ref[0, k0], dither_ref[0, k1]
        taps0 = [rows_ref[k0, a] for a in range(TAPS)]
        taps1 = [rows_ref[k1, a] for a in range(TAPS)]
        for j, (shift, taps) in enumerate(((shift0, taps0), (shift1, taps1))):
            for u in range(low_rows // 16):
                begin = low_rows * j + 16 * u
                ahead_ref[c, begin : begin + 16, :] = low_part(pick(base_main - (32 * u + shift), taps))
        upper = row < 4
        ahead_ref[c, 2 * low_rows : SLOT, :] = low_part(
            pick(
                base_halo - jnp.where(upper, shift0, shift1),
                [jnp.where(upper, a, b) for a, b in zip(taps0, taps1)],
            )
        )
        taps = [jnp.where(second_visit, b, a) for a, b in zip(taps0, taps1)]
        weights = [
            jnp.where(second_visit, b * share, a * share) for a, b in zip(col_weights(k0), col_weights(k1))
        ]
        base = base_back - jnp.where(second_visit, shift1, shift0)
        for u in range(height // 16):
            value = pick(base + 16 * u, taps)
            for d in range(SHIFTS):
                begin = height * d + 16 * u
                back_ref[c, begin : begin + 16, :] = low_part(value * weights[d])
        return carry

    lax.fori_loop(0, visit_count, build, 0)

    own_model.wait()

    @pl.when(has_down)
    def _():
        rim_copy(0).wait_recv()

    @pl.when(has_up)
    def _():
        rim_copy(1).wait_recv()

    lane8 = iota((8, LANES), 1)
    groups = (height + 2 * ROWS) // 8
    for side in range(2):
        packed = jnp.zeros((8, LANES), f32)
        begin = (width - LANES) * side
        for t in range(groups):
            piece = turn(grid_ref[8 * t : 8 * (t + 1), begin : begin + LANES], 8 * t + 8 * side, 1)
            packed = jnp.where((lane8 >= 8 * t) & (lane8 < 8 * t + 8), piece, packed)
        side_out[side] = packed

    @pl.when(has_left)
    def _():
        side_copy(0).start()

    @pl.when(has_down)
    def _():
        edge_copy(0).wait_recv()

    @pl.when(has_up)
    def _():
        edge_copy(1).wait_recv()

    halo = []
    for p2 in range(visit_count // 2):
        both = edge_in[0, 16 * p2 : 16 * (p2 + 1), :].astype(f32) + edge_in[1, 16 * p2 : 16 * (p2 + 1), :].astype(f32)
        halo += [both[0:8], both[8:16]]
    for p in range(visit_count):
        for b in range(low_cols // LANES // 2):
            two = [halo[p][:, LANES * n : LANES * (n + 1)] for n in (2 * b, 2 * b + 1)]
            aux_out[p, 16 * b : 16 * (b + 1), :] = jnp.concatenate(two, axis=0).astype(bf16)
        right = low_cols * (p + 1) if p < visit_count - 1 else 0
        left = low_cols * p - LANES if p > 0 else 0
        pieces = []
        for j in range(PAIR):
            for u in range(low_rows // 16):
                after = own_ref[j, 16 * u : 16 * (u + 1), right : right + LANES].astype(f32)
                before = own_ref[j, 16 * u : 16 * (u + 1), left : left + LANES].astype(f32)
                for n in range(2):
                    pieces.append((after[8 * n : 8 * (n + 1)], before[8 * n : 8 * (n + 1)]))
        pieces.append(
            (
                halo[(p + 1) % visit_count][:, 0:LANES],
                halo[(p - 1) % visit_count][:, low_cols - LANES : low_cols],
            )
        )
        packed = jnp.zeros((8, LANES), f32)
        for g, (after, before) in enumerate(pieces):
            piece = turn(jnp.where(lane8 < LANES // 2, after, before), 4 * g, 1)
            packed = jnp.where((lane8 - 4 * g + 2 + LANES) % LANES < 4, piece, packed)
        aux_out[p, 32:48, :] = jnp.concatenate([packed, jnp.zeros((8, LANES), f32)], axis=0).astype(bf16)
    for u in range(3):
        aux_in[visit, 16 * u : 16 * (u + 1), :] = aux_out[visit, 16 * u : 16 * (u + 1), :]

    def send_low(q, carry):
        aux_copy(q, visit).start()

        @pl.when(q > 0)
        def _():
            frame_copy(q, visit).start()

        return carry

    lax.fori_loop(0, visit, send_low, 0)

    def send_high(q, carry):
        pl.semaphore_wait(here_visit.at[q], 1)

        @pl.when(q == visit + 1)
        def _():
            side_copy(1).start()

        aux_copy(q, visit).start()
        frame_copy(q, visit).start()
        return carry

    following = jnp.minimum(visit + 2, visit_count)
    lax.fori_loop(visit + 1, following, send_high, 0)

    total_ref[...] = jnp.zeros(total_ref.shape, f32)
    model_stack[3 * SLOT : DEPTH, :] = jnp.zeros((DEPTH - 3 * SLOT, full_cols), bf16)
    stack_ref[3 * SLOT : DEPTH, :] = jnp.zeros((DEPTH - 3 * SLOT, half_cols), bf16)

    spread = selection(
        (2 * LANES, 2 * LANES),
        lambda a, b: a == jnp.where(b < LANES, 2 * b, 2 * b - (2 * LANES - 1)),
    )
    operator = ahead_ref[...].reshape(visit_count * SLOT, DEPTH)

    def rows_ahead(n):
        cols = slice(2 * LANES * n, 2 * LANES * (n + 1))
        high, low = halves(grid_ref[:, cols])
        high, low = dot(high, spread).astype(bf16), dot(low, spread).astype(bf16)
        model_stack[0:SLOT, cols] = high
        model_stack[SLOT : 2 * SLOT, cols] = low
        model_stack[2 * SLOT : 3 * SLOT, cols] = high
        rowed_ref[:, :, cols] = dot(operator, model_stack[:, cols]).reshape(visit_count, SLOT, 2 * LANES)

    for n in range(blocks - 1):
        rows_ahead(n)

    lax.fori_loop(following, visit_count, send_high, 0)

    for side, ok in ((0, has_right), (1, has_left)):
        begin = width + LANES * side

        @pl.when(ok)
        def _():
            side_copy(side).wait_recv()
            packed = side_in[side]
            keep = lane8 >= LANES - 8 if side else lane8 < 8
            for t in range(groups):
                piece = turn(packed, -8 * t - 8 * side, 1)
                grid_ref[8 * t : 8 * (t + 1), begin : begin + LANES] = jnp.where(keep, piece, 0.0)

        @pl.when(jnp.logical_not(ok))
        def _():
            grid_ref[:, begin : begin + LANES] = jnp.zeros((height + 2 * ROWS, LANES), f32)

    rows_ahead(blocks - 1)

    first_lane, last_lane = lane8 == 0, lane8 == LANES - 1
    upper8 = iota((8, LANES), 0) < 4

    def predict(c, carry):
        weights0, weights1 = col_weights(PAIR * c), col_weights(PAIR * c + 1)
        for g in range(2 * low_rows // 8 + 1):
            if g < low_rows // 8:
                weights = weights0
            elif g < 2 * low_rows // 8:
                weights = weights1
            else:
                weights = [jnp.where(upper8, a, b) for a, b in zip(weights0, weights1)]
            rows = slice(8 * g, 8 * (g + 1))
            before, here, after = [], [], []
            for n in range(blocks):
                even = rowed_ref[c, rows, 2 * LANES * n : 2 * LANES * n + LANES]
                odd = rowed_ref[c, rows, 2 * LANES * n + LANES : 2 * LANES * (n + 1)]
                before.append(pltpu.roll(weights[0] * even + weights[1] * odd, 1, 1))
                here.append(weights[2] * even + weights[3] * odd)
                after.append(pltpu.roll(weights[4] * even + weights[5] * odd, LANES - 1, 1))
            for n in range(blocks):
                value = here[n] + jnp.where(first_lane, before[n - 1], before[n])
                value = value + jnp.where(last_lane, after[(n + 1) % blocks], after[n])
                pred_ref[c, rows, LANES * n : LANES * (n + 1)] = value
        return carry

    lax.fori_loop(0, visit_count, predict, 0)

    def next_col(value):
        return pltpu.roll(value, full_cols - 1, 1)

    strip = 16
    for t in range(height // strip):
        above = grid_ref[ROWS - 1 + strip * t : ROWS - 1 + strip * (t + 1), :]
        here = grid_ref[ROWS + strip * t : ROWS + strip * (t + 1), :]
        below = grid_ref[ROWS + 1 + strip * t : ROWS + 1 + strip * (t + 1), :]
        gx, gy = here - above, next_col(above) - above
        value = gx * lax.rsqrt(gx * gx + gy * gy + eps_flux)
        gx, gy = below - here, next_col(here) - here
        scale = lax.rsqrt(gx * gx + gy * gy + eps_flux)
        flux = gy * scale
        value = value - gx * scale + (pltpu.roll(flux, 1, 1) - flux)
        out_ref[strip * t : strip * (t + 1), :] = tv_weight * value[:, :width]

    own_block.wait()
    row16 = iota((16, LANES), 0)
    lane16 = iota((16, LANES), 1)
    halo_index = row_of_halo(iota((16, LANES), 0)) + sky * low_rows
    upper16 = row16 < 4
    columns = [lane16 + LANES * n for n in range(blocks - 1)]
    columns.append(jnp.where(lane16 < LANES // 2, lane16 + low_cols, lane16 - LANES))
    columns = [value + visit * low_cols for value in columns]
    all_cols = low_cols * visit_count

    order = [sorted(range(visit_count), key=lambda q: (abs(q - v), q)) for v in range(visit_count)]

    def owner_of(o):
        owner = jnp.int32(0)
        for v in range(visit_count):
            for n in range(visit_count):
                if order[v][n]:
                    owner = jnp.where((visit == v) & (o == n), order[v][n], owner)
        return owner

    def shifted(values, shift):
        turned = [pltpu.roll(value, jnp.where(shift < 0, LANES - 1, shift), 1) for value in values]
        to_right, to_left = (lane16 == 0) & (shift > 0), (lane16 == LANES - 1) & (shift < 0)
        return [
            jnp.where(to_right, turned[n - 1], jnp.where(to_left, turned[(n + 1) % blocks], turned[n]))
            for n in range(blocks)
        ]

    def limits(limit, shift):
        result = []
        for n in range(blocks):
            if 0 < n < blocks - 2:
                result.append(limit)
            else:
                result.append(jnp.where((columns[n] >= shift) & (columns[n] < all_cols + shift), limit, 0.0))
        return result

    def put(begin, predicted, values, limit):
        for n in range(blocks):
            cols = slice(LANES * n, LANES * (n + 1))
            error = predicted[n] - values[n]
            high, low = halves(jnp.minimum(jnp.maximum(error, -limit[n]), limit[n]))
            stack_ref[begin : begin + 16, cols] = high
            stack_ref[SLOT + begin : SLOT + begin + 16, cols] = low
            stack_ref[2 * SLOT + begin : 2 * SLOT + begin + 16, cols] = high

    def chunk(o, carry):
        c = owner_of(o)

        @pl.when(o > 0)
        def _():
            frame_copy(c, c).wait_recv()
            aux_copy(c, c).wait_recv()

        packed = aux_in[c, 32:48, :].astype(f32)[0:8]
        shifts = [col_shift(PAIR * c + j) for j in range(PAIR)]
        for j in range(PAIR):
            k = PAIR * c + j
            cut, first, last = cut_ref[k], footprint_ref[0, k], footprint_ref[1, k]
            for u in range(low_rows // 16):
                begin = low_rows * j + 16 * u
                start = sky * low_rows + 16 * u
                rows = slice(16 * u, 16 * (u + 1))
                values = [
                    frame_ref[c, j, rows, LANES * n : LANES * (n + 1)].astype(f32) for n in range(blocks - 1)
                ]
                g = begin // 8
                values.append(jnp.concatenate([turn(packed, -4 * g, 1), turn(packed, -4 * (g + 1), 1)], axis=0))
                limit = jnp.where((row16 >= first - start) & (row16 < last - start), cut, 0.0)
                predicted = [pred_ref[c, begin : begin + 16, LANES * n : LANES * (n + 1)] for n in range(blocks)]
                put(begin, predicted, shifted(values, shifts[j]), limits(limit, shifts[j]))
        k0, k1 = PAIR * c, PAIR * c + 1
        begin = 2 * low_rows
        blank8 = jnp.zeros((8, LANES), f32)
        values = []
        for b in range(low_cols // LANES // 2):
            two = aux_in[c, 16 * b : 16 * (b + 1), :].astype(f32)
            values += [jnp.concatenate([two[8 * n : 8 * (n + 1)], blank8], axis=0) for n in range(2)]
        values.append(jnp.concatenate([turn(packed, -4 * (begin // 8), 1), blank8], axis=0))
        values = [jnp.where(upper16, a, b) for a, b in zip(shifted(values, shifts[0]), shifted(values, shifts[1]))]
        inside = (halo_index >= jnp.where(upper16, footprint_ref[0, k0], footprint_ref[0, k1])) & (
            halo_index < jnp.where(upper16, footprint_ref[1, k0], footprint_ref[1, k1])
        )
        limit = jnp.where(inside & (row16 < 8), jnp.where(upper16, cut_ref[k0], cut_ref[k1]), 0.0)
        predicted = [
            jnp.concatenate([pred_ref[c, begin : begin + 8, LANES * n : LANES * (n + 1)], blank8], axis=0)
            for n in range(blocks)
        ]
        put(begin, predicted, values, limits(limit, jnp.where(upper16, shifts[0], shifts[1])))
        for begin in range(0, half_cols, 2 * LANES):
            cols = slice(begin, min(begin + 2 * LANES, half_cols))
            total_ref[:, cols] += dot(back_ref[c], stack_ref[:, cols])
        return carry

    lax.fori_loop(0, visit_count, chunk, 0)

    join = selection(
        (4 * LANES, 2 * LANES),
        lambda a, b: b == jnp.where(a % (2 * LANES) < LANES, 2 * (a % LANES), 2 * (a % LANES) + 1),
    )
    for u in range(height // 16):
        parts = []
        for odd in range(2):
            value = None
            for step in range(-1, 2):
                begin = height * (2 * (step + 1) + odd) + 16 * u
                piece = turn(total_ref[begin : begin + 16, :], step, 1)
                value = piece if value is None else value + piece
            parts.append(halves(value[:, :low_cols]))
        for b in range(low_cols // LANES):
            cols = slice(LANES * b, LANES * (b + 1))
            for n, part in enumerate((parts[0][0], parts[1][0], parts[0][1], parts[1][1])):
                inter_ref[height * b + 16 * u : height * b + 16 * (u + 1), LANES * n : LANES * (n + 1)] = part[:, cols]
    joined = dot(inter_ref[...], join)
    for b in range(low_cols // LANES):
        out_ref[:, 2 * LANES * b : 2 * LANES * (b + 1)] += joined[height * b : height * (b + 1)]

    def sent(q, carry):
        @pl.when(q != visit)
        def _():
            frame_copy(q, visit).wait_send()
            aux_copy(q, visit).wait_send()

        return carry

    lax.fori_loop(0, visit_count, sent, 0)
    for side, ok in ((0, has_left), (1, has_right)):

        @pl.when(ok)
        def _():
            side_copy(side).wait_send()

    for way, ok in ((0, has_up), (1, has_down)):

        @pl.when(ok)
        def _():
            rim_copy(way).wait_send()
            edge_copy(way).wait_send()


def solution(mesh):
    in_specs = (
        P(("tiles", "sky"), "visit"),
        P(("tiles", "visit"), "sky", None),
        P("tiles", None),
        P("tiles", None),
        P("tiles", None),
        P("tiles", None),
        P("tiles"),
    )
    out_specs = P(("tiles", "sky"), "visit")
    sky_count, visit_count = mesh.shape["sky"], mesh.shape["visit"]

    def on_device(sky_model, frames, psf_rows, psf_cols, dither, footprint, huber_cut):
        height, width = sky_model.shape
        per_device, low_rows, all_cols = frames.shape
        visits = psf_rows.shape[0]
        low_cols = all_cols // visit_count
        half_cols = width // 2 + LANES
        f32, bf16 = jnp.float32, jnp.bfloat16
        arguments = [
            pltpu.with_memory_space_constraint(x, pltpu.HBM)
            for x in (sky_model, frames, psf_rows, psf_cols, dither.T, footprint.T, huber_cut)
        ]
        dma = pltpu.SemaphoreType.DMA
        return pl.pallas_call(
            functools.partial(kernel, (sky_count, visit_count)),
            out_shape=pltpu.VMEM((height, width), f32),
            in_specs=[pl.BlockSpec(memory_space=pltpu.HBM)] * 7,
            out_specs=pl.BlockSpec(memory_space=pltpu.VMEM),
            scratch_shapes=[
                pltpu.SMEM(psf_rows.shape, f32),
                pltpu.SMEM(psf_cols.shape, f32),
                pltpu.SMEM(dither.shape[::-1], jnp.int32),
                pltpu.SMEM(footprint.shape[::-1], jnp.int32),
                pltpu.SMEM(huber_cut.shape, f32),
                pltpu.VMEM((height + 2 * ROWS, width + 2 * LANES), f32),
                pltpu.VMEM(frames.shape, bf16),
                pltpu.VMEM((visit_count, per_device, low_rows, low_cols), bf16),
                pltpu.VMEM((2, 8 * visit_count, low_cols), bf16),
                pltpu.VMEM((2, 8 * visit_count, low_cols), bf16),
                pltpu.VMEM((2, 8, LANES), f32),
                pltpu.VMEM((2, 8, LANES), f32),
                pltpu.VMEM((visit_count, 48, LANES), bf16),
                pltpu.VMEM((visit_count, 48, LANES), bf16),
                pltpu.VMEM((DEPTH, 2 * half_cols), bf16),
                pltpu.VMEM((visit_count, SLOT, DEPTH), bf16),
                pltpu.VMEM((visit_count, SLOT, 2 * half_cols), f32),
                pltpu.VMEM((visit_count, SLOT, half_cols), f32),
                pltpu.VMEM((visit_count, SHIFTS * height, DEPTH), bf16),
                pltpu.VMEM((DEPTH, half_cols), bf16),
                pltpu.VMEM((SHIFTS * height, half_cols), f32),
                pltpu.VMEM((low_cols // LANES * height, 4 * LANES), bf16),
                dma((3,)),
                dma((5,)),
                pltpu.SemaphoreType.REGULAR((visit_count,)),
                pltpu.SemaphoreType.REGULAR,
                dma((visit_count,)),
                dma((visit_count,)),
                dma((visit_count,)),
                dma((visit_count,)),
                dma((2,)),
                dma((2,)),
                dma((2,)),
                dma((2,)),
                dma((2,)),
                dma((2,)),
            ],
            compiler_params=pltpu.CompilerParams(
                collective_id=0, has_side_effects=True, vmem_limit_bytes=48 * 1024 * 1024
            ),
        )(*arguments)

    return jax.shard_map(
        on_device, mesh=mesh, in_specs=in_specs, out_specs=out_specs, check_vma=False
    )
```

```python
import functools

import jax
import jax.numpy as jnp
from jax import lax
from jax.experimental import pallas as pl
from jax.experimental.pallas import tpu as pltpu
from jax.sharding import PartitionSpec as P

TAPS = 5
SHIFTS = TAPS + 1

eps_flux = 0.1
tv_weight = 0.5

ROWS = 8
LANES = 128
PAIR = 2
SLOT = 80
DEPTH = 256
MESH = pl.DeviceIdType.MESH


def dot(a, b):
    return jnp.dot(a, b, preferred_element_type=jnp.float32)


def iota(shape, dim):
    return lax.broadcasted_iota(jnp.int32, shape, dim)


def selection(shape, source_of):
    row, col = iota(shape, 0), iota(shape, 1)
    return jnp.where(source_of(row, col), 1.0, 0.0).astype(jnp.bfloat16)


def halves(value):
    high = value.astype(jnp.bfloat16)
    return high, (value - high.astype(jnp.float32)).astype(jnp.bfloat16)


def turn(value, shift, axis):
    shift %= value.shape[axis]
    return pltpu.roll(value, shift, axis) if shift else value


def pick(at, taps):
    value = jnp.zeros(at.shape, jnp.float32)
    for a, tap in enumerate(taps):
        value = jnp.where(at == a, tap, value)
    return value


def kernel(
    counts,
    model_ref,
    frames_ref,
    rows_in,
    cols_in,
    dither_in,
    footprint_in,
    cut_in,
    out_ref,
    rows_ref,
    cols_ref,
    dither_ref,
    footprint_ref,
    cut_ref,
    grid_ref,
    own_ref,
    frame_ref,
    row_out,
    row_in,
    aux_out,
    aux_in,
    side_out,
    side_in,
    model_stack,
    ahead_ref,
    rowed_ref,
    pred_ref,
    back_ref,
    stack_ref,
    total_ref,
    inter_ref,
    local_sem,
    small_sem,
    here_visit,
    here_sky,
    frame_send,
    frame_recv,
    row_send,
    row_recv,
    aux_send,
    aux_recv,
    side_send,
    side_recv,
    rim_send,
    rim_recv,
):
    sky_count, visit_count = counts
    height, width = out_ref.shape
    low_rows, low_cols = frame_ref.shape[2:]
    full_cols = grid_ref.shape[1]
    half_cols = full_cols // 2
    blocks = full_cols // (2 * LANES)
    visits = rows_ref.shape[0]
    tile = lax.axis_index("tiles")
    sky = lax.axis_index("sky")
    visit = lax.axis_index("visit")
    has_up, has_down = sky > 0, sky < sky_count - 1
    has_left, has_right = visit > 0, visit < visit_count - 1
    f32, bf16 = jnp.float32, jnp.bfloat16

    def remote(source, target, send, recv, device):
        return pltpu.make_async_remote_copy(
            src_ref=source, dst_ref=target, send_sem=send, recv_sem=recv, device_id=device, device_id_type=MESH
        )

    def at_visit(q):
        return (tile, sky, q)

    def at_sky(step):
        return (tile, sky + step, visit)

    ways = ((0, has_up, has_down), (1, has_down, has_up))

    def columns_of(q):
        return pl.ds(pl.multiple_of(q * low_cols, low_cols), low_cols)

    def frame_copy(peer, owner):
        return remote(
            frames_ref.at[:, :, columns_of(peer)],
            frame_ref.at[owner],
            frame_send.at[peer],
            frame_recv.at[owner],
            at_visit(peer),
        )

    def aux_copy(peer, owner):
        return remote(aux_out.at[peer], aux_in.at[owner], aux_send.at[peer], aux_recv.at[owner], at_visit(peer))

    def row_copy(way):
        return remote(row_out.at[way], row_in.at[way], row_send.at[way], row_recv.at[way], at_sky(2 * way - 1))

    def side_copy(side):
        return remote(
            side_out.at[side], side_in.at[side], side_send.at[side], side_recv.at[side], at_visit(visit + 2 * side - 1)
        )

    def rim_copy(way):
        source = model_ref.at[pl.ds((height - ROWS) * way, ROWS), :]
        target = grid_ref.at[pl.ds((ROWS + height) * (1 - way), ROWS), pl.ds(0, width)]
        return remote(source, target, rim_send.at[way], rim_recv.at[way], at_sky(2 * way - 1))

    own_frames = pltpu.make_async_copy(frames_ref, own_ref, local_sem.at[1])
    small = [
        pltpu.make_async_copy(source, target, small_sem.at[n])
        for n, (source, target) in enumerate(
            (
                (rows_in, rows_ref),
                (cols_in, cols_ref),
                (dither_in, dither_ref),
                (footprint_in, footprint_ref),
                (cut_in, cut_ref),
            )
        )
    ]
    own_model = pltpu.make_async_copy(
        model_ref, grid_ref.at[pl.ds(ROWS, height), pl.ds(0, width)], local_sem.at[0]
    )
    own_block = pltpu.make_async_copy(frames_ref.at[:, :, columns_of(visit)], frame_ref.at[visit], local_sem.at[2])
    own_frames.start()
    own_model.start()
    for copy in small:
        copy.start()
    barrier = pltpu.get_barrier_semaphore()
    is_odd = sky % 2 > 0

    def greet(q, carry):
        pl.semaphore_signal(barrier, inc=1, device_id=at_visit(q), device_id_type=MESH)
        return carry

    lax.fori_loop(visit + 1, visit_count, greet, 0)
    for way, ok, _ in ways:

        @pl.when(ok & is_odd)
        def _():
            pl.semaphore_signal(barrier, inc=1, device_id=at_sky(2 * way - 1), device_id_type=MESH)

    beside = has_up.astype(jnp.int32) + has_down.astype(jnp.int32)
    smaller = visit + jnp.where(is_odd, 0, beside)

    @pl.when(smaller > 0)
    def _():
        pl.semaphore_wait(barrier, smaller)

    def answer(q, carry):
        pl.semaphore_signal(here_visit.at[visit], inc=1, device_id=at_visit(q), device_id_type=MESH)
        return carry

    lax.fori_loop(0, visit, answer, 0)

    for way, ok, _ in ways:

        @pl.when(ok & jnp.logical_not(is_odd))
        def _():
            pl.semaphore_signal(here_sky.at[1 - way], inc=1, device_id=at_sky(2 * way - 1), device_id_type=MESH)

    @pl.when(visit > 1)
    def _():
        frame_copy(0, visit).start()

    for way, ok, _ in ways:

        @pl.when(ok & jnp.logical_not(is_odd))
        def _():
            rim_copy(way).start()

    own_block.start()

    @pl.when(jnp.logical_not(has_up))
    def _():
        grid_ref[0:ROWS, 0:width] = jnp.zeros((ROWS, width), f32)
        row_in[1] = jnp.zeros(row_in.shape[1:], bf16)

    @pl.when(jnp.logical_not(has_down))
    def _():
        grid_ref[ROWS + height :, 0:width] = jnp.zeros((ROWS, width), f32)
        row_in[0] = jnp.zeros(row_in.shape[1:], bf16)

    own_frames.wait()
    sub8 = iota((8, LANES), 0)
    lane8 = iota((8, LANES), 1)
    blank8 = jnp.zeros((8, LANES), f32)
    low_blocks = low_cols // LANES
    for way in range(2):
        piled, moved = [], []
        for n in range(low_blocks * visit_count):
            cols = slice(LANES * n, LANES * (n + 1))
            if way == 0:
                first = own_ref[0, 0:16, cols].astype(f32)[0:8]
                second = turn(own_ref[1, 0:16, cols].astype(f32)[0:8], 2, 0)
            else:
                first = turn(own_ref[0, low_rows - 16 : low_rows, cols].astype(f32)[8:16], 2, 0)
                second = turn(own_ref[1, low_rows - 16 : low_rows, cols].astype(f32)[8:16], 4, 0)
            piled.append(jnp.where(sub8 < 2, first, second))
            moved.append(turn(piled[-1], 4, 0))
        for p in range(visit_count):
            n = low_blocks * p
            for b in range(low_blocks // 4):
                tiles = [jnp.where(sub8 < 4, piled[m], moved[m + 1]) for m in (n + 4 * b, n + 4 * b + 2)]
                row_out[way, p, 16 * b : 16 * (b + 1), :] = jnp.concatenate(tiles, axis=0).astype(bf16)
            ends = moved if way else piled
            corner = jnp.where(lane8 < LANES // 2, ends[(n + low_blocks) % len(ends)], ends[n - 1])
            row_out[way, p, 16:32, :] = jnp.concatenate([corner, blank8], axis=0).astype(bf16)
    for p in range(visit_count):
        right = low_cols * (p + 1) if p < visit_count - 1 else 0
        left = low_cols * p - LANES if p > 0 else 0
        packed = blank8
        for j in range(PAIR):
            for u in range(low_rows // 16):
                after = own_ref[j, 16 * u : 16 * (u + 1), right : right + LANES].astype(f32)
                before = own_ref[j, 16 * u : 16 * (u + 1), left : left + LANES].astype(f32)
                for n in range(2):
                    g = (low_rows * j + 16 * u) // 8 + n
                    piece = jnp.where(lane8 < LANES // 2, after[8 * n : 8 * (n + 1)], before[8 * n : 8 * (n + 1)])
                    packed = jnp.where((lane8 - 4 * g + 2 + LANES) % LANES < 4, turn(piece, 4 * g, 1), packed)
        aux_out[p, 32:48, :] = jnp.concatenate([blank8, packed], axis=0).astype(bf16)

    for way, ok, _ in ways:

        @pl.when(ok & jnp.logical_not(is_odd))
        def _():
            row_copy(way).start()

    for way, ok, _ in ways:

        @pl.when(ok & is_odd)
        def _():
            pl.semaphore_wait(here_sky.at[way], 1)
            row_copy(way).start()
            rim_copy(way).start()

    for copy in small:
        copy.wait()
    share = 1.0 / float(visits) ** 0.5

    def col_shift(k):
        return (dither_ref[1, k] + 4) // 2 - 2

    def col_weights(k):
        odd = dither_ref[1, k] - 2 * col_shift(k)
        weights = []
        for d in range(SHIFTS):
            value = jnp.where(odd > 0, cols_ref[k, max(d - 1, 0)], cols_ref[k, min(d, TAPS - 1)])
            weights.append(jnp.where(odd > 0, 0.0, value) if d == 0 else value)
        weights[TAPS] = jnp.where(odd > 0, weights[TAPS], 0.0)
        return weights

    def row_of_halo(n):
        return jnp.where(n % 8 < 4, low_rows + n % 2, n % 2 - 2)

    lane = iota((16, DEPTH), 1)
    row = iota((16, DEPTH), 0)
    model_row = lane % SLOT - ROWS
    is_low = lane >= 2 * SLOT
    blank = lane >= 3 * SLOT
    far = 4 * height

    def low_part(value):
        return jnp.where(is_low, value - value.astype(bf16).astype(f32), value).astype(bf16)

    slot = lane % SLOT
    source_row = jnp.where(slot < 2 * low_rows, slot % low_rows, row_of_halo(slot))
    source_row = jnp.where((slot >= 2 * low_rows + 8) | blank, far, source_row)
    second_visit = jnp.where(slot < 2 * low_rows, slot // low_rows, slot % 4 // 2) > 0
    base_main = jnp.where(blank, -far, model_row + TAPS // 2 - 2 * row)
    halo_row = jnp.where(row < 8, row_of_halo(row), far)
    base_halo = jnp.where(blank, -far, model_row + TAPS // 2 - 2 * halo_row)
    base_back = row + TAPS // 2 - 2 * source_row

    def build(c, carry):
        k0, k1 = PAIR * c, PAIR * c + 1
        shift0, shift1 = dither_ref[0, k0], dither_ref[0, k1]
        taps0 = [rows_ref[k0, a] for a in range(TAPS)]
        taps1 = [rows_ref[k1, a] for a in range(TAPS)]
        for j, (shift, taps) in enumerate(((shift0, taps0), (shift1, taps1))):
            for u in range(low_rows // 16):
                begin = low_rows * j + 16 * u
                ahead_ref[c, begin : begin + 16, :] = low_part(pick(base_main - (32 * u + shift), taps))
        upper = row % 4 < 2
        ahead_ref[c, 2 * low_rows : SLOT, :] = low_part(
            pick(
                base_halo - jnp.where(upper, shift0, shift1),
                [jnp.where(upper, a, b) for a, b in zip(taps0, taps1)],
            )
        )
        taps = [jnp.where(second_visit, b, a) for a, b in zip(taps0, taps1)]
        weights = [
            jnp.where(second_visit, b * share, a * share) for a, b in zip(col_weights(k0), col_weights(k1))
        ]
        base = base_back - jnp.where(second_visit, shift1, shift0)
        for u in range(height // 16):
            value = pick(base + 16 * u, taps)
            for d in range(SHIFTS):
                begin = height * d + 16 * u
                back_ref[c, begin : begin + 16, :] = low_part(value * weights[d])
        return carry

    lax.fori_loop(0, visit_count, build, 0)

    own_model.wait()

    @pl.when(has_down)
    def _():
        rim_copy(0).wait_recv()

    @pl.when(has_up)
    def _():
        rim_copy(1).wait_recv()

    groups = (height + 2 * ROWS) // 8
    for side in range(2):
        packed = jnp.zeros((8, LANES), f32)
        begin = (width - LANES) * side
        for t in range(groups):
            piece = turn(grid_ref[8 * t : 8 * (t + 1), begin : begin + LANES], 8 * t + 8 * side, 1)
            packed = jnp.where((lane8 >= 8 * t) & (lane8 < 8 * t + 8), piece, packed)
        side_out[side] = packed

    @pl.when(has_left)
    def _():
        side_copy(0).start()

    for way, _, ok in ways:

        @pl.when(ok)
        def _():
            row_copy(way).wait_recv()

    for p in range(visit_count):
        aux_out[p, 0:16, :] = row_in[0, p, 0:16, :]
        aux_out[p, 16:32, :] = row_in[1, p, 0:16, :]
        down, up = [row_in[way, p, 16:32, :].astype(f32)[0:8] for way in range(2)]
        packed = aux_out[p, 32:48, :].astype(f32)[8:16]
        aux_out[p, 32:48, :] = jnp.concatenate([jnp.where(sub8 < 4, down, up), packed], axis=0).astype(bf16)
    aux_in[visit] = aux_out[visit]

    def send_low(q, carry):
        aux_copy(q, visit).start()
        return carry

    lax.fori_loop(0, visit, send_low, 0)

    def send_main(q, carry):
        frame_copy(q, visit).start()
        return carry

    lax.fori_loop((visit > 1).astype(jnp.int32), visit, send_main, 0)

    def send_high(q, carry):
        pl.semaphore_wait(here_visit.at[q], 1)

        @pl.when(q == visit + 1)
        def _():
            side_copy(1).start()

        aux_copy(q, visit).start()
        frame_copy(q, visit).start()
        return carry

    following = jnp.where(visit > 0, visit_count, jnp.minimum(visit + 2, visit_count))
    lax.fori_loop(visit + 1, following, send_high, 0)

    model_stack[3 * SLOT : DEPTH, :] = jnp.zeros((DEPTH - 3 * SLOT, full_cols), bf16)
    stack_ref[3 * SLOT : DEPTH, :] = jnp.zeros((DEPTH - 3 * SLOT, half_cols), bf16)

    spread = selection(
        (2 * LANES, 2 * LANES),
        lambda a, b: a == jnp.where(b < LANES, 2 * b, 2 * b - (2 * LANES - 1)),
    )
    operator = ahead_ref[...].reshape(visit_count * SLOT, DEPTH)

    def rows_ahead(some):
        parts = [halves(grid_ref[:, 2 * LANES * n : 2 * LANES * (n + 1)]) for n in some]
        apart = dot(jnp.concatenate([part for pair in parts for part in pair], axis=0), spread).astype(bf16)
        for m, n in enumerate(some):
            cols = slice(2 * LANES * n, 2 * LANES * (n + 1))
            high = apart[2 * SLOT * m : 2 * SLOT * m + SLOT]
            model_stack[0:SLOT, cols] = high
            model_stack[SLOT : 2 * SLOT, cols] = apart[2 * SLOT * m + SLOT : 2 * SLOT * (m + 1)]
            model_stack[2 * SLOT : 3 * SLOT, cols] = high
            rowed_ref[:, :, cols] = dot(operator, model_stack[:, cols]).reshape(visit_count, SLOT, 2 * LANES)

    rows_ahead(range(blocks - 1))

    first_lane, last_lane = lane8 == 0, lane8 == LANES - 1
    upper8 = sub8 % 4 < 2

    def row_groups(c):
        weights0, weights1 = col_weights(PAIR * c), col_weights(PAIR * c + 1)
        for g in range(2 * low_rows // 8 + 1):
            if g < low_rows // 8:
                weights = weights0
            elif g < 2 * low_rows // 8:
                weights = weights1
            else:
                weights = [jnp.where(upper8, a, b) for a, b in zip(weights0, weights1)]
            yield slice(8 * g, 8 * (g + 1)), weights

    def tap(c, rows, weights, n, step):
        even = rowed_ref[c, rows, 2 * LANES * n : 2 * LANES * n + LANES]
        odd = rowed_ref[c, rows, 2 * LANES * n + LANES : 2 * LANES * (n + 1)]
        value = weights[2 * step + 2] * even + weights[2 * step + 3] * odd
        return turn(value, -step, 1)

    last = blocks - 1

    def predict(c):
        for rows, weights in row_groups(c):
            before, here, after = [[tap(c, rows, weights, n, step) for n in range(last)] for step in (-1, 0, 1)]
            for n in range(last):
                value = here[n] + jnp.where(first_lane, before[n - 1] if n else 0.0, before[n])
                value = value + jnp.where(last_lane, after[n + 1] if n < last - 1 else 0.0, after[n])
                pred_ref[c, rows, LANES * n : LANES * (n + 1)] = value

    def predict_ends(c):
        for rows, weights in row_groups(c):
            before, here, after = [tap(c, rows, weights, last, step) for step in (-1, 0, 1)]
            value = here + jnp.where(first_lane, tap(c, rows, weights, last - 1, -1), before)
            value = value + jnp.where(last_lane, tap(c, rows, weights, 0, 1), after)
            pred_ref[c, rows, LANES * last : LANES * blocks] = value
            pred_ref[c, rows, 0:LANES] += jnp.where(first_lane, before, 0.0)
            pred_ref[c, rows, LANES * (last - 1) : LANES * last] += jnp.where(last_lane, after, 0.0)

    def by_four(body):
        def four(n, carry):
            for c in range(4):
                body(4 * n + c)
            return carry

        return four

    fours = visit_count // 4
    early = jnp.where(visit > 0, 0, fours)
    lax.fori_loop(0, early, by_four(predict), 0)
    lax.fori_loop(following, visit_count, send_high, 0)
    lax.fori_loop(early, fours, by_four(predict), 0)

    for side, ok in ((0, has_right), (1, has_left)):
        begin = width + LANES * side

        @pl.when(ok)
        def _():
            side_copy(side).wait_recv()
            packed = side_in[side]
            keep = lane8 >= LANES - 8 if side else lane8 < 8
            for t in range(groups):
                piece = turn(packed, -8 * t - 8 * side, 1)
                grid_ref[8 * t : 8 * (t + 1), begin : begin + LANES] = jnp.where(keep, piece, 0.0)

        @pl.when(jnp.logical_not(ok))
        def _():
            grid_ref[:, begin : begin + LANES] = jnp.zeros((height + 2 * ROWS, LANES), f32)

    rows_ahead([last])
    lax.fori_loop(0, fours, by_four(predict_ends), 0)

    own_block.wait()
    row16 = iota((16, LANES), 0)
    lane16 = iota((16, LANES), 1)
    halo_index = row_of_halo(iota((16, LANES), 0)) + sky * low_rows
    upper16 = row16 % 4 < 2
    columns = [lane16 + LANES * n for n in range(blocks - 1)]
    columns.append(jnp.where(lane16 < LANES // 2, lane16 + low_cols, lane16 - LANES))
    columns = [value + visit * low_cols for value in columns]
    all_cols = low_cols * visit_count

    order = [sorted(range(visit_count), key=lambda q: (abs(q - v), q)) for v in range(visit_count)]

    def owner_of(o):
        owner = jnp.int32(0)
        for v in range(visit_count):
            for n in range(visit_count):
                if order[v][n]:
                    owner = jnp.where((visit == v) & (o == n), order[v][n], owner)
        return owner

    def shifted(values, shift):
        turned = [pltpu.roll(value, jnp.where(shift < 0, LANES - 1, shift), 1) for value in values]
        to_right, to_left = (lane16 == 0) & (shift > 0), (lane16 == LANES - 1) & (shift < 0)
        return [
            jnp.where(to_right, turned[n - 1], jnp.where(to_left, turned[(n + 1) % blocks], turned[n]))
            for n in range(blocks)
        ]

    def limits(limit, shift):
        result = []
        for n in range(blocks):
            if 0 < n < blocks - 2:
                result.append(limit)
            else:
                result.append(jnp.where((columns[n] >= shift) & (columns[n] < all_cols + shift), limit, 0.0))
        return result

    def put(begin, predicted, values, limit):
        for n in range(blocks):
            cols = slice(LANES * n, LANES * (n + 1))
            error = predicted[n] - values[n]
            high, low = halves(jnp.minimum(jnp.maximum(error, -limit[n]), limit[n]))
            stack_ref[begin : begin + 16, cols] = high
            stack_ref[SLOT + begin : SLOT + begin + 16, cols] = low
            stack_ref[2 * SLOT + begin : 2 * SLOT + begin + 16, cols] = high

    def arrived(c):
        frame_copy(c, c).wait_recv()
        aux_copy(c, c).wait_recv()

    def work(c, is_first):
        rest = aux_in[c, 32:48, :].astype(f32)
        packed = rest[8:16]
        shifts = [col_shift(PAIR * c + j) for j in range(PAIR)]
        for j in range(PAIR):
            k = PAIR * c + j
            cut, first, last = cut_ref[k], footprint_ref[0, k], footprint_ref[1, k]
            for u in range(low_rows // 16):
                begin = low_rows * j + 16 * u
                start = sky * low_rows + 16 * u
                rows = slice(16 * u, 16 * (u + 1))
                values = [
                    frame_ref[c, j, rows, LANES * n : LANES * (n + 1)].astype(f32) for n in range(blocks - 1)
                ]
                g = begin // 8
                values.append(jnp.concatenate([turn(packed, -4 * g, 1), turn(packed, -4 * (g + 1), 1)], axis=0))
                limit = jnp.where((row16 >= first - start) & (row16 < last - start), cut, 0.0)
                predicted = [pred_ref[c, begin : begin + 16, LANES * n : LANES * (n + 1)] for n in range(blocks)]
                put(begin, predicted, shifted(values, shifts[j]), limits(limit, shifts[j]))
        k0, k1 = PAIR * c, PAIR * c + 1
        begin = 2 * low_rows
        values = []
        for _ in range(low_blocks // 4):
            down, up = [aux_in[c, 16 * way : 16 * (way + 1), :].astype(f32) for way in range(2)]
            for n in range(2):
                down8, up8 = down[8 * n : 8 * (n + 1)], up[8 * n : 8 * (n + 1)]
                values.append(jnp.where(sub8 < 4, down8, turn(up8, 4, 0)))
                values.append(jnp.where(sub8 < 4, turn(down8, 4, 0), up8))
        values.append(rest[0:8])
        values = [jnp.concatenate([value, blank8], axis=0) for value in values]
        values = [jnp.where(upper16, a, b) for a, b in zip(shifted(values, shifts[0]), shifted(values, shifts[1]))]
        inside = (halo_index >= jnp.where(upper16, footprint_ref[0, k0], footprint_ref[0, k1])) & (
            halo_index < jnp.where(upper16, footprint_ref[1, k0], footprint_ref[1, k1])
        )
        limit = jnp.where(inside & (row16 < 8), jnp.where(upper16, cut_ref[k0], cut_ref[k1]), 0.0)
        predicted = [
            jnp.concatenate([pred_ref[c, begin : begin + 8, LANES * n : LANES * (n + 1)], blank8], axis=0)
            for n in range(blocks)
        ]
        put(begin, predicted, values, limits(limit, jnp.where(upper16, shifts[0], shifts[1])))
        for begin in range(0, half_cols, 2 * LANES):
            cols = slice(begin, min(begin + 2 * LANES, half_cols))
            product = dot(back_ref[c], stack_ref[:, cols])
            total_ref[:, cols] = product if is_first else total_ref[:, cols] + product

    owners = [owner_of(o) for o in range(visit_count)]
    work(owners[0], True)

    def next_col(value):
        return pltpu.roll(value, full_cols - 1, 1)

    strip = 16
    for t in range(height // strip):
        above = grid_ref[ROWS - 1 + strip * t : ROWS - 1 + strip * (t + 1), :]
        here = grid_ref[ROWS + strip * t : ROWS + strip * (t + 1), :]
        below = grid_ref[ROWS + 1 + strip * t : ROWS + 1 + strip * (t + 1), :]
        gx, gy = here - above, next_col(above) - above
        value = gx * lax.rsqrt(gx * gx + gy * gy + eps_flux)
        gx, gy = below - here, next_col(here) - here
        scale = lax.rsqrt(gx * gx + gy * gy + eps_flux)
        flux = gy * scale
        value = value - gx * scale + (pltpu.roll(flux, 1, 1) - flux)
        out_ref[strip * t : strip * (t + 1), :] = tv_weight * value[:, :width]

    for c in owners[1:-1]:
        arrived(c)
    for c in owners[1:-1]:
        work(c, False)
    arrived(owners[-1])
    work(owners[-1], False)

    join = selection(
        (4 * LANES, 2 * LANES),
        lambda a, b: b == jnp.where(a % (2 * LANES) < LANES, 2 * (a % LANES), 2 * (a % LANES) + 1),
    )
    for u in range(height // 16):
        parts = []
        for odd in range(2):
            value = None
            for step in range(-1, 2):
                begin = height * (2 * (step + 1) + odd) + 16 * u
                piece = turn(total_ref[begin : begin + 16, :], step, 1)
                value = piece if value is None else value + piece
            parts.append(halves(value[:, :low_cols]))
        for b in range(low_cols // LANES):
            cols = slice(LANES * b, LANES * (b + 1))
            for n, part in enumerate((parts[0][0], parts[1][0], parts[0][1], parts[1][1])):
                inter_ref[height * b + 16 * u : height * b + 16 * (u + 1), LANES * n : LANES * (n + 1)] = part[:, cols]
    joined = dot(inter_ref[...], join)
    for b in range(low_cols // LANES):
        out_ref[:, 2 * LANES * b : 2 * LANES * (b + 1)] += joined[height * b : height * (b + 1)]

    def sent(q, carry):
        @pl.when(q != visit)
        def _():
            frame_copy(q, visit).wait_send()
            aux_copy(q, visit).wait_send()

        return carry

    lax.fori_loop(0, visit_count, sent, 0)
    for side, ok in ((0, has_left), (1, has_right)):

        @pl.when(ok)
        def _():
            side_copy(side).wait_send()

    for way, ok in ((0, has_up), (1, has_down)):

        @pl.when(ok)
        def _():
            rim_copy(way).wait_send()
            row_copy(way).wait_send()


def solution(mesh):
    in_specs = (
        P(("tiles", "sky"), "visit"),
        P(("tiles", "visit"), "sky", None),
        P("tiles", None),
        P("tiles", None),
        P("tiles", None),
        P("tiles", None),
        P("tiles"),
    )
    out_specs = P(("tiles", "sky"), "visit")
    sky_count, visit_count = mesh.shape["sky"], mesh.shape["visit"]

    def on_device(sky_model, frames, psf_rows, psf_cols, dither, footprint, huber_cut):
        height, width = sky_model.shape
        per_device, low_rows, all_cols = frames.shape
        visits = psf_rows.shape[0]
        low_cols = all_cols // visit_count
        half_cols = width // 2 + LANES
        f32, bf16 = jnp.float32, jnp.bfloat16
        arguments = [
            pltpu.with_memory_space_constraint(x, pltpu.HBM)
            for x in (sky_model, frames, psf_rows, psf_cols, dither.T, footprint.T, huber_cut)
        ]
        dma = pltpu.SemaphoreType.DMA
        return pl.pallas_call(
            functools.partial(kernel, (sky_count, visit_count)),
            out_shape=pltpu.VMEM((height, width), f32),
            in_specs=[pl.BlockSpec(memory_space=pltpu.HBM)] * 7,
            out_specs=pl.BlockSpec(memory_space=pltpu.VMEM),
            scratch_shapes=[
                pltpu.SMEM(psf_rows.shape, f32),
                pltpu.SMEM(psf_cols.shape, f32),
                pltpu.SMEM(dither.shape[::-1], jnp.int32),
                pltpu.SMEM(footprint.shape[::-1], jnp.int32),
                pltpu.SMEM(huber_cut.shape, f32),
                pltpu.VMEM((height + 2 * ROWS, width + 2 * LANES), f32),
                pltpu.VMEM(frames.shape, bf16),
                pltpu.VMEM((visit_count, per_device, low_rows, low_cols), bf16),
                pltpu.VMEM((2, visit_count, 32, LANES), bf16),
                pltpu.VMEM((2, visit_count, 32, LANES), bf16),
                pltpu.VMEM((visit_count, 48, LANES), bf16),
                pltpu.VMEM((visit_count, 48, LANES), bf16),
                pltpu.VMEM((2, 8, LANES), f32),
                pltpu.VMEM((2, 8, LANES), f32),
                pltpu.VMEM((DEPTH, 2 * half_cols), bf16),
                pltpu.VMEM((visit_count, SLOT, DEPTH), bf16),
                pltpu.VMEM((visit_count, SLOT, 2 * half_cols), f32),
                pltpu.VMEM((visit_count, SLOT, half_cols), f32),
                pltpu.VMEM((visit_count, SHIFTS * height, DEPTH), bf16),
                pltpu.VMEM((DEPTH, half_cols), bf16),
                pltpu.VMEM((SHIFTS * height, half_cols), f32),
                pltpu.VMEM((low_cols // LANES * height, 4 * LANES), bf16),
                dma((3,)),
                dma((5,)),
                pltpu.SemaphoreType.REGULAR((visit_count,)),
                pltpu.SemaphoreType.REGULAR((2,)),
                dma((visit_count,)),
                dma((visit_count,)),
                dma((2,)),
                dma((2,)),
                dma((visit_count,)),
                dma((visit_count,)),
                dma((2,)),
                dma((2,)),
                dma((2,)),
                dma((2,)),
            ],
            compiler_params=pltpu.CompilerParams(
                collective_id=0, has_side_effects=True, vmem_limit_bytes=48 * 1024 * 1024
            ),
        )(*arguments)

    return jax.shard_map(
        on_device, mesh=mesh, in_specs=in_specs, out_specs=out_specs, check_vma=False
    )
```

```python
import functools

import jax
import jax.numpy as jnp
from jax import lax
from jax.experimental import pallas as pl
from jax.experimental.pallas import tpu as pltpu
from jax.sharding import PartitionSpec as P

TAPS = 5
SHIFTS = TAPS + 1

eps_flux = 0.1
tv_weight = 0.5

ROWS = 8
LANES = 128
PAIR = 2
SLOT = 80
DEPTH = 256
MESH = pl.DeviceIdType.MESH


def dot(a, b):
    return jnp.dot(a, b, preferred_element_type=jnp.float32)


def iota(shape, dim):
    return lax.broadcasted_iota(jnp.int32, shape, dim)


def selection(shape, source_of):
    row, col = iota(shape, 0), iota(shape, 1)
    return jnp.where(source_of(row, col), 1.0, 0.0).astype(jnp.bfloat16)


def halves(value):
    high = value.astype(jnp.bfloat16)
    return high, (value - high.astype(jnp.float32)).astype(jnp.bfloat16)


def turn(value, shift, axis):
    shift %= value.shape[axis]
    return pltpu.roll(value, shift, axis) if shift else value


def pick(at, taps):
    value = jnp.zeros(at.shape, jnp.float32)
    for a, tap in enumerate(taps):
        value = jnp.where(at == a, tap, value)
    return value


def kernel(
    counts,
    model_ref,
    frames_ref,
    rows_in,
    cols_in,
    dither_in,
    footprint_in,
    cut_in,
    out_ref,
    rows_ref,
    cols_ref,
    dither_ref,
    footprint_ref,
    cut_ref,
    grid_ref,
    own_ref,
    frame_ref,
    row_out,
    row_in,
    aux_out,
    aux_in,
    side_out,
    side_in,
    model_stack,
    ahead_ref,
    rowed_ref,
    pred_ref,
    back_ref,
    stack_ref,
    total_ref,
    inter_ref,
    local_sem,
    small_sem,
    here_visit,
    here_sky,
    frame_send,
    frame_recv,
    row_send,
    row_recv,
    aux_send,
    aux_recv,
    side_send,
    side_recv,
    rim_send,
    rim_recv,
):
    sky_count, visit_count = counts
    height, width = out_ref.shape
    low_rows, low_cols = frame_ref.shape[2:]
    full_cols = grid_ref.shape[1]
    half_cols = full_cols // 2
    blocks = full_cols // (2 * LANES)
    visits = rows_ref.shape[0]
    tile = lax.axis_index("tiles")
    sky = lax.axis_index("sky")
    visit = lax.axis_index("visit")
    has_up, has_down = sky > 0, sky < sky_count - 1
    has_left, has_right = visit > 0, visit < visit_count - 1
    f32, bf16 = jnp.float32, jnp.bfloat16

    def remote(source, target, send, recv, device):
        return pltpu.make_async_remote_copy(
            src_ref=source, dst_ref=target, send_sem=send, recv_sem=recv, device_id=device, device_id_type=MESH
        )

    def at_visit(q):
        return (tile, sky, q)

    def at_sky(step):
        return (tile, sky + step, visit)

    ways = ((0, has_up, has_down), (1, has_down, has_up))

    def columns_of(q):
        return pl.ds(pl.multiple_of(q * low_cols, low_cols), low_cols)

    def frame_copy(peer, owner):
        return remote(
            frames_ref.at[:, :, columns_of(peer)],
            frame_ref.at[owner],
            frame_send.at[peer],
            frame_recv.at[owner],
            at_visit(peer),
        )

    def aux_copy(peer, owner):
        return remote(aux_out.at[peer], aux_in.at[owner], aux_send.at[peer], aux_recv.at[owner], at_visit(peer))

    def row_copy(way):
        return remote(row_out.at[way], row_in.at[way], row_send.at[way], row_recv.at[way], at_sky(2 * way - 1))

    def side_copy(side):
        return remote(
            side_out.at[side], side_in.at[side], side_send.at[side], side_recv.at[side], at_visit(visit + 2 * side - 1)
        )

    def rim_copy(way):
        source = model_ref.at[pl.ds((height - ROWS) * way, ROWS), :]
        target = grid_ref.at[pl.ds((ROWS + height) * (1 - way), ROWS), pl.ds(0, width)]
        return remote(source, target, rim_send.at[way], rim_recv.at[way], at_sky(2 * way - 1))

    own_frames = pltpu.make_async_copy(frames_ref, own_ref, local_sem.at[1])
    small = [
        pltpu.make_async_copy(source, target, small_sem.at[n])
        for n, (source, target) in enumerate(
            (
                (rows_in, rows_ref),
                (cols_in, cols_ref),
                (dither_in, dither_ref),
                (footprint_in, footprint_ref),
                (cut_in, cut_ref),
            )
        )
    ]
    own_model = pltpu.make_async_copy(
        model_ref, grid_ref.at[pl.ds(ROWS, height), pl.ds(0, width)], local_sem.at[0]
    )
    own_block = pltpu.make_async_copy(frames_ref.at[:, :, columns_of(visit)], frame_ref.at[visit], local_sem.at[2])
    own_frames.start()
    own_model.start()
    for copy in small:
        copy.start()
    barrier = pltpu.get_barrier_semaphore()
    is_odd = sky % 2 > 0

    def greet(q, carry):
        pl.semaphore_signal(barrier, inc=1, device_id=at_visit(q), device_id_type=MESH)
        return carry

    lax.fori_loop(visit + 1, visit_count, greet, 0)
    for way, ok, _ in ways:

        @pl.when(ok & is_odd)
        def _():
            pl.semaphore_signal(barrier, inc=1, device_id=at_sky(2 * way - 1), device_id_type=MESH)

    beside = has_up.astype(jnp.int32) + has_down.astype(jnp.int32)
    smaller = visit + jnp.where(is_odd, 0, beside)

    @pl.when(smaller > 0)
    def _():
        pl.semaphore_wait(barrier, smaller)

    def answer(q, carry):
        pl.semaphore_signal(here_visit.at[visit], inc=1, device_id=at_visit(q), device_id_type=MESH)
        return carry

    lax.fori_loop(0, visit, answer, 0)

    for way, ok, _ in ways:

        @pl.when(ok & jnp.logical_not(is_odd))
        def _():
            pl.semaphore_signal(here_sky.at[1 - way], inc=1, device_id=at_sky(2 * way - 1), device_id_type=MESH)

    @pl.when(visit > 1)
    def _():
        frame_copy(0, visit).start()

    for way, ok, _ in ways:

        @pl.when(ok & jnp.logical_not(is_odd))
        def _():
            rim_copy(way).start()

    own_block.start()

    @pl.when(jnp.logical_not(has_up))
    def _():
        grid_ref[0:ROWS, 0:width] = jnp.zeros((ROWS, width), f32)
        row_in[1] = jnp.zeros(row_in.shape[1:], bf16)

    @pl.when(jnp.logical_not(has_down))
    def _():
        grid_ref[ROWS + height :, 0:width] = jnp.zeros((ROWS, width), f32)
        row_in[0] = jnp.zeros(row_in.shape[1:], bf16)

    own_frames.wait()
    sub8 = iota((8, LANES), 0)
    lane8 = iota((8, LANES), 1)
    blank8 = jnp.zeros((8, LANES), f32)
    low_blocks = low_cols // LANES
    for way in range(2):
        piled, moved = [], []
        for n in range(low_blocks * visit_count):
            cols = slice(LANES * n, LANES * (n + 1))
            if way == 0:
                first = own_ref[0, 0:16, cols].astype(f32)[0:8]
                second = turn(own_ref[1, 0:16, cols].astype(f32)[0:8], 2, 0)
            else:
                first = turn(own_ref[0, low_rows - 16 : low_rows, cols].astype(f32)[8:16], 2, 0)
                second = turn(own_ref[1, low_rows - 16 : low_rows, cols].astype(f32)[8:16], 4, 0)
            piled.append(jnp.where(sub8 < 2, first, second))
            moved.append(turn(piled[-1], 4, 0))
        for p in range(visit_count):
            n = low_blocks * p
            for b in range(low_blocks // 4):
                tiles = [jnp.where(sub8 < 4, piled[m], moved[m + 1]) for m in (n + 4 * b, n + 4 * b + 2)]
                row_out[way, p, 16 * b : 16 * (b + 1), :] = jnp.concatenate(tiles, axis=0).astype(bf16)
            ends = moved if way else piled
            corner = jnp.where(lane8 < LANES // 2, ends[(n + low_blocks) % len(ends)], ends[n - 1])
            row_out[way, p, 16:32, :] = jnp.concatenate([corner, blank8], axis=0).astype(bf16)
    for p in range(visit_count):
        right = low_cols * (p + 1) if p < visit_count - 1 else 0
        left = low_cols * p - LANES if p > 0 else 0
        packed = blank8
        for j in range(PAIR):
            for u in range(low_rows // 16):
                after = own_ref[j, 16 * u : 16 * (u + 1), right : right + LANES].astype(f32)
                before = own_ref[j, 16 * u : 16 * (u + 1), left : left + LANES].astype(f32)
                for n in range(2):
                    g = (low_rows * j + 16 * u) // 8 + n
                    piece = jnp.where(lane8 < LANES // 2, after[8 * n : 8 * (n + 1)], before[8 * n : 8 * (n + 1)])
                    packed = jnp.where((lane8 - 4 * g + 2 + LANES) % LANES < 4, turn(piece, 4 * g, 1), packed)
        aux_out[p, 32:48, :] = jnp.concatenate([blank8, packed], axis=0).astype(bf16)

    for way, ok, _ in ways:

        @pl.when(ok & jnp.logical_not(is_odd))
        def _():
            row_copy(way).start()

    for way, ok, _ in ways:

        @pl.when(ok & is_odd)
        def _():
            pl.semaphore_wait(here_sky.at[way], 1)
            row_copy(way).start()
            rim_copy(way).start()

    for copy in small:
        copy.wait()
    share = 1.0 / float(visits) ** 0.5

    def col_shift(k):
        return (dither_ref[1, k] + 4) // 2 - 2

    def col_weights(k):
        odd = dither_ref[1, k] - 2 * col_shift(k)
        weights = []
        for d in range(SHIFTS):
            value = jnp.where(odd > 0, cols_ref[k, max(d - 1, 0)], cols_ref[k, min(d, TAPS - 1)])
            weights.append(jnp.where(odd > 0, 0.0, value) if d == 0 else value)
        weights[TAPS] = jnp.where(odd > 0, weights[TAPS], 0.0)
        return weights

    def row_of_halo(n):
        return jnp.where(n % 8 < 4, low_rows + n % 2, n % 2 - 2)

    lane = iota((16, DEPTH), 1)
    row = iota((16, DEPTH), 0)
    model_row = lane % SLOT - ROWS
    is_low = lane >= 2 * SLOT
    blank = lane >= 3 * SLOT
    far = 4 * height

    def low_part(value):
        return jnp.where(is_low, value - value.astype(bf16).astype(f32), value).astype(bf16)

    slot = lane % SLOT
    source_row = jnp.where(slot < 2 * low_rows, slot % low_rows, row_of_halo(slot))
    source_row = jnp.where((slot >= 2 * low_rows + 8) | blank, far, source_row)
    second_visit = jnp.where(slot < 2 * low_rows, slot // low_rows, slot % 4 // 2) > 0
    base_main = jnp.where(blank, -far, model_row + TAPS // 2 - 2 * row)
    halo_row = jnp.where(row < 8, row_of_halo(row), far)
    base_halo = jnp.where(blank, -far, model_row + TAPS // 2 - 2 * halo_row)
    base_back = row + TAPS // 2 - 2 * source_row

    def build(c, carry):
        k0, k1 = PAIR * c, PAIR * c + 1
        shift0, shift1 = dither_ref[0, k0], dither_ref[0, k1]
        taps0 = [rows_ref[k0, a] for a in range(TAPS)]
        taps1 = [rows_ref[k1, a] for a in range(TAPS)]
        for j, (shift, taps) in enumerate(((shift0, taps0), (shift1, taps1))):
            for u in range(low_rows // 16):
                begin = low_rows * j + 16 * u
                ahead_ref[c, begin : begin + 16, :] = low_part(pick(base_main - (32 * u + shift), taps))
        upper = row % 4 < 2
        ahead_ref[c, 2 * low_rows : SLOT, :] = low_part(
            pick(
                base_halo - jnp.where(upper, shift0, shift1),
                [jnp.where(upper, a, b) for a, b in zip(taps0, taps1)],
            )
        )
        taps = [jnp.where(second_visit, b, a) for a, b in zip(taps0, taps1)]
        weights = [
            jnp.where(second_visit, b * share, a * share) for a, b in zip(col_weights(k0), col_weights(k1))
        ]
        base = base_back - jnp.where(second_visit, shift1, shift0)
        for u in range(height // 16):
            value = pick(base + 16 * u, taps)
            for d in range(SHIFTS):
                begin = height * d + 16 * u
                back_ref[c, begin : begin + 16, :] = low_part(value * weights[d])
        return carry

    lax.fori_loop(0, visit_count, build, 0)

    own_model.wait()

    @pl.when(has_down)
    def _():
        rim_copy(0).wait_recv()

    @pl.when(has_up)
    def _():
        rim_copy(1).wait_recv()

    groups = (height + 2 * ROWS) // 8
    for side in range(2):
        packed = jnp.zeros((8, LANES), f32)
        begin = (width - LANES) * side
        for t in range(groups):
            piece = turn(grid_ref[8 * t : 8 * (t + 1), begin : begin + LANES], 8 * t + 8 * side, 1)
            packed = jnp.where((lane8 >= 8 * t) & (lane8 < 8 * t + 8), piece, packed)
        side_out[side] = packed

    @pl.when(has_left)
    def _():
        side_copy(0).start()

    for way, _, ok in ways:

        @pl.when(ok)
        def _():
            row_copy(way).wait_recv()

    for p in range(visit_count):
        aux_out[p, 0:16, :] = row_in[0, p, 0:16, :]
        aux_out[p, 16:32, :] = row_in[1, p, 0:16, :]
        down, up = [row_in[way, p, 16:32, :].astype(f32)[0:8] for way in range(2)]
        packed = aux_out[p, 32:48, :].astype(f32)[8:16]
        aux_out[p, 32:48, :] = jnp.concatenate([jnp.where(sub8 < 4, down, up), packed], axis=0).astype(bf16)
    aux_in[visit] = aux_out[visit]

    def send_low(q, carry):
        aux_copy(q, visit).start()
        return carry

    lax.fori_loop(0, visit, send_low, 0)

    def send_main(q, carry):
        frame_copy(q, visit).start()
        return carry

    lax.fori_loop((visit > 1).astype(jnp.int32), visit, send_main, 0)

    def send_high(q, carry):
        pl.semaphore_wait(here_visit.at[q], 1)

        @pl.when(q == visit + 1)
        def _():
            side_copy(1).start()

        aux_copy(q, visit).start()
        frame_copy(q, visit).start()
        return carry

    at_once = has_left | (has_up & has_down)
    following = jnp.where(at_once, visit_count, jnp.minimum(visit + 2, visit_count))
    lax.fori_loop(visit + 1, following, send_high, 0)

    model_stack[3 * SLOT : DEPTH, :] = jnp.zeros((DEPTH - 3 * SLOT, full_cols), bf16)
    stack_ref[3 * SLOT : DEPTH, :] = jnp.zeros((DEPTH - 3 * SLOT, half_cols), bf16)

    spread = selection(
        (2 * LANES, 2 * LANES),
        lambda a, b: a == jnp.where(b < LANES, 2 * b, 2 * b - (2 * LANES - 1)),
    )
    operator = ahead_ref[...].reshape(visit_count * SLOT, DEPTH)

    def rows_ahead(some):
        parts = [halves(grid_ref[:, 2 * LANES * n : 2 * LANES * (n + 1)]) for n in some]
        apart = dot(jnp.concatenate([part for pair in parts for part in pair], axis=0), spread).astype(bf16)
        for m, n in enumerate(some):
            cols = slice(2 * LANES * n, 2 * LANES * (n + 1))
            high = apart[2 * SLOT * m : 2 * SLOT * m + SLOT]
            model_stack[0:SLOT, cols] = high
            model_stack[SLOT : 2 * SLOT, cols] = apart[2 * SLOT * m + SLOT : 2 * SLOT * (m + 1)]
            model_stack[2 * SLOT : 3 * SLOT, cols] = high
            rowed_ref[:, :, cols] = dot(operator, model_stack[:, cols]).reshape(visit_count, SLOT, 2 * LANES)

    rows_ahead(range(blocks - 1))

    first_lane, last_lane = lane8 == 0, lane8 == LANES - 1
    upper8 = sub8 % 4 < 2

    def row_groups(c):
        weights0, weights1 = col_weights(PAIR * c), col_weights(PAIR * c + 1)
        for g in range(2 * low_rows // 8 + 1):
            if g < low_rows // 8:
                weights = weights0
            elif g < 2 * low_rows // 8:
                weights = weights1
            else:
                weights = [jnp.where(upper8, a, b) for a, b in zip(weights0, weights1)]
            yield slice(8 * g, 8 * (g + 1)), weights

    def tap(c, rows, weights, n, step):
        even = rowed_ref[c, rows, 2 * LANES * n : 2 * LANES * n + LANES]
        odd = rowed_ref[c, rows, 2 * LANES * n + LANES : 2 * LANES * (n + 1)]
        value = weights[2 * step + 2] * even + weights[2 * step + 3] * odd
        return turn(value, -step, 1)

    last = blocks - 1

    def predict(c):
        for rows, weights in row_groups(c):
            before, here, after = [[tap(c, rows, weights, n, step) for n in range(last)] for step in (-1, 0, 1)]
            for n in range(last):
                value = here[n] + jnp.where(first_lane, before[n - 1] if n else 0.0, before[n])
                value = value + jnp.where(last_lane, after[n + 1] if n < last - 1 else 0.0, after[n])
                pred_ref[c, rows, LANES * n : LANES * (n + 1)] = value

    def predict_ends(c):
        for rows, weights in row_groups(c):
            before, here, after = [tap(c, rows, weights, last, step) for step in (-1, 0, 1)]
            value = here + jnp.where(first_lane, tap(c, rows, weights, last - 1, -1), before)
            value = value + jnp.where(last_lane, tap(c, rows, weights, 0, 1), after)
            pred_ref[c, rows, LANES * last : LANES * blocks] = value
            pred_ref[c, rows, 0:LANES] += jnp.where(first_lane, before, 0.0)
            pred_ref[c, rows, LANES * (last - 1) : LANES * last] += jnp.where(last_lane, after, 0.0)

    def by_four(body):
        def four(n, carry):
            for c in range(4):
                body(4 * n + c)
            return carry

        return four

    fours = visit_count // 4
    early = jnp.where(at_once, 0, fours)
    lax.fori_loop(0, early, by_four(predict), 0)
    lax.fori_loop(following, visit_count, send_high, 0)
    lax.fori_loop(early, fours, by_four(predict), 0)

    for side, ok in ((0, has_right), (1, has_left)):
        begin = width + LANES * side

        @pl.when(ok)
        def _():
            side_copy(side).wait_recv()
            packed = side_in[side]
            keep = lane8 >= LANES - 8 if side else lane8 < 8
            for t in range(groups):
                piece = turn(packed, -8 * t - 8 * side, 1)
                grid_ref[8 * t : 8 * (t + 1), begin : begin + LANES] = jnp.where(keep, piece, 0.0)

        @pl.when(jnp.logical_not(ok))
        def _():
            grid_ref[:, begin : begin + LANES] = jnp.zeros((height + 2 * ROWS, LANES), f32)

    rows_ahead([last])
    lax.fori_loop(0, fours, by_four(predict_ends), 0)

    own_block.wait()
    row16 = iota((16, LANES), 0)
    lane16 = iota((16, LANES), 1)
    halo_index = row_of_halo(iota((16, LANES), 0)) + sky * low_rows
    upper16 = row16 % 4 < 2
    columns = [lane16 + LANES * n for n in range(blocks - 1)]
    columns.append(jnp.where(lane16 < LANES // 2, lane16 + low_cols, lane16 - LANES))
    columns = [value + visit * low_cols for value in columns]
    all_cols = low_cols * visit_count

    order = [sorted(range(visit_count), key=lambda q: (abs(q - v), q)) for v in range(visit_count)]

    def owner_of(o):
        owner = jnp.int32(0)
        for v in range(visit_count):
            for n in range(visit_count):
                if order[v][n]:
                    owner = jnp.where((visit == v) & (o == n), order[v][n], owner)
        return owner

    def shifted(values, shift):
        turned = [pltpu.roll(value, jnp.where(shift < 0, LANES - 1, shift), 1) for value in values]
        to_right, to_left = (lane16 == 0) & (shift > 0), (lane16 == LANES - 1) & (shift < 0)
        return [
            jnp.where(to_right, turned[n - 1], jnp.where(to_left, turned[(n + 1) % blocks], turned[n]))
            for n in range(blocks)
        ]

    def limits(limit, shift):
        result = []
        for n in range(blocks):
            if 0 < n < blocks - 2:
                result.append(limit)
            else:
                result.append(jnp.where((columns[n] >= shift) & (columns[n] < all_cols + shift), limit, 0.0))
        return result

    def put(begin, predicted, values, limit):
        for n in range(blocks):
            cols = slice(LANES * n, LANES * (n + 1))
            error = predicted[n] - values[n]
            high, low = halves(jnp.minimum(jnp.maximum(error, -limit[n]), limit[n]))
            stack_ref[begin : begin + 16, cols] = high
            stack_ref[SLOT + begin : SLOT + begin + 16, cols] = low
            stack_ref[2 * SLOT + begin : 2 * SLOT + begin + 16, cols] = high

    def arrived(c):
        frame_copy(c, c).wait_recv()
        aux_copy(c, c).wait_recv()

    def work(c, is_first):
        rest = aux_in[c, 32:48, :].astype(f32)
        packed = rest[8:16]
        shifts = [col_shift(PAIR * c + j) for j in range(PAIR)]
        for j in range(PAIR):
            k = PAIR * c + j
            cut, first, last = cut_ref[k], footprint_ref[0, k], footprint_ref[1, k]
            for u in range(low_rows // 16):
                begin = low_rows * j + 16 * u
                start = sky * low_rows + 16 * u
                rows = slice(16 * u, 16 * (u + 1))
                values = [
                    frame_ref[c, j, rows, LANES * n : LANES * (n + 1)].astype(f32) for n in range(blocks - 1)
                ]
                g = begin // 8
                values.append(jnp.concatenate([turn(packed, -4 * g, 1), turn(packed, -4 * (g + 1), 1)], axis=0))
                limit = jnp.where((row16 >= first - start) & (row16 < last - start), cut, 0.0)
                predicted = [pred_ref[c, begin : begin + 16, LANES * n : LANES * (n + 1)] for n in range(blocks)]
                put(begin, predicted, shifted(values, shifts[j]), limits(limit, shifts[j]))
        k0, k1 = PAIR * c, PAIR * c + 1
        begin = 2 * low_rows
        values = []
        for _ in range(low_blocks // 4):
            down, up = [aux_in[c, 16 * way : 16 * (way + 1), :].astype(f32) for way in range(2)]
            for n in range(2):
                down8, up8 = down[8 * n : 8 * (n + 1)], up[8 * n : 8 * (n + 1)]
                values.append(jnp.where(sub8 < 4, down8, turn(up8, 4, 0)))
                values.append(jnp.where(sub8 < 4, turn(down8, 4, 0), up8))
        values.append(rest[0:8])
        values = [jnp.concatenate([value, blank8], axis=0) for value in values]
        values = [jnp.where(upper16, a, b) for a, b in zip(shifted(values, shifts[0]), shifted(values, shifts[1]))]
        inside = (halo_index >= jnp.where(upper16, footprint_ref[0, k0], footprint_ref[0, k1])) & (
            halo_index < jnp.where(upper16, footprint_ref[1, k0], footprint_ref[1, k1])
        )
        limit = jnp.where(inside & (row16 < 8), jnp.where(upper16, cut_ref[k0], cut_ref[k1]), 0.0)
        predicted = [
            jnp.concatenate([pred_ref[c, begin : begin + 8, LANES * n : LANES * (n + 1)], blank8], axis=0)
            for n in range(blocks)
        ]
        put(begin, predicted, values, limits(limit, jnp.where(upper16, shifts[0], shifts[1])))
        for begin in range(0, half_cols, 2 * LANES):
            cols = slice(begin, min(begin + 2 * LANES, half_cols))
            product = dot(back_ref[c], stack_ref[:, cols])
            total_ref[:, cols] = product if is_first else total_ref[:, cols] + product

    owners = [owner_of(o) for o in range(visit_count)]
    work(owners[0], True)

    def next_col(value):
        return pltpu.roll(value, full_cols - 1, 1)

    strip = 16
    for t in range(height // strip):
        above = grid_ref[ROWS - 1 + strip * t : ROWS - 1 + strip * (t + 1), :]
        here = grid_ref[ROWS + strip * t : ROWS + strip * (t + 1), :]
        below = grid_ref[ROWS + 1 + strip * t : ROWS + 1 + strip * (t + 1), :]
        gx, gy = here - above, next_col(above) - above
        value = gx * lax.rsqrt(gx * gx + gy * gy + eps_flux)
        gx, gy = below - here, next_col(here) - here
        scale = lax.rsqrt(gx * gx + gy * gy + eps_flux)
        flux = gy * scale
        value = value - gx * scale + (pltpu.roll(flux, 1, 1) - flux)
        out_ref[strip * t : strip * (t + 1), :] = tv_weight * value[:, :width]

    for c in owners[1:]:
        arrived(c)
        work(c, False)

    join = selection(
        (4 * LANES, 2 * LANES),
        lambda a, b: b == jnp.where(a % (2 * LANES) < LANES, 2 * (a % LANES), 2 * (a % LANES) + 1),
    )
    for u in range(height // 16):
        parts = []
        for odd in range(2):
            value = None
            for step in range(-1, 2):
                begin = height * (2 * (step + 1) + odd) + 16 * u
                piece = turn(total_ref[begin : begin + 16, :], step, 1)
                value = piece if value is None else value + piece
            parts.append(halves(value[:, :low_cols]))
        for b in range(low_cols // LANES):
            cols = slice(LANES * b, LANES * (b + 1))
            for n, part in enumerate((parts[0][0], parts[1][0], parts[0][1], parts[1][1])):
                inter_ref[height * b + 16 * u : height * b + 16 * (u + 1), LANES * n : LANES * (n + 1)] = part[:, cols]
    joined = dot(inter_ref[...], join)
    for b in range(low_cols // LANES):
        out_ref[:, 2 * LANES * b : 2 * LANES * (b + 1)] += joined[height * b : height * (b + 1)]

    def sent(q, carry):
        @pl.when(q != visit)
        def _():
            frame_copy(q, visit).wait_send()
            aux_copy(q, visit).wait_send()

        return carry

    lax.fori_loop(0, visit_count, sent, 0)
    for side, ok in ((0, has_left), (1, has_right)):

        @pl.when(ok)
        def _():
            side_copy(side).wait_send()

    for way, ok in ((0, has_up), (1, has_down)):

        @pl.when(ok)
        def _():
            rim_copy(way).wait_send()
            row_copy(way).wait_send()


def solution(mesh):
    in_specs = (
        P(("tiles", "sky"), "visit"),
        P(("tiles", "visit"), "sky", None),
        P("tiles", None),
        P("tiles", None),
        P("tiles", None),
        P("tiles", None),
        P("tiles"),
    )
    out_specs = P(("tiles", "sky"), "visit")
    sky_count, visit_count = mesh.shape["sky"], mesh.shape["visit"]

    def on_device(sky_model, frames, psf_rows, psf_cols, dither, footprint, huber_cut):
        height, width = sky_model.shape
        per_device, low_rows, all_cols = frames.shape
        visits = psf_rows.shape[0]
        low_cols = all_cols // visit_count
        half_cols = width // 2 + LANES
        f32, bf16 = jnp.float32, jnp.bfloat16
        arguments = [
            pltpu.with_memory_space_constraint(x, pltpu.HBM)
            for x in (sky_model, frames, psf_rows, psf_cols, dither.T, footprint.T, huber_cut)
        ]
        dma = pltpu.SemaphoreType.DMA
        return pl.pallas_call(
            functools.partial(kernel, (sky_count, visit_count)),
            out_shape=pltpu.VMEM((height, width), f32),
            in_specs=[pl.BlockSpec(memory_space=pltpu.HBM)] * 7,
            out_specs=pl.BlockSpec(memory_space=pltpu.VMEM),
            scratch_shapes=[
                pltpu.SMEM(psf_rows.shape, f32),
                pltpu.SMEM(psf_cols.shape, f32),
                pltpu.SMEM(dither.shape[::-1], jnp.int32),
                pltpu.SMEM(footprint.shape[::-1], jnp.int32),
                pltpu.SMEM(huber_cut.shape, f32),
                pltpu.VMEM((height + 2 * ROWS, width + 2 * LANES), f32),
                pltpu.VMEM(frames.shape, bf16),
                pltpu.VMEM((visit_count, per_device, low_rows, low_cols), bf16),
                pltpu.VMEM((2, visit_count, 32, LANES), bf16),
                pltpu.VMEM((2, visit_count, 32, LANES), bf16),
                pltpu.VMEM((visit_count, 48, LANES), bf16),
                pltpu.VMEM((visit_count, 48, LANES), bf16),
                pltpu.VMEM((2, 8, LANES), f32),
                pltpu.VMEM((2, 8, LANES), f32),
                pltpu.VMEM((DEPTH, 2 * half_cols), bf16),
                pltpu.VMEM((visit_count, SLOT, DEPTH), bf16),
                pltpu.VMEM((visit_count, SLOT, 2 * half_cols), f32),
                pltpu.VMEM((visit_count, SLOT, half_cols), f32),
                pltpu.VMEM((visit_count, SHIFTS * height, DEPTH), bf16),
                pltpu.VMEM((DEPTH, half_cols), bf16),
                pltpu.VMEM((SHIFTS * height, half_cols), f32),
                pltpu.VMEM((low_cols // LANES * height, 4 * LANES), bf16),
                dma((3,)),
                dma((5,)),
                pltpu.SemaphoreType.REGULAR((visit_count,)),
                pltpu.SemaphoreType.REGULAR((2,)),
                dma((visit_count,)),
                dma((visit_count,)),
                dma((2,)),
                dma((2,)),
                dma((visit_count,)),
                dma((visit_count,)),
                dma((2,)),
                dma((2,)),
                dma((2,)),
                dma((2,)),
            ],
            compiler_params=pltpu.CompilerParams(
                collective_id=0, has_side_effects=True, vmem_limit_bytes=48 * 1024 * 1024
            ),
        )(*arguments)

    return jax.shard_map(
        on_device, mesh=mesh, in_specs=in_specs, out_specs=out_specs, check_vma=False
    )
```

```python
import functools

import jax
import jax.numpy as jnp
from jax import lax
from jax.experimental import pallas as pl
from jax.experimental.pallas import tpu as pltpu
from jax.sharding import PartitionSpec as P

TAPS = 5
SHIFTS = TAPS + 1

eps_flux = 0.1
tv_weight = 0.5

ROWS = 8
LANES = 128
PAIR = 2
SLOT = 80
DEPTH = 256
MESH = pl.DeviceIdType.MESH


def dot(a, b):
    return jnp.dot(a, b, preferred_element_type=jnp.float32)


def iota(shape, dim):
    return lax.broadcasted_iota(jnp.int32, shape, dim)


def selection(shape, source_of):
    row, col = iota(shape, 0), iota(shape, 1)
    return jnp.where(source_of(row, col), 1.0, 0.0).astype(jnp.bfloat16)


def halves(value):
    high = value.astype(jnp.bfloat16)
    return high, (value - high.astype(jnp.float32)).astype(jnp.bfloat16)


def turn(value, shift, axis):
    shift %= value.shape[axis]
    return pltpu.roll(value, shift, axis) if shift else value


def pick(at, taps):
    value = jnp.zeros(at.shape, jnp.float32)
    for a, tap in enumerate(taps):
        value = jnp.where(at == a, tap, value)
    return value


def kernel(
    counts,
    model_ref,
    frames_ref,
    rows_in,
    cols_in,
    dither_in,
    footprint_in,
    cut_in,
    out_ref,
    total_ref,
    rows_ref,
    cols_ref,
    dither_ref,
    footprint_ref,
    cut_ref,
    grid_ref,
    own_ref,
    frame_ref,
    row_out,
    row_in,
    aux_out,
    aux_in,
    side_out,
    side_in,
    model_stack,
    ahead_ref,
    rowed_ref,
    pred_ref,
    back_ref,
    stack_ref,
    local_sem,
    small_sem,
    here_visit,
    here_sky,
    frame_send,
    frame_recv,
    row_send,
    row_recv,
    aux_send,
    aux_recv,
    side_send,
    side_recv,
    rim_send,
    rim_recv,
):
    sky_count, visit_count = counts
    height, width = out_ref.shape
    low_rows, low_cols = frame_ref.shape[2:]
    full_cols = grid_ref.shape[1]
    half_cols = full_cols // 2
    blocks = full_cols // (2 * LANES)
    visits = rows_ref.shape[0]
    tile = lax.axis_index("tiles")
    sky = lax.axis_index("sky")
    visit = lax.axis_index("visit")
    has_up, has_down = sky > 0, sky < sky_count - 1
    has_left, has_right = visit > 0, visit < visit_count - 1
    f32, bf16 = jnp.float32, jnp.bfloat16

    def remote(source, target, send, recv, device):
        return pltpu.make_async_remote_copy(
            src_ref=source, dst_ref=target, send_sem=send, recv_sem=recv, device_id=device, device_id_type=MESH
        )

    def at_visit(q):
        return (tile, sky, q)

    def at_sky(step):
        return (tile, sky + step, visit)

    ways = ((0, has_up, has_down), (1, has_down, has_up))

    def columns_of(q):
        return pl.ds(pl.multiple_of(q * low_cols, low_cols), low_cols)

    def frame_copy(peer, owner):
        return remote(
            frames_ref.at[:, :, columns_of(peer)],
            frame_ref.at[owner],
            frame_send.at[peer],
            frame_recv.at[owner],
            at_visit(peer),
        )

    def aux_copy(peer, owner):
        return remote(aux_out.at[peer], aux_in.at[owner], aux_send.at[peer], aux_recv.at[owner], at_visit(peer))

    def row_copy(way):
        return remote(row_out.at[way], row_in.at[way], row_send.at[way], row_recv.at[way], at_sky(2 * way - 1))

    def side_copy(side):
        return remote(
            side_out.at[side], side_in.at[side], side_send.at[side], side_recv.at[side], at_visit(visit + 2 * side - 1)
        )

    def rim_copy(way):
        source = model_ref.at[pl.ds((height - ROWS) * way, ROWS), :]
        target = grid_ref.at[pl.ds((ROWS + height) * (1 - way), ROWS), pl.ds(0, width)]
        return remote(source, target, rim_send.at[way], rim_recv.at[way], at_sky(2 * way - 1))

    own_frames = pltpu.make_async_copy(frames_ref, own_ref, local_sem.at[1])
    small = [
        pltpu.make_async_copy(source, target, small_sem.at[n])
        for n, (source, target) in enumerate(
            (
                (rows_in, rows_ref),
                (cols_in, cols_ref),
                (dither_in, dither_ref),
                (footprint_in, footprint_ref),
                (cut_in, cut_ref),
            )
        )
    ]
    own_model = pltpu.make_async_copy(
        model_ref, grid_ref.at[pl.ds(ROWS, height), pl.ds(0, width)], local_sem.at[0]
    )
    own_block = pltpu.make_async_copy(frames_ref.at[:, :, columns_of(visit)], frame_ref.at[visit], local_sem.at[2])
    own_frames.start()
    own_model.start()
    for copy in small:
        copy.start()
    barrier = pltpu.get_barrier_semaphore()
    is_odd = sky % 2 > 0

    def greet(q, carry):
        pl.semaphore_signal(barrier, inc=1, device_id=at_visit(q), device_id_type=MESH)
        return carry

    lax.fori_loop(visit + 1, visit_count, greet, 0)
    for way, ok, _ in ways:

        @pl.when(ok & is_odd)
        def _():
            pl.semaphore_signal(barrier, inc=1, device_id=at_sky(2 * way - 1), device_id_type=MESH)

    beside = has_up.astype(jnp.int32) + has_down.astype(jnp.int32)
    smaller = visit + jnp.where(is_odd, 0, beside)

    @pl.when(smaller > 0)
    def _():
        pl.semaphore_wait(barrier, smaller)

    def answer(q, carry):
        pl.semaphore_signal(here_visit.at[visit], inc=1, device_id=at_visit(q), device_id_type=MESH)
        return carry

    lax.fori_loop(0, visit, answer, 0)

    for way, ok, _ in ways:

        @pl.when(ok & jnp.logical_not(is_odd))
        def _():
            pl.semaphore_signal(here_sky.at[1 - way], inc=1, device_id=at_sky(2 * way - 1), device_id_type=MESH)

    @pl.when(visit > 1)
    def _():
        frame_copy(0, visit).start()

    for way, ok, _ in ways:

        @pl.when(ok & jnp.logical_not(is_odd))
        def _():
            rim_copy(way).start()

    own_block.start()

    @pl.when(jnp.logical_not(has_up))
    def _():
        grid_ref[0:ROWS, 0:width] = jnp.zeros((ROWS, width), f32)
        row_in[1] = jnp.zeros(row_in.shape[1:], bf16)

    @pl.when(jnp.logical_not(has_down))
    def _():
        grid_ref[ROWS + height :, 0:width] = jnp.zeros((ROWS, width), f32)
        row_in[0] = jnp.zeros(row_in.shape[1:], bf16)

    own_frames.wait()
    sub8 = iota((8, LANES), 0)
    lane8 = iota((8, LANES), 1)
    blank8 = jnp.zeros((8, LANES), f32)
    low_blocks = low_cols // LANES
    for way in range(2):
        piled, moved = [], []
        for n in range(low_blocks * visit_count):
            cols = slice(LANES * n, LANES * (n + 1))
            if way == 0:
                first = own_ref[0, 0:16, cols].astype(f32)[0:8]
                second = turn(own_ref[1, 0:16, cols].astype(f32)[0:8], 2, 0)
            else:
                first = turn(own_ref[0, low_rows - 16 : low_rows, cols].astype(f32)[8:16], 2, 0)
                second = turn(own_ref[1, low_rows - 16 : low_rows, cols].astype(f32)[8:16], 4, 0)
            piled.append(jnp.where(sub8 < 2, first, second))
            moved.append(turn(piled[-1], 4, 0))
        for p in range(visit_count):
            n = low_blocks * p
            for b in range(low_blocks // 4):
                tiles = [jnp.where(sub8 < 4, piled[m], moved[m + 1]) for m in (n + 4 * b, n + 4 * b + 2)]
                row_out[way, p, 16 * b : 16 * (b + 1), :] = jnp.concatenate(tiles, axis=0).astype(bf16)
            ends = moved if way else piled
            corner = jnp.where(lane8 < LANES // 2, ends[(n + low_blocks) % len(ends)], ends[n - 1])
            row_out[way, p, 16:32, :] = jnp.concatenate([corner, blank8], axis=0).astype(bf16)
    for p in range(visit_count):
        right = low_cols * (p + 1) if p < visit_count - 1 else 0
        left = low_cols * p - LANES if p > 0 else 0
        packed = blank8
        for j in range(PAIR):
            for u in range(low_rows // 16):
                after = own_ref[j, 16 * u : 16 * (u + 1), right : right + LANES].astype(f32)
                before = own_ref[j, 16 * u : 16 * (u + 1), left : left + LANES].astype(f32)
                for n in range(2):
                    g = (low_rows * j + 16 * u) // 8 + n
                    piece = jnp.where(lane8 < LANES // 2, after[8 * n : 8 * (n + 1)], before[8 * n : 8 * (n + 1)])
                    packed = jnp.where((lane8 - 4 * g + 2 + LANES) % LANES < 4, turn(piece, 4 * g, 1), packed)
        aux_out[p, 32:48, :] = jnp.concatenate([blank8, packed], axis=0).astype(bf16)

    for way, ok, _ in ways:

        @pl.when(ok & jnp.logical_not(is_odd))
        def _():
            row_copy(way).start()

    for way, ok, _ in ways:

        @pl.when(ok & is_odd)
        def _():
            pl.semaphore_wait(here_sky.at[way], 1)
            row_copy(way).start()
            rim_copy(way).start()

    for copy in small:
        copy.wait()
    share = 1.0 / float(visits) ** 0.5

    def col_shift(k):
        return (dither_ref[1, k] + 4) // 2 - 2

    def col_weights(k):
        odd = dither_ref[1, k] - 2 * col_shift(k)
        weights = []
        for d in range(SHIFTS):
            value = jnp.where(odd > 0, cols_ref[k, max(d - 1, 0)], cols_ref[k, min(d, TAPS - 1)])
            weights.append(jnp.where(odd > 0, 0.0, value) if d == 0 else value)
        weights[TAPS] = jnp.where(odd > 0, weights[TAPS], 0.0)
        return weights

    def row_of_halo(n):
        return jnp.where(n % 8 < 4, low_rows + n % 2, n % 2 - 2)

    lane = iota((16, DEPTH), 1)
    row = iota((16, DEPTH), 0)
    model_row = lane % SLOT - ROWS
    is_low = lane >= 2 * SLOT
    blank = lane >= 3 * SLOT
    far = 4 * height

    def low_part(value):
        return jnp.where(is_low, value - value.astype(bf16).astype(f32), value).astype(bf16)

    slot = lane % SLOT
    source_row = jnp.where(slot < 2 * low_rows, slot % low_rows, row_of_halo(slot))
    source_row = jnp.where((slot >= 2 * low_rows + 8) | blank, far, source_row)
    second_visit = jnp.where(slot < 2 * low_rows, slot // low_rows, slot % 4 // 2) > 0
    base_main = jnp.where(blank, -far, model_row + TAPS // 2 - 2 * row)
    halo_row = jnp.where(row < 8, row_of_halo(row), far)
    base_halo = jnp.where(blank, -far, model_row + TAPS // 2 - 2 * halo_row)
    base_back = row + TAPS // 2 - 2 * source_row

    def build(c, carry):
        k0, k1 = PAIR * c, PAIR * c + 1
        shift0, shift1 = dither_ref[0, k0], dither_ref[0, k1]
        taps0 = [rows_ref[k0, a] for a in range(TAPS)]
        taps1 = [rows_ref[k1, a] for a in range(TAPS)]
        for j, (shift, taps) in enumerate(((shift0, taps0), (shift1, taps1))):
            for u in range(low_rows // 16):
                begin = low_rows * j + 16 * u
                ahead_ref[c, begin : begin + 16, :] = low_part(pick(base_main - (32 * u + shift), taps))
        upper = row % 4 < 2
        ahead_ref[c, 2 * low_rows : SLOT, :] = low_part(
            pick(
                base_halo - jnp.where(upper, shift0, shift1),
                [jnp.where(upper, a, b) for a, b in zip(taps0, taps1)],
            )
        )
        taps = [jnp.where(second_visit, b, a) for a, b in zip(taps0, taps1)]
        weights = [
            jnp.where(second_visit, b * share, a * share) for a, b in zip(col_weights(k0), col_weights(k1))
        ]
        base = base_back - jnp.where(second_visit, shift1, shift0)
        for u in range(height // 16):
            value = pick(base + 16 * u, taps)
            for d in range(SHIFTS):
                begin = height * d + 16 * u
                back_ref[c, begin : begin + 16, :] = low_part(value * weights[d])
        return carry

    lax.fori_loop(0, visit_count, build, 0)

    own_model.wait()

    @pl.when(has_down)
    def _():
        rim_copy(0).wait_recv()

    @pl.when(has_up)
    def _():
        rim_copy(1).wait_recv()

    groups = (height + 2 * ROWS) // 8
    for side in range(2):
        packed = jnp.zeros((8, LANES), f32)
        begin = (width - LANES) * side
        for t in range(groups):
            piece = turn(grid_ref[8 * t : 8 * (t + 1), begin : begin + LANES], 8 * t + 8 * side, 1)
            packed = jnp.where((lane8 >= 8 * t) & (lane8 < 8 * t + 8), piece, packed)
        side_out[side] = packed

    @pl.when(has_left)
    def _():
        side_copy(0).start()

    for way, _, ok in ways:

        @pl.when(ok)
        def _():
            row_copy(way).wait_recv()

    for p in range(visit_count):
        aux_out[p, 0:16, :] = row_in[0, p, 0:16, :]
        aux_out[p, 16:32, :] = row_in[1, p, 0:16, :]
        down, up = [row_in[way, p, 16:32, :].astype(f32)[0:8] for way in range(2)]
        packed = aux_out[p, 32:48, :].astype(f32)[8:16]
        aux_out[p, 32:48, :] = jnp.concatenate([jnp.where(sub8 < 4, down, up), packed], axis=0).astype(bf16)
    aux_in[visit] = aux_out[visit]

    def send_low(q, carry):
        aux_copy(q, visit).start()
        return carry

    lax.fori_loop(0, visit, send_low, 0)

    def send_main(q, carry):
        frame_copy(q, visit).start()
        return carry

    lax.fori_loop((visit > 1).astype(jnp.int32), visit, send_main, 0)

    def send_high(q, carry):
        pl.semaphore_wait(here_visit.at[q], 1)

        @pl.when(q == visit + 1)
        def _():
            side_copy(1).start()

        aux_copy(q, visit).start()
        frame_copy(q, visit).start()
        return carry

    at_once = has_left | (has_up & has_down)
    following = jnp.where(at_once, visit_count, jnp.minimum(visit + 2, visit_count))
    lax.fori_loop(visit + 1, following, send_high, 0)

    model_stack[3 * SLOT : DEPTH, :] = jnp.zeros((DEPTH - 3 * SLOT, full_cols), bf16)
    stack_ref[3 * SLOT : DEPTH, :] = jnp.zeros((DEPTH - 3 * SLOT, half_cols), bf16)

    spread = selection(
        (2 * LANES, 2 * LANES),
        lambda a, b: a == jnp.where(b < LANES, 2 * b, 2 * b - (2 * LANES - 1)),
    )
    operator = ahead_ref[...].reshape(visit_count * SLOT, DEPTH)

    def rows_ahead(some):
        parts = [halves(grid_ref[:, 2 * LANES * n : 2 * LANES * (n + 1)]) for n in some]
        apart = dot(jnp.concatenate([part for pair in parts for part in pair], axis=0), spread).astype(bf16)
        for m, n in enumerate(some):
            cols = slice(2 * LANES * n, 2 * LANES * (n + 1))
            high = apart[2 * SLOT * m : 2 * SLOT * m + SLOT]
            model_stack[0:SLOT, cols] = high
            model_stack[SLOT : 2 * SLOT, cols] = apart[2 * SLOT * m + SLOT : 2 * SLOT * (m + 1)]
            model_stack[2 * SLOT : 3 * SLOT, cols] = high
            rowed_ref[:, :, cols] = dot(operator, model_stack[:, cols]).reshape(visit_count, SLOT, 2 * LANES)

    rows_ahead(range(blocks - 1))

    first_lane, last_lane = lane8 == 0, lane8 == LANES - 1
    upper8 = sub8 % 4 < 2

    def row_groups(c):
        weights0, weights1 = col_weights(PAIR * c), col_weights(PAIR * c + 1)
        for g in range(2 * low_rows // 8 + 1):
            if g < low_rows // 8:
                weights = weights0
            elif g < 2 * low_rows // 8:
                weights = weights1
            else:
                weights = [jnp.where(upper8, a, b) for a, b in zip(weights0, weights1)]
            yield slice(8 * g, 8 * (g + 1)), weights

    def tap(c, rows, weights, n, step):
        even = rowed_ref[c, rows, 2 * LANES * n : 2 * LANES * n + LANES]
        odd = rowed_ref[c, rows, 2 * LANES * n + LANES : 2 * LANES * (n + 1)]
        value = weights[2 * step + 2] * even + weights[2 * step + 3] * odd
        return turn(value, -step, 1)

    last = blocks - 1

    def predict(c):
        for rows, weights in row_groups(c):
            before, here, after = [[tap(c, rows, weights, n, step) for n in range(last)] for step in (-1, 0, 1)]
            for n in range(last):
                value = here[n] + jnp.where(first_lane, before[n - 1] if n else 0.0, before[n])
                value = value + jnp.where(last_lane, after[n + 1] if n < last - 1 else 0.0, after[n])
                pred_ref[c, rows, LANES * n : LANES * (n + 1)] = value

    def predict_ends(c):
        for rows, weights in row_groups(c):
            before, here, after = [tap(c, rows, weights, last, step) for step in (-1, 0, 1)]
            value = here + jnp.where(first_lane, tap(c, rows, weights, last - 1, -1), before)
            value = value + jnp.where(last_lane, tap(c, rows, weights, 0, 1), after)
            pred_ref[c, rows, LANES * last : LANES * blocks] = value
            pred_ref[c, rows, 0:LANES] += jnp.where(first_lane, before, 0.0)
            pred_ref[c, rows, LANES * (last - 1) : LANES * last] += jnp.where(last_lane, after, 0.0)

    def by_four(body):
        def four(n, carry):
            for c in range(4):
                body(4 * n + c)
            return carry

        return four

    fours = visit_count // 4
    early = jnp.where(at_once, 0, fours)
    lax.fori_loop(0, early, by_four(predict), 0)
    lax.fori_loop(following, visit_count, send_high, 0)
    lax.fori_loop(early, fours, by_four(predict), 0)

    for side, ok in ((0, has_right), (1, has_left)):
        begin = width + LANES * side

        @pl.when(ok)
        def _():
            side_copy(side).wait_recv()
            packed = side_in[side]
            keep = lane8 >= LANES - 8 if side else lane8 < 8
            for t in range(groups):
                piece = turn(packed, -8 * t - 8 * side, 1)
                grid_ref[8 * t : 8 * (t + 1), begin : begin + LANES] = jnp.where(keep, piece, 0.0)

        @pl.when(jnp.logical_not(ok))
        def _():
            grid_ref[:, begin : begin + LANES] = jnp.zeros((height + 2 * ROWS, LANES), f32)

    rows_ahead([last])
    lax.fori_loop(0, fours, by_four(predict_ends), 0)

    own_block.wait()
    row16 = iota((16, LANES), 0)
    lane16 = iota((16, LANES), 1)
    halo_index = row_of_halo(iota((16, LANES), 0)) + sky * low_rows
    upper16 = row16 % 4 < 2
    columns = [lane16 + LANES * n for n in range(blocks - 1)]
    columns.append(jnp.where(lane16 < LANES // 2, lane16 + low_cols, lane16 - LANES))
    columns = [value + visit * low_cols for value in columns]
    all_cols = low_cols * visit_count

    order = [sorted(range(visit_count), key=lambda q: (abs(q - v), q)) for v in range(visit_count)]

    def owner_of(o):
        owner = jnp.int32(0)
        for v in range(visit_count):
            for n in range(visit_count):
                if order[v][n]:
                    owner = jnp.where((visit == v) & (o == n), order[v][n], owner)
        return owner

    def shifted(values, shift):
        turned = [pltpu.roll(value, jnp.where(shift < 0, LANES - 1, shift), 1) for value in values]
        to_right, to_left = (lane16 == 0) & (shift > 0), (lane16 == LANES - 1) & (shift < 0)
        return [
            jnp.where(to_right, turned[n - 1], jnp.where(to_left, turned[(n + 1) % blocks], turned[n]))
            for n in range(blocks)
        ]

    def limits(limit, shift):
        result = []
        for n in range(blocks):
            if 0 < n < blocks - 2:
                result.append(limit)
            else:
                result.append(jnp.where((columns[n] >= shift) & (columns[n] < all_cols + shift), limit, 0.0))
        return result

    def put(begin, predicted, values, limit):
        for n in range(blocks):
            cols = slice(LANES * n, LANES * (n + 1))
            error = predicted[n] - values[n]
            high, low = halves(jnp.minimum(jnp.maximum(error, -limit[n]), limit[n]))
            stack_ref[begin : begin + 16, cols] = high
            stack_ref[SLOT + begin : SLOT + begin + 16, cols] = low
            stack_ref[2 * SLOT + begin : 2 * SLOT + begin + 16, cols] = high

    def arrived(c):
        frame_copy(c, c).wait_recv()
        aux_copy(c, c).wait_recv()

    def work(c, is_first):
        rest = aux_in[c, 32:48, :].astype(f32)
        packed = rest[8:16]
        shifts = [col_shift(PAIR * c + j) for j in range(PAIR)]
        for j in range(PAIR):
            k = PAIR * c + j
            cut, first, last = cut_ref[k], footprint_ref[0, k], footprint_ref[1, k]
            for u in range(low_rows // 16):
                begin = low_rows * j + 16 * u
                start = sky * low_rows + 16 * u
                rows = slice(16 * u, 16 * (u + 1))
                values = [
                    frame_ref[c, j, rows, LANES * n : LANES * (n + 1)].astype(f32) for n in range(blocks - 1)
                ]
                g = begin // 8
                values.append(jnp.concatenate([turn(packed, -4 * g, 1), turn(packed, -4 * (g + 1), 1)], axis=0))
                limit = jnp.where((row16 >= first - start) & (row16 < last - start), cut, 0.0)
                predicted = [pred_ref[c, begin : begin + 16, LANES * n : LANES * (n + 1)] for n in range(blocks)]
                put(begin, predicted, shifted(values, shifts[j]), limits(limit, shifts[j]))
        k0, k1 = PAIR * c, PAIR * c + 1
        begin = 2 * low_rows
        values = []
        for _ in range(low_blocks // 4):
            down, up = [aux_in[c, 16 * way : 16 * (way + 1), :].astype(f32) for way in range(2)]
            for n in range(2):
                down8, up8 = down[8 * n : 8 * (n + 1)], up[8 * n : 8 * (n + 1)]
                values.append(jnp.where(sub8 < 4, down8, turn(up8, 4, 0)))
                values.append(jnp.where(sub8 < 4, turn(down8, 4, 0), up8))
        values.append(rest[0:8])
        values = [jnp.concatenate([value, blank8], axis=0) for value in values]
        values = [jnp.where(upper16, a, b) for a, b in zip(shifted(values, shifts[0]), shifted(values, shifts[1]))]
        inside = (halo_index >= jnp.where(upper16, footprint_ref[0, k0], footprint_ref[0, k1])) & (
            halo_index < jnp.where(upper16, footprint_ref[1, k0], footprint_ref[1, k1])
        )
        limit = jnp.where(inside & (row16 < 8), jnp.where(upper16, cut_ref[k0], cut_ref[k1]), 0.0)
        predicted = [
            jnp.concatenate([pred_ref[c, begin : begin + 8, LANES * n : LANES * (n + 1)], blank8], axis=0)
            for n in range(blocks)
        ]
        put(begin, predicted, values, limits(limit, jnp.where(upper16, shifts[0], shifts[1])))
        for begin in range(0, half_cols, 2 * LANES):
            cols = slice(begin, min(begin + 2 * LANES, half_cols))
            product = dot(back_ref[c], stack_ref[:, cols])
            total_ref[:, cols] = product if is_first else total_ref[:, cols] + product

    owners = [owner_of(o) for o in range(visit_count)]
    work(owners[0], True)

    def next_col(value):
        return pltpu.roll(value, full_cols - 1, 1)

    strip = 16
    for t in range(height // strip):
        above = grid_ref[ROWS - 1 + strip * t : ROWS - 1 + strip * (t + 1), :]
        here = grid_ref[ROWS + strip * t : ROWS + strip * (t + 1), :]
        below = grid_ref[ROWS + 1 + strip * t : ROWS + 1 + strip * (t + 1), :]
        gx, gy = here - above, next_col(above) - above
        value = gx * lax.rsqrt(gx * gx + gy * gy + eps_flux)
        gx, gy = below - here, next_col(here) - here
        scale = lax.rsqrt(gx * gx + gy * gy + eps_flux)
        flux = gy * scale
        value = value - gx * scale + (pltpu.roll(flux, 1, 1) - flux)
        out_ref[strip * t : strip * (t + 1), :] = tv_weight * value[:, :width]

    for c in owners[1:]:
        arrived(c)
        work(c, False)

    def sent(q, carry):
        @pl.when(q != visit)
        def _():
            frame_copy(q, visit).wait_send()
            aux_copy(q, visit).wait_send()

        return carry

    lax.fori_loop(0, visit_count, sent, 0)
    for side, ok in ((0, has_left), (1, has_right)):

        @pl.when(ok)
        def _():
            side_copy(side).wait_send()

    for way, ok in ((0, has_up), (1, has_down)):

        @pl.when(ok)
        def _():
            rim_copy(way).wait_send()
            row_copy(way).wait_send()


def finish(total_ref, smooth_ref, out_ref, whole_ref, sem):
    height, width = whole_ref.shape
    low_cols = width // 2
    join = selection(
        (4 * LANES, 2 * LANES),
        lambda a, b: b == jnp.where(a % (2 * LANES) < LANES, 2 * (a % LANES), 2 * (a % LANES) + 1),
    )
    strip = 32
    copies = []
    for u in range(height // strip):
        parts = []
        for odd in range(2):
            value = None
            for step in range(-1, 2):
                begin = height * (2 * (step + 1) + odd) + strip * u
                piece = turn(total_ref[begin : begin + strip, :], step, 1)
                value = piece if value is None else value + piece
            parts.append(halves(value[:, :low_cols]))
        pieces = []
        for b in range(low_cols // LANES):
            cols = slice(LANES * b, LANES * (b + 1))
            four = [part[:, cols] for part in (parts[0][0], parts[1][0], parts[0][1], parts[1][1])]
            pieces.append(jnp.concatenate(four, axis=1))
        joined = dot(jnp.concatenate(pieces, axis=0), join)
        rows = slice(strip * u, strip * (u + 1))
        for b in range(low_cols // LANES):
            cols = slice(2 * LANES * b, 2 * LANES * (b + 1))
            whole_ref[rows, cols] = smooth_ref[rows, cols] + joined[strip * b : strip * (b + 1)]
        span = pl.ds(strip * u, strip)
        copies.append(pltpu.make_async_copy(whole_ref.at[span], out_ref.at[span], sem.at[u]))
        copies[-1].start()
    for copy in copies:
        copy.wait()


def solution(mesh):
    in_specs = (
        P(("tiles", "sky"), "visit"),
        P(("tiles", "visit"), "sky", None),
        P("tiles", None),
        P("tiles", None),
        P("tiles", None),
        P("tiles", None),
        P("tiles"),
    )
    out_specs = P(("tiles", "sky"), "visit")
    sky_count, visit_count = mesh.shape["sky"], mesh.shape["visit"]

    def on_device(sky_model, frames, psf_rows, psf_cols, dither, footprint, huber_cut):
        height, width = sky_model.shape
        per_device, low_rows, all_cols = frames.shape
        visits = psf_rows.shape[0]
        low_cols = all_cols // visit_count
        half_cols = width // 2 + LANES
        f32, bf16 = jnp.float32, jnp.bfloat16
        arguments = [
            pltpu.with_memory_space_constraint(x, pltpu.HBM)
            for x in (sky_model, frames, psf_rows, psf_cols, dither.T, footprint.T, huber_cut)
        ]
        dma = pltpu.SemaphoreType.DMA
        smooth, total = pl.pallas_call(
            functools.partial(kernel, (sky_count, visit_count)),
            out_shape=(pltpu.VMEM((height, width), f32), pltpu.VMEM((SHIFTS * height, half_cols), f32)),
            in_specs=[pl.BlockSpec(memory_space=pltpu.HBM)] * 7,
            out_specs=(pl.BlockSpec(memory_space=pltpu.VMEM),) * 2,
            scratch_shapes=[
                pltpu.SMEM(psf_rows.shape, f32),
                pltpu.SMEM(psf_cols.shape, f32),
                pltpu.SMEM(dither.shape[::-1], jnp.int32),
                pltpu.SMEM(footprint.shape[::-1], jnp.int32),
                pltpu.SMEM(huber_cut.shape, f32),
                pltpu.VMEM((height + 2 * ROWS, width + 2 * LANES), f32),
                pltpu.VMEM(frames.shape, bf16),
                pltpu.VMEM((visit_count, per_device, low_rows, low_cols), bf16),
                pltpu.VMEM((2, visit_count, 32, LANES), bf16),
                pltpu.VMEM((2, visit_count, 32, LANES), bf16),
                pltpu.VMEM((visit_count, 48, LANES), bf16),
                pltpu.VMEM((visit_count, 48, LANES), bf16),
                pltpu.VMEM((2, 8, LANES), f32),
                pltpu.VMEM((2, 8, LANES), f32),
                pltpu.VMEM((DEPTH, 2 * half_cols), bf16),
                pltpu.VMEM((visit_count, SLOT, DEPTH), bf16),
                pltpu.VMEM((visit_count, SLOT, 2 * half_cols), f32),
                pltpu.VMEM((visit_count, SLOT, half_cols), f32),
                pltpu.VMEM((visit_count, SHIFTS * height, DEPTH), bf16),
                pltpu.VMEM((DEPTH, half_cols), bf16),
                dma((3,)),
                dma((5,)),
                pltpu.SemaphoreType.REGULAR((visit_count,)),
                pltpu.SemaphoreType.REGULAR((2,)),
                dma((visit_count,)),
                dma((visit_count,)),
                dma((2,)),
                dma((2,)),
                dma((visit_count,)),
                dma((visit_count,)),
                dma((2,)),
                dma((2,)),
                dma((2,)),
                dma((2,)),
            ],
            compiler_params=pltpu.CompilerParams(
                collective_id=0, has_side_effects=True, vmem_limit_bytes=48 * 1024 * 1024
            ),
        )(*arguments)
        return pl.pallas_call(
            finish,
            out_shape=pltpu.HBM((height, width), f32),
            in_specs=[pl.BlockSpec(memory_space=pltpu.VMEM)] * 2,
            out_specs=pl.BlockSpec(memory_space=pltpu.HBM),
            scratch_shapes=[pltpu.VMEM((height, width), f32), dma((height // 32,))],
            compiler_params=pltpu.CompilerParams(vmem_limit_bytes=8 * 1024 * 1024),
        )(
            pltpu.with_memory_space_constraint(total, pltpu.VMEM),
            pltpu.with_memory_space_constraint(smooth, pltpu.VMEM),
        )

    return jax.shard_map(
        on_device, mesh=mesh, in_specs=in_specs, out_specs=out_specs, check_vma=False
    )
```

```python
import functools

import jax
import jax.numpy as jnp
from jax import lax
from jax.experimental import pallas as pl
from jax.experimental.pallas import tpu as pltpu
from jax.sharding import PartitionSpec as P

TAPS = 5
SHIFTS = TAPS + 1

eps_flux = 0.1
tv_weight = 0.5

ROWS = 8
LANES = 128
PAIR = 2
SLOT = 80
DEPTH = 256
MESH = pl.DeviceIdType.MESH


def dot(a, b):
    return jnp.dot(a, b, preferred_element_type=jnp.float32)


def iota(shape, dim):
    return lax.broadcasted_iota(jnp.int32, shape, dim)


def selection(shape, source_of):
    row, col = iota(shape, 0), iota(shape, 1)
    return jnp.where(source_of(row, col), 1.0, 0.0).astype(jnp.bfloat16)


def halves(value):
    high = value.astype(jnp.bfloat16)
    return high, (value - high.astype(jnp.float32)).astype(jnp.bfloat16)


def turn(value, shift, axis):
    shift %= value.shape[axis]
    return pltpu.roll(value, shift, axis) if shift else value


def pick(at, taps):
    value = jnp.zeros(at.shape, jnp.float32)
    for a, tap in enumerate(taps):
        value = jnp.where(at == a, tap, value)
    return value


def kernel(
    counts,
    model_ref,
    frames_ref,
    rows_in,
    cols_in,
    dither_in,
    footprint_in,
    cut_in,
    out_ref,
    total_ref,
    rows_ref,
    cols_ref,
    dither_ref,
    footprint_ref,
    cut_ref,
    grid_ref,
    own_ref,
    frame_ref,
    row_out,
    row_in,
    aux_out,
    aux_in,
    side_out,
    side_in,
    model_stack,
    ahead_ref,
    rowed_ref,
    pred_ref,
    back_ref,
    stack_ref,
    local_sem,
    small_sem,
    here_visit,
    here_sky,
    frame_send,
    frame_recv,
    row_send,
    row_recv,
    aux_send,
    aux_recv,
    side_send,
    side_recv,
    rim_send,
    rim_recv,
):
    sky_count, visit_count = counts
    height, width = out_ref.shape
    low_rows, low_cols = frame_ref.shape[2:]
    full_cols = grid_ref.shape[1]
    half_cols = full_cols // 2
    blocks = full_cols // (2 * LANES)
    visits = rows_ref.shape[0]
    tile = lax.axis_index("tiles")
    sky = lax.axis_index("sky")
    visit = lax.axis_index("visit")
    has_up, has_down = sky > 0, sky < sky_count - 1
    has_left, has_right = visit > 0, visit < visit_count - 1
    f32, bf16 = jnp.float32, jnp.bfloat16

    def remote(source, target, send, recv, device):
        return pltpu.make_async_remote_copy(
            src_ref=source, dst_ref=target, send_sem=send, recv_sem=recv, device_id=device, device_id_type=MESH
        )

    def at_visit(q):
        return (tile, sky, q)

    def at_sky(step):
        return (tile, sky + step, visit)

    ways = ((0, has_up, has_down), (1, has_down, has_up))

    def columns_of(q):
        return pl.ds(pl.multiple_of(q * low_cols, low_cols), low_cols)

    def frame_copy(peer, owner):
        return remote(
            frames_ref.at[:, :, columns_of(peer)],
            frame_ref.at[owner],
            frame_send.at[peer],
            frame_recv.at[owner],
            at_visit(peer),
        )

    def aux_copy(peer, owner):
        return remote(aux_out.at[peer], aux_in.at[owner], aux_send.at[peer], aux_recv.at[owner], at_visit(peer))

    def row_copy(way):
        return remote(row_out.at[way], row_in.at[way], row_send.at[way], row_recv.at[way], at_sky(2 * way - 1))

    def side_copy(side):
        return remote(
            side_out.at[side], side_in.at[side], side_send.at[side], side_recv.at[side], at_visit(visit + 2 * side - 1)
        )

    def rim_copy(way):
        source = model_ref.at[pl.ds((height - ROWS) * way, ROWS), :]
        target = grid_ref.at[pl.ds((ROWS + height) * (1 - way), ROWS), pl.ds(0, width)]
        return remote(source, target, rim_send.at[way], rim_recv.at[way], at_sky(2 * way - 1))

    own_frames = pltpu.make_async_copy(frames_ref, own_ref, local_sem.at[1])
    small = [
        pltpu.make_async_copy(source, target, small_sem.at[n])
        for n, (source, target) in enumerate(
            (
                (rows_in, rows_ref),
                (cols_in, cols_ref),
                (dither_in, dither_ref),
                (footprint_in, footprint_ref),
                (cut_in, cut_ref),
            )
        )
    ]
    own_model = pltpu.make_async_copy(
        model_ref, grid_ref.at[pl.ds(ROWS, height), pl.ds(0, width)], local_sem.at[0]
    )
    own_block = pltpu.make_async_copy(frames_ref.at[:, :, columns_of(visit)], frame_ref.at[visit], local_sem.at[2])
    own_frames.start()
    own_model.start()
    for copy in small:
        copy.start()
    barrier = pltpu.get_barrier_semaphore()
    is_odd = sky % 2 > 0

    def greet(q, carry):
        pl.semaphore_signal(barrier, inc=1, device_id=at_visit(q), device_id_type=MESH)
        return carry

    lax.fori_loop(visit + 1, visit_count, greet, 0)
    for way, ok, _ in ways:

        @pl.when(ok & is_odd)
        def _():
            pl.semaphore_signal(barrier, inc=1, device_id=at_sky(2 * way - 1), device_id_type=MESH)

    beside = has_up.astype(jnp.int32) + has_down.astype(jnp.int32)
    smaller = visit + jnp.where(is_odd, 0, beside)

    @pl.when(smaller > 0)
    def _():
        pl.semaphore_wait(barrier, smaller)

    def answer(q, carry):
        pl.semaphore_signal(here_visit.at[visit], inc=1, device_id=at_visit(q), device_id_type=MESH)
        return carry

    lax.fori_loop(0, visit, answer, 0)

    for way, ok, _ in ways:

        @pl.when(ok & jnp.logical_not(is_odd))
        def _():
            pl.semaphore_signal(here_sky.at[1 - way], inc=1, device_id=at_sky(2 * way - 1), device_id_type=MESH)

    @pl.when(visit > 1)
    def _():
        frame_copy(0, visit).start()

    for way, ok, _ in ways:

        @pl.when(ok & jnp.logical_not(is_odd))
        def _():
            rim_copy(way).start()

    own_block.start()

    @pl.when(jnp.logical_not(has_up))
    def _():
        grid_ref[0:ROWS, 0:width] = jnp.zeros((ROWS, width), f32)
        row_in[1] = jnp.zeros(row_in.shape[1:], bf16)

    @pl.when(jnp.logical_not(has_down))
    def _():
        grid_ref[ROWS + height :, 0:width] = jnp.zeros((ROWS, width), f32)
        row_in[0] = jnp.zeros(row_in.shape[1:], bf16)

    own_frames.wait()
    sub8 = iota((8, LANES), 0)
    lane8 = iota((8, LANES), 1)
    blank8 = jnp.zeros((8, LANES), f32)
    low_blocks = low_cols // LANES
    for way in range(2):
        piled, moved = [], []
        for n in range(low_blocks * visit_count):
            cols = slice(LANES * n, LANES * (n + 1))
            if way == 0:
                first = own_ref[0, 0:16, cols].astype(f32)[0:8]
                second = turn(own_ref[1, 0:16, cols].astype(f32)[0:8], 2, 0)
            else:
                first = turn(own_ref[0, low_rows - 16 : low_rows, cols].astype(f32)[8:16], 2, 0)
                second = turn(own_ref[1, low_rows - 16 : low_rows, cols].astype(f32)[8:16], 4, 0)
            piled.append(jnp.where(sub8 < 2, first, second))
            moved.append(turn(piled[-1], 4, 0))
        for p in range(visit_count):
            n = low_blocks * p
            for b in range(low_blocks // 4):
                tiles = [jnp.where(sub8 < 4, piled[m], moved[m + 1]) for m in (n + 4 * b, n + 4 * b + 2)]
                row_out[way, p, 16 * b : 16 * (b + 1), :] = jnp.concatenate(tiles, axis=0).astype(bf16)
            ends = moved if way else piled
            corner = jnp.where(lane8 < LANES // 2, ends[(n + low_blocks) % len(ends)], ends[n - 1])
            row_out[way, p, 16:32, :] = jnp.concatenate([corner, blank8], axis=0).astype(bf16)
    for p in range(visit_count):
        right = low_cols * (p + 1) if p < visit_count - 1 else 0
        left = low_cols * p - LANES if p > 0 else 0
        packed = blank8
        for j in range(PAIR):
            for u in range(low_rows // 16):
                after = own_ref[j, 16 * u : 16 * (u + 1), right : right + LANES].astype(f32)
                before = own_ref[j, 16 * u : 16 * (u + 1), left : left + LANES].astype(f32)
                for n in range(2):
                    g = (low_rows * j + 16 * u) // 8 + n
                    piece = jnp.where(lane8 < LANES // 2, after[8 * n : 8 * (n + 1)], before[8 * n : 8 * (n + 1)])
                    packed = jnp.where((lane8 - 4 * g + 2 + LANES) % LANES < 4, turn(piece, 4 * g, 1), packed)
        aux_out[p, 32:48, :] = jnp.concatenate([blank8, packed], axis=0).astype(bf16)

    for way, ok, _ in ways:

        @pl.when(ok & jnp.logical_not(is_odd))
        def _():
            row_copy(way).start()

    for way, ok, _ in ways:

        @pl.when(ok & is_odd)
        def _():
            pl.semaphore_wait(here_sky.at[way], 1)
            row_copy(way).start()
            rim_copy(way).start()

    for copy in small:
        copy.wait()
    share = 1.0 / float(visits) ** 0.5

    def col_shift(k):
        return (dither_ref[1, k] + 4) // 2 - 2

    def col_weights(k):
        odd = dither_ref[1, k] - 2 * col_shift(k)
        weights = []
        for d in range(SHIFTS):
            value = jnp.where(odd > 0, cols_ref[k, max(d - 1, 0)], cols_ref[k, min(d, TAPS - 1)])
            weights.append(jnp.where(odd > 0, 0.0, value) if d == 0 else value)
        weights[TAPS] = jnp.where(odd > 0, weights[TAPS], 0.0)
        return weights

    def row_of_halo(n):
        return jnp.where(n % 8 < 4, low_rows + n % 2, n % 2 - 2)

    lane = iota((16, DEPTH), 1)
    row = iota((16, DEPTH), 0)
    model_row = lane % SLOT - ROWS
    is_low = lane >= 2 * SLOT
    blank = lane >= 3 * SLOT
    far = 4 * height

    def low_part(value):
        return jnp.where(is_low, value - value.astype(bf16).astype(f32), value).astype(bf16)

    slot = lane % SLOT
    source_row = jnp.where(slot < 2 * low_rows, slot % low_rows, row_of_halo(slot))
    source_row = jnp.where((slot >= 2 * low_rows + 8) | blank, far, source_row)
    second_visit = jnp.where(slot < 2 * low_rows, slot // low_rows, slot % 4 // 2) > 0
    base_main = jnp.where(blank, -far, model_row + TAPS // 2 - 2 * row)
    halo_row = jnp.where(row < 8, row_of_halo(row), far)
    base_halo = jnp.where(blank, -far, model_row + TAPS // 2 - 2 * halo_row)
    base_back = row + TAPS // 2 - 2 * source_row

    def build(c, carry):
        k0, k1 = PAIR * c, PAIR * c + 1
        shift0, shift1 = dither_ref[0, k0], dither_ref[0, k1]
        taps0 = [rows_ref[k0, a] for a in range(TAPS)]
        taps1 = [rows_ref[k1, a] for a in range(TAPS)]
        for j, (shift, taps) in enumerate(((shift0, taps0), (shift1, taps1))):
            for u in range(low_rows // 16):
                begin = low_rows * j + 16 * u
                ahead_ref[c, begin : begin + 16, :] = low_part(pick(base_main - (32 * u + shift), taps))
        upper = row % 4 < 2
        ahead_ref[c, 2 * low_rows : SLOT, :] = low_part(
            pick(
                base_halo - jnp.where(upper, shift0, shift1),
                [jnp.where(upper, a, b) for a, b in zip(taps0, taps1)],
            )
        )
        taps = [jnp.where(second_visit, b, a) for a, b in zip(taps0, taps1)]
        weights = [
            jnp.where(second_visit, b * share, a * share) for a, b in zip(col_weights(k0), col_weights(k1))
        ]
        base = base_back - jnp.where(second_visit, shift1, shift0)
        for u in range(height // 16):
            value = pick(base + 16 * u, taps)
            for d in range(SHIFTS):
                begin = height * d + 16 * u
                back_ref[c, begin : begin + 16, :] = low_part(value * weights[d])
        return carry

    lax.fori_loop(0, visit_count, build, 0)

    own_model.wait()

    @pl.when(has_down)
    def _():
        rim_copy(0).wait_recv()

    @pl.when(has_up)
    def _():
        rim_copy(1).wait_recv()

    groups = (height + 2 * ROWS) // 8
    for side in range(2):
        packed = jnp.zeros((8, LANES), f32)
        begin = (width - LANES) * side
        for t in range(groups):
            piece = turn(grid_ref[8 * t : 8 * (t + 1), begin : begin + LANES], 8 * t + 8 * side, 1)
            packed = jnp.where((lane8 >= 8 * t) & (lane8 < 8 * t + 8), piece, packed)
        side_out[side] = packed

    @pl.when(has_left)
    def _():
        side_copy(0).start()

    for way, _, ok in ways:

        @pl.when(ok)
        def _():
            row_copy(way).wait_recv()

    for p in range(visit_count):
        aux_out[p, 0:16, :] = row_in[0, p, 0:16, :]
        aux_out[p, 16:32, :] = row_in[1, p, 0:16, :]
        down, up = [row_in[way, p, 16:32, :].astype(f32)[0:8] for way in range(2)]
        packed = aux_out[p, 32:48, :].astype(f32)[8:16]
        aux_out[p, 32:48, :] = jnp.concatenate([jnp.where(sub8 < 4, down, up), packed], axis=0).astype(bf16)
    aux_in[visit] = aux_out[visit]

    def send_low(q, carry):
        aux_copy(q, visit).start()
        return carry

    lax.fori_loop(0, visit, send_low, 0)

    def send_main(q, carry):
        frame_copy(q, visit).start()
        return carry

    lax.fori_loop((visit > 1).astype(jnp.int32), visit, send_main, 0)

    def send_high(q, carry):
        pl.semaphore_wait(here_visit.at[q], 1)

        @pl.when(q == visit + 1)
        def _():
            side_copy(1).start()

        aux_copy(q, visit).start()
        frame_copy(q, visit).start()
        return carry

    at_once = has_left | (has_up & has_down)
    following = jnp.where(at_once, visit_count, jnp.minimum(visit + 2, visit_count))
    lax.fori_loop(visit + 1, following, send_high, 0)

    model_stack[3 * SLOT : DEPTH, :] = jnp.zeros((DEPTH - 3 * SLOT, full_cols), bf16)
    stack_ref[3 * SLOT : DEPTH, :] = jnp.zeros((DEPTH - 3 * SLOT, half_cols), bf16)

    spread = selection(
        (2 * LANES, 2 * LANES),
        lambda a, b: a == jnp.where(b < LANES, 2 * b, 2 * b - (2 * LANES - 1)),
    )
    operator = ahead_ref[...].reshape(visit_count * SLOT, DEPTH)

    def rows_ahead(some):
        parts = [halves(grid_ref[:, 2 * LANES * n : 2 * LANES * (n + 1)]) for n in some]
        apart = dot(jnp.concatenate([part for pair in parts for part in pair], axis=0), spread).astype(bf16)
        for m, n in enumerate(some):
            cols = slice(2 * LANES * n, 2 * LANES * (n + 1))
            high = apart[2 * SLOT * m : 2 * SLOT * m + SLOT]
            model_stack[0:SLOT, cols] = high
            model_stack[SLOT : 2 * SLOT, cols] = apart[2 * SLOT * m + SLOT : 2 * SLOT * (m + 1)]
            model_stack[2 * SLOT : 3 * SLOT, cols] = high
            rowed_ref[:, :, cols] = dot(operator, model_stack[:, cols]).reshape(visit_count, SLOT, 2 * LANES)

    rows_ahead(range(blocks - 1))

    first_lane, last_lane = lane8 == 0, lane8 == LANES - 1
    upper8 = sub8 % 4 < 2

    def row_groups(c):
        weights0, weights1 = col_weights(PAIR * c), col_weights(PAIR * c + 1)
        for g in range(2 * low_rows // 8 + 1):
            if g < low_rows // 8:
                weights = weights0
            elif g < 2 * low_rows // 8:
                weights = weights1
            else:
                weights = [jnp.where(upper8, a, b) for a, b in zip(weights0, weights1)]
            yield slice(8 * g, 8 * (g + 1)), weights

    def tap(c, rows, weights, n, step):
        even = rowed_ref[c, rows, 2 * LANES * n : 2 * LANES * n + LANES]
        odd = rowed_ref[c, rows, 2 * LANES * n + LANES : 2 * LANES * (n + 1)]
        value = weights[2 * step + 2] * even + weights[2 * step + 3] * odd
        return turn(value, -step, 1)

    last = blocks - 1

    def predict(c):
        for rows, weights in row_groups(c):
            before, here, after = [[tap(c, rows, weights, n, step) for n in range(last)] for step in (-1, 0, 1)]
            for n in range(last):
                value = here[n] + jnp.where(first_lane, before[n - 1] if n else 0.0, before[n])
                value = value + jnp.where(last_lane, after[n + 1] if n < last - 1 else 0.0, after[n])
                pred_ref[c, rows, LANES * n : LANES * (n + 1)] = value

    def predict_ends(c):
        for rows, weights in row_groups(c):
            before, here, after = [tap(c, rows, weights, last, step) for step in (-1, 0, 1)]
            value = here + jnp.where(first_lane, tap(c, rows, weights, last - 1, -1), before)
            value = value + jnp.where(last_lane, tap(c, rows, weights, 0, 1), after)
            pred_ref[c, rows, LANES * last : LANES * blocks] = value
            pred_ref[c, rows, 0:LANES] += jnp.where(first_lane, before, 0.0)
            pred_ref[c, rows, LANES * (last - 1) : LANES * last] += jnp.where(last_lane, after, 0.0)

    def by_four(body):
        def four(n, carry):
            for c in range(4):
                body(4 * n + c)
            return carry

        return four

    fours = visit_count // 4
    early = jnp.where(at_once, 0, fours)
    lax.fori_loop(0, early, by_four(predict), 0)
    lax.fori_loop(following, visit_count, send_high, 0)
    lax.fori_loop(early, fours, by_four(predict), 0)

    for side, ok in ((0, has_right), (1, has_left)):
        begin = width + LANES * side

        @pl.when(ok)
        def _():
            side_copy(side).wait_recv()
            packed = side_in[side]
            keep = lane8 >= LANES - 8 if side else lane8 < 8
            for t in range(groups):
                piece = turn(packed, -8 * t - 8 * side, 1)
                grid_ref[8 * t : 8 * (t + 1), begin : begin + LANES] = jnp.where(keep, piece, 0.0)

        @pl.when(jnp.logical_not(ok))
        def _():
            grid_ref[:, begin : begin + LANES] = jnp.zeros((height + 2 * ROWS, LANES), f32)

    rows_ahead([last])
    lax.fori_loop(0, fours, by_four(predict_ends), 0)

    own_block.wait()
    row16 = iota((16, LANES), 0)
    lane16 = iota((16, LANES), 1)
    halo_index = row_of_halo(iota((16, LANES), 0)) + sky * low_rows
    upper16 = row16 % 4 < 2
    columns = [lane16 + LANES * n for n in range(blocks - 1)]
    columns.append(jnp.where(lane16 < LANES // 2, lane16 + low_cols, lane16 - LANES))
    columns = [value + visit * low_cols for value in columns]
    all_cols = low_cols * visit_count

    order = [sorted(range(visit_count), key=lambda q: (abs(q - v), q)) for v in range(visit_count)]

    def owner_of(o):
        owner = jnp.int32(0)
        for v in range(visit_count):
            for n in range(visit_count):
                if order[v][n]:
                    owner = jnp.where((visit == v) & (o == n), order[v][n], owner)
        return owner

    def shifted(values, shift):
        turned = [pltpu.roll(value, jnp.where(shift < 0, LANES - 1, shift), 1) for value in values]
        to_right, to_left = (lane16 == 0) & (shift > 0), (lane16 == LANES - 1) & (shift < 0)
        return [
            jnp.where(to_right, turned[n - 1], jnp.where(to_left, turned[(n + 1) % blocks], turned[n]))
            for n in range(blocks)
        ]

    def limits(limit, shift):
        result = []
        for n in range(blocks):
            if 0 < n < blocks - 2:
                result.append(limit)
            else:
                result.append(jnp.where((columns[n] >= shift) & (columns[n] < all_cols + shift), limit, 0.0))
        return result

    def put(begin, predicted, values, limit):
        for n in range(blocks):
            cols = slice(LANES * n, LANES * (n + 1))
            error = predicted[n] - values[n]
            high, low = halves(jnp.minimum(jnp.maximum(error, -limit[n]), limit[n]))
            stack_ref[begin : begin + 16, cols] = high
            stack_ref[SLOT + begin : SLOT + begin + 16, cols] = low
            stack_ref[2 * SLOT + begin : 2 * SLOT + begin + 16, cols] = high

    def arrived(c):
        frame_copy(c, c).wait_recv()
        aux_copy(c, c).wait_recv()

    def work(c, is_first):
        rest = aux_in[c, 32:48, :].astype(f32)
        packed = rest[8:16]
        shifts = [col_shift(PAIR * c + j) for j in range(PAIR)]
        for j in range(PAIR):
            k = PAIR * c + j
            cut, first, last = cut_ref[k], footprint_ref[0, k], footprint_ref[1, k]
            for u in range(low_rows // 16):
                begin = low_rows * j + 16 * u
                start = sky * low_rows + 16 * u
                rows = slice(16 * u, 16 * (u + 1))
                values = [
                    frame_ref[c, j, rows, LANES * n : LANES * (n + 1)].astype(f32) for n in range(blocks - 1)
                ]
                g = begin // 8
                values.append(jnp.concatenate([turn(packed, -4 * g, 1), turn(packed, -4 * (g + 1), 1)], axis=0))
                limit = jnp.where((row16 >= first - start) & (row16 < last - start), cut, 0.0)
                predicted = [pred_ref[c, begin : begin + 16, LANES * n : LANES * (n + 1)] for n in range(blocks)]
                put(begin, predicted, shifted(values, shifts[j]), limits(limit, shifts[j]))
        k0, k1 = PAIR * c, PAIR * c + 1
        begin = 2 * low_rows
        values = []
        for _ in range(low_blocks // 4):
            down, up = [aux_in[c, 16 * way : 16 * (way + 1), :].astype(f32) for way in range(2)]
            for n in range(2):
                down8, up8 = down[8 * n : 8 * (n + 1)], up[8 * n : 8 * (n + 1)]
                values.append(jnp.where(sub8 < 4, down8, turn(up8, 4, 0)))
                values.append(jnp.where(sub8 < 4, turn(down8, 4, 0), up8))
        values.append(rest[0:8])
        values = [jnp.concatenate([value, blank8], axis=0) for value in values]
        values = [jnp.where(upper16, a, b) for a, b in zip(shifted(values, shifts[0]), shifted(values, shifts[1]))]
        inside = (halo_index >= jnp.where(upper16, footprint_ref[0, k0], footprint_ref[0, k1])) & (
            halo_index < jnp.where(upper16, footprint_ref[1, k0], footprint_ref[1, k1])
        )
        limit = jnp.where(inside & (row16 < 8), jnp.where(upper16, cut_ref[k0], cut_ref[k1]), 0.0)
        predicted = [
            jnp.concatenate([pred_ref[c, begin : begin + 8, LANES * n : LANES * (n + 1)], blank8], axis=0)
            for n in range(blocks)
        ]
        put(begin, predicted, values, limits(limit, jnp.where(upper16, shifts[0], shifts[1])))
        for begin in range(0, half_cols, 2 * LANES):
            cols = slice(begin, min(begin + 2 * LANES, half_cols))
            product = dot(back_ref[c], stack_ref[:, cols])
            total_ref[:, cols] = product if is_first else total_ref[:, cols] + product

    owners = [owner_of(o) for o in range(visit_count)]
    work(owners[0], True)

    def next_col(value):
        return pltpu.roll(value, full_cols - 1, 1)

    strip = 16
    for t in range(height // strip):
        above = grid_ref[ROWS - 1 + strip * t : ROWS - 1 + strip * (t + 1), :]
        here = grid_ref[ROWS + strip * t : ROWS + strip * (t + 1), :]
        below = grid_ref[ROWS + 1 + strip * t : ROWS + 1 + strip * (t + 1), :]
        gx, gy = here - above, next_col(above) - above
        value = gx * lax.rsqrt(gx * gx + gy * gy + eps_flux)
        gx, gy = below - here, next_col(here) - here
        scale = lax.rsqrt(gx * gx + gy * gy + eps_flux)
        flux = gy * scale
        value = value - gx * scale + (pltpu.roll(flux, 1, 1) - flux)
        out_ref[strip * t : strip * (t + 1), :] = tv_weight * value[:, :width]

    for c in owners[1:]:
        arrived(c)
        work(c, False)

    def sent(q, carry):
        @pl.when(q != visit)
        def _():
            frame_copy(q, visit).wait_send()
            aux_copy(q, visit).wait_send()

        return carry

    lax.fori_loop(0, visit_count, sent, 0)
    for side, ok in ((0, has_left), (1, has_right)):

        @pl.when(ok)
        def _():
            side_copy(side).wait_send()

    for way, ok in ((0, has_up), (1, has_down)):

        @pl.when(ok)
        def _():
            rim_copy(way).wait_send()
            row_copy(way).wait_send()


def finish(total_ref, smooth_ref, out_ref, whole_ref, sem):
    height, width = whole_ref.shape
    low_cols = width // 2
    join = selection(
        (4 * LANES, 2 * LANES),
        lambda a, b: b == jnp.where(a % (2 * LANES) < LANES, 2 * (a % LANES), 2 * (a % LANES) + 1),
    )
    strip = 16
    copies = []
    for u in range(height // strip):
        parts = []
        for odd in range(2):
            value = None
            for step in range(-1, 2):
                begin = height * (2 * (step + 1) + odd) + strip * u
                piece = turn(total_ref[begin : begin + strip, :], step, 1)
                value = piece if value is None else value + piece
            parts.append(halves(value[:, :low_cols]))
        pieces = []
        for b in range(low_cols // LANES):
            cols = slice(LANES * b, LANES * (b + 1))
            four = [part[:, cols] for part in (parts[0][0], parts[1][0], parts[0][1], parts[1][1])]
            pieces.append(jnp.concatenate(four, axis=1))
        joined = dot(jnp.concatenate(pieces, axis=0), join)
        rows = slice(strip * u, strip * (u + 1))
        for b in range(low_cols // LANES):
            cols = slice(2 * LANES * b, 2 * LANES * (b + 1))
            whole_ref[rows, cols] = smooth_ref[rows, cols] + joined[strip * b : strip * (b + 1)]
        span = pl.ds(strip * u, strip)
        copies.append(pltpu.make_async_copy(whole_ref.at[span], out_ref.at[span], sem.at[u]))
        copies[-1].start()
    for copy in copies:
        copy.wait()


def solution(mesh):
    in_specs = (
        P(("tiles", "sky"), "visit"),
        P(("tiles", "visit"), "sky", None),
        P("tiles", None),
        P("tiles", None),
        P("tiles", None),
        P("tiles", None),
        P("tiles"),
    )
    out_specs = P(("tiles", "sky"), "visit")
    sky_count, visit_count = mesh.shape["sky"], mesh.shape["visit"]

    def on_device(sky_model, frames, psf_rows, psf_cols, dither, footprint, huber_cut):
        height, width = sky_model.shape
        per_device, low_rows, all_cols = frames.shape
        visits = psf_rows.shape[0]
        low_cols = all_cols // visit_count
        half_cols = width // 2 + LANES
        f32, bf16 = jnp.float32, jnp.bfloat16
        arguments = [
            pltpu.with_memory_space_constraint(x, pltpu.HBM)
            for x in (sky_model, frames, psf_rows, psf_cols, dither.T, footprint.T, huber_cut)
        ]
        dma = pltpu.SemaphoreType.DMA
        smooth, total = pl.pallas_call(
            functools.partial(kernel, (sky_count, visit_count)),
            out_shape=(pltpu.VMEM((height, width), f32), pltpu.VMEM((SHIFTS * height, half_cols), f32)),
            in_specs=[pl.BlockSpec(memory_space=pltpu.HBM)] * 7,
            out_specs=(pl.BlockSpec(memory_space=pltpu.VMEM),) * 2,
            scratch_shapes=[
                pltpu.SMEM(psf_rows.shape, f32),
                pltpu.SMEM(psf_cols.shape, f32),
                pltpu.SMEM(dither.shape[::-1], jnp.int32),
                pltpu.SMEM(footprint.shape[::-1], jnp.int32),
                pltpu.SMEM(huber_cut.shape, f32),
                pltpu.VMEM((height + 2 * ROWS, width + 2 * LANES), f32),
                pltpu.VMEM(frames.shape, bf16),
                pltpu.VMEM((visit_count, per_device, low_rows, low_cols), bf16),
                pltpu.VMEM((2, visit_count, 32, LANES), bf16),
                pltpu.VMEM((2, visit_count, 32, LANES), bf16),
                pltpu.VMEM((visit_count, 48, LANES), bf16),
                pltpu.VMEM((visit_count, 48, LANES), bf16),
                pltpu.VMEM((2, 8, LANES), f32),
                pltpu.VMEM((2, 8, LANES), f32),
                pltpu.VMEM((DEPTH, 2 * half_cols), bf16),
                pltpu.VMEM((visit_count, SLOT, DEPTH), bf16),
                pltpu.VMEM((visit_count, SLOT, 2 * half_cols), f32),
                pltpu.VMEM((visit_count, SLOT, half_cols), f32),
                pltpu.VMEM((visit_count, SHIFTS * height, DEPTH), bf16),
                pltpu.VMEM((DEPTH, half_cols), bf16),
                dma((3,)),
                dma((5,)),
                pltpu.SemaphoreType.REGULAR((visit_count,)),
                pltpu.SemaphoreType.REGULAR((2,)),
                dma((visit_count,)),
                dma((visit_count,)),
                dma((2,)),
                dma((2,)),
                dma((visit_count,)),
                dma((visit_count,)),
                dma((2,)),
                dma((2,)),
                dma((2,)),
                dma((2,)),
            ],
            compiler_params=pltpu.CompilerParams(
                collective_id=0, has_side_effects=True, vmem_limit_bytes=48 * 1024 * 1024
            ),
        )(*arguments)
        return pl.pallas_call(
            finish,
            out_shape=pltpu.HBM((height, width), f32),
            in_specs=[pl.BlockSpec(memory_space=pltpu.VMEM)] * 2,
            out_specs=pl.BlockSpec(memory_space=pltpu.HBM),
            scratch_shapes=[pltpu.VMEM((height, width), f32), dma((height // 16,))],
            compiler_params=pltpu.CompilerParams(vmem_limit_bytes=8 * 1024 * 1024),
        )(
            pltpu.with_memory_space_constraint(total, pltpu.VMEM),
            pltpu.with_memory_space_constraint(smooth, pltpu.VMEM),
        )

    return jax.shard_map(
        on_device, mesh=mesh, in_specs=in_specs, out_specs=out_specs, check_vma=False
    )
```
